32 devices in a mesh: ctx: 8 (over y, x, core), wa: 4 (over z).
Axes of the slice: x: 2, y: 2, z: 4, core: 2. Of those that a mesh axis runs over, the one named last changes fastest.
Arguments:
- inputs: bfloat16 [4, 4096, 768], P('wa', 'ctx'), may hold values from -6 to 6
- cotangent: bfloat16 [4, 4096, 768], P('wa', 'ctx'), may hold values from -6 to 6
- lengths: int32 [4], P('wa'), may hold values from 2049 to 4096, as said below
- global_ids: int32 [4, 2], P('wa'), may hold values from 0 to 63, as said below
- random_ids: int32 [4, 64, 3], P('wa', 'ctx'), may hold values from 0 to 63, as said below
- attn_master: float32 [4, 768, 768], P(None, 'wa')
- attn_m: float32 [4, 768, 768], P(None, 'wa'), may hold values from -120 to 120
- attn_v: float32 [4, 768, 768], P(None, 'wa'), may hold values from 100 to 10000
- ffn_master: float32 [2, 768, 3072], P(None, 'wa')
- ffn_m: float32 [2, 768, 3072], P(None, 'wa'), may hold values from -120 to 120
- ffn_v: float32 [2, 768, 3072], P(None, 'wa'), may hold values from 100 to 10000
- vec_master: float32 [8, 768], P(None, 'wa')
- vec_m: float32 [8, 768], P(None, 'wa'), may hold values from -120 to 120
- vec_v: float32 [8, 768], P(None, 'wa'), may hold values from 100 to 10000
- bias_master: float32 [3072], P('wa'), may hold values from -3 to 3
- bias_m: float32 [3072], P('wa'), may hold values from -120 to 120
- bias_v: float32 [3072], P('wa'), may hold values from 100 to 10000
Outputs:
- output: bfloat16 [4, 4096, 768], P('wa', 'ctx')
- input_grad: float32 [4, 4096, 768], P('wa', 'ctx')
- attn_grad: float32 [4, 768, 768], P(None, 'wa')
- ffn_grad: float32 [2, 768, 3072], P(None, 'wa')
- vec_grad: float32 [8, 768], P(None, 'wa')
- bias_grad: float32 [3072], P('wa')
- attn_new: float32 [4, 768, 768], P(None, 'wa')
- ffn_new: float32 [2, 768, 3072], P(None, 'wa')
- vec_new: float32 [8, 768], P(None, 'wa')
- bias_new: float32 [3072], P('wa')
- attn_copy: bfloat16 [4, 768, 768], P(None, 'wa')
- ffn_copy: bfloat16 [2, 768, 3072], P(None, 'wa')
- vec_copy: bfloat16 [8, 768], P(None, 'wa')
- bias_copy: bfloat16 [3072], P('wa')
- attn_m_new: float32 [4, 768, 768], P(None, 'wa')
- ffn_m_new: float32 [2, 768, 3072], P(None, 'wa')
- vec_m_new: float32 [8, 768], P(None, 'wa')
- bias_m_new: float32 [3072], P('wa')
- attn_v_new: float32 [4, 768, 768], P(None, 'wa')
- ffn_v_new: float32 [2, 768, 3072], P(None, 'wa')
- vec_v_new: float32 [8, 768], P(None, 'wa')
- bias_v_new: float32 [3072], P('wa')
- norms: float32 [6, 2], replicated
- ratios: float32 [6], replicated
The draws below stay inside these ranges and needn't reach their ends.
Inputs may be any that keep to these rules, and one draw needn't show every extreme that they name: `lengths`: every sequence uses more than half of its 4096 positions, and at least one uses all of them. `global_ids`: two different blocks of a sequence that lie wholly below its length. `random_ids`: blocks of the same sequence that lie wholly below its length; repeats may occur; of the 24 entries of the query blocks on one index of ctx, at most 6 name blocks held by any one index of ctx, and in every sequence the first index of ctx has exactly 6 entries naming blocks of the first.
All inputs are finite; a program needn't handle non-finite values.
Results may differ from the reference program's by a relative error of at most 0.025.
Values may be sent and summed in bfloat16 or wider, within the bound.
No kernel may reach another device: no remote copies, remote signals or barrier semaphores. Data moves between devices by JAX's collectives and lax.ppermute only.
A program may use at most 384 MiB of HBM per device.

```python
import math
import jax
import jax.numpy as jnp
from jax import lax

D = 768
HEADS = 12
HEAD = 64
FF = 3072
BLOCK = 64
RAND = 3
TOK_DEV = 512
LENGTH = 4096
SEQS = 4
RCAP = 6


def device_random(key, seq_usable, device):
    ctx_total = LENGTH // TOK_DEV
    per_dev = TOK_DEV // BLOCK
    entry_count = RAND * per_dev
    candidates = ctx_total * RCAP
    ranking = jax.random.permutation(jax.random.fold_in(key, 1), candidates).astype(jnp.int32)
    owner_of = jnp.arange(candidates, dtype=jnp.int32) // RCAP
    usable_owner = owner_of * per_dev < seq_usable
    forced = (device == 0) & (owner_of == 0)
    priority = jnp.where(forced, -1, jnp.where(usable_owner, ranking, candidates + ranking)).astype(jnp.int32)
    chosen = jnp.argsort(priority, stable=True)[:entry_count].astype(jnp.int32)
    owners = chosen // RCAP
    low_block = owners * per_dev
    high_block = jnp.minimum(low_block + per_dev, seq_usable)
    blocks = jax.random.randint(jax.random.fold_in(key, 2), (entry_count,), low_block, high_block)
    blocks = jax.random.permutation(jax.random.fold_in(key, 3), blocks)
    return blocks.reshape(per_dev, RAND).astype(jnp.int32)


def sequence_plan(key):
    base = jax.random.fold_in(key, 11)
    keys_list = jax.random.split(base, 5)
    seq_lens = jax.random.randint(keys_list[0], (SEQS,), LENGTH // 2 + 1, LENGTH + 1)
    filled = jax.random.randint(keys_list[1], (), 0, SEQS)
    seq_lens = jnp.where(jnp.arange(SEQS) == filled, LENGTH, seq_lens).astype(jnp.int32)
    usable = seq_lens // BLOCK
    first_glob = jax.random.randint(keys_list[2], (SEQS,), 0, usable)
    offset = jax.random.randint(keys_list[3], (SEQS,), 1, usable)
    second_glob = (first_glob + offset) % usable
    glob_pairs = jnp.stack([first_glob, second_glob], axis=1).astype(jnp.int32)
    ctx_total = LENGTH // TOK_DEV
    seq_index = jnp.arange(SEQS, dtype=jnp.int32)
    dev_index = jnp.arange(ctx_total, dtype=jnp.int32)

    def per_sequence(seq_number, seq_usable):
        seq_key = jax.random.fold_in(keys_list[4], seq_number)

        def per_device(dev_number):
            return device_random(jax.random.fold_in(seq_key, dev_number), seq_usable, dev_number)
        return jax.vmap(per_device)(dev_index)
    random_blocks = jax.vmap(per_sequence)(seq_index, usable).reshape(SEQS, LENGTH // BLOCK, RAND).astype(jnp.int32)
    return (seq_lens, glob_pairs, random_blocks)


def draw_lengths(key, part):
    return sequence_plan(key)[0]


def draw_global_ids(key, part):
    return sequence_plan(key)[1]


def draw_random_ids(key, part):
    return sequence_plan(key)[2]


def base_values(key, shape):
    return jax.random.normal(key, shape, jnp.float32)


def draw_attn_master(key, part):
    values = base_values(jax.random.fold_in(key, 21), (4, D, D))
    rising = 0.5 + jnp.arange(D, dtype=jnp.float32) / (D - 1)
    scales = jnp.array([D ** (-0.5), D ** (-0.5), D ** (-0.5), 0.5], jnp.float32)
    return (values * rising[None, :, None] * scales[:, None, None]).astype(jnp.float32)


def draw_ffn_master(key, part):
    values = base_values(jax.random.fold_in(key, 22), (2, D, FF))
    rising = 0.5 + jnp.arange(D, dtype=jnp.float32) / (D - 1)
    scales = jnp.array([D ** (-0.5), FF ** (-0.5)], jnp.float32)
    return (values * rising[None, :, None] * scales[:, None, None]).astype(jnp.float32)


def draw_vec_master(key, part):
    normal_part = 0.5 * base_values(jax.random.fold_in(key, 23), (8, D))
    gain_part = jax.random.uniform(jax.random.fold_in(key, 24), (8, D), jnp.float32, 0.5, 1.5)
    row_index = jnp.arange(8)
    is_gain = (row_index == 4) | (row_index == 6)
    return jnp.where(is_gain[:, None], gain_part, normal_part).astype(jnp.float32)


def levels(key, shape, shards, smallest, largest):
    def one(dim, parts):
        draws = jax.random.uniform(jax.random.fold_in(jax.random.fold_in(key, 6), dim), (parts,), jnp.float32, smallest / len(shards), largest / len(shards))
        return jnp.repeat(jnp.exp(draws), shape[dim] // parts).reshape((-1,) + (1,) * (len(shape) - dim - 1))

    loudness = one(*shards[0])
    for cut in shards[1:]:
        loudness = loudness * one(*cut)
    return loudness


def gaussian(rng, extent, deviation, bound, cuts=(), kind=jnp.bfloat16):
    values = jax.random.normal(rng, extent, jnp.float32) * deviation
    if len(cuts) > 0:
        values = levels(rng, extent, cuts, -0.22, 0.18) * values
    return jnp.clip(values, min=-bound, max=bound).astype(kind)


def setup_inputs(seed: int = 0) -> dict:
    streams_of = jax.random.split(jax.random.key(seed), 18)
    return {
        "inputs": gaussian(streams_of[0], (SEQS, LENGTH, D), 1.0, 6.0, ((0, 4), (1, 8))),
        "cotangent": gaussian(streams_of[1], (SEQS, LENGTH, D), 1.0, 6.0, ((0, 4), (1, 8))),
        "lengths": draw_lengths(jax.random.fold_in(streams_of[17], 71), 0),
        "global_ids": draw_global_ids(jax.random.fold_in(streams_of[17], 71), 0),
        "random_ids": draw_random_ids(jax.random.fold_in(streams_of[17], 71), 0),
        "attn_master": draw_attn_master(jax.random.fold_in(streams_of[17], 71), 0),
        "attn_m": gaussian(streams_of[6], (4, D, D), 20.0, 120.0, ((1, 4),), jnp.float32),
        "attn_v": jnp.clip(jnp.exp(math.log(10000.0) - 4.6051702 * jax.random.uniform(streams_of[7], (4, D, D), jnp.float32) ** levels(streams_of[7], (4, D, D), ((1, 4),), -0.2, 0.2)), 100.0, 10000.0),
        "ffn_master": draw_ffn_master(jax.random.fold_in(streams_of[17], 71), 0),
        "ffn_m": gaussian(streams_of[9], (2, D, FF), 20.0, 120.0, ((1, 4),), jnp.float32),
        "ffn_v": jnp.clip(jnp.exp(math.log(10000.0) - 4.6051702 * jax.random.uniform(streams_of[10], (2, D, FF), jnp.float32) ** levels(streams_of[10], (2, D, FF), ((1, 4),), -0.2, 0.2)), 100.0, 10000.0),
        "vec_master": draw_vec_master(jax.random.fold_in(streams_of[17], 71), 0),
        "vec_m": gaussian(streams_of[12], (8, D), 20.0, 120.0, ((1, 4),), jnp.float32),
        "vec_v": jnp.clip(jnp.exp(math.log(10000.0) - 4.6051702 * jax.random.uniform(streams_of[13], (8, D), jnp.float32) ** levels(streams_of[13], (8, D), ((1, 4),), -0.2, 0.2)), 100.0, 10000.0),
        "bias_master": gaussian(streams_of[14], (FF,), 0.5, 3.0, ((0, 4),), jnp.float32),
        "bias_m": gaussian(streams_of[15], (FF,), 20.0, 120.0, ((0, 4),), jnp.float32),
        "bias_v": jnp.clip(jnp.exp(math.log(10000.0) - 4.6051702 * jax.random.uniform(streams_of[16], (FF,), jnp.float32) ** levels(streams_of[16], (FF,), ((0, 4),), -0.2, 0.2)), 100.0, 10000.0),
    }


MASKED_SCORE = -1e+30
LN_EPS = 1e-06
ADAM_EPS = 1e-06
RATIO_EPS = 1e-06
BETA_ONE = 0.5
BETA_TWO = 0.5
WEIGHT_DECAY = 0.01
STEP_RATE = 0.2

@jax.custom_vjp
def low(v):
    return lax.optimization_barrier(v.astype(jnp.bfloat16)).astype(jnp.float32)

@jax.custom_vjp
def low_back(v):
    return v

def low_keep(v):
    return (low(v), None)

def low_pass(kept, grad):
    return (grad,)

def back_keep(v):
    return (v, None)

def back_low(kept, grad):
    return (low(grad),)
low.defvjp(low_keep, low_pass)
low_back.defvjp(back_keep, back_low)

def copy_rounded(weight):
    return lax.optimization_barrier(weight.astype(jnp.bfloat16)).astype(jnp.float32)

def norm_layer(hidden, gain, shift):
    centre = hidden - lax.optimization_barrier(jnp.mean(hidden, axis=-1, keepdims=True))
    spread = lax.optimization_barrier(jnp.mean(centre * centre, axis=-1, keepdims=True))
    return centre * lax.rsqrt(spread + LN_EPS) * gain + shift

def gelu_exact(values):
    return jax.nn.gelu(values, approximate=False)

def softmax_rows(scores):
    expo = jnp.exp(scores - lax.optimization_barrier(jnp.max(scores, axis=-1, keepdims=True)))
    return expo / lax.optimization_barrier(jnp.sum(expo, axis=-1, keepdims=True))

def layer_forward(params, tokens, seq_len, glob_ids, rand_ids):
    attn_weights, ffn_weights, vectors, bias_up = params
    highest = lax.Precision.HIGHEST
    block_total = LENGTH // BLOCK
    scale = HEAD ** (-0.5)
    query_rows = low_back(low(jnp.dot(tokens, attn_weights[0], precision=highest) + vectors[0]))
    key_rows = low_back(low(jnp.dot(tokens, attn_weights[1], precision=highest)))
    value_rows = low_back(low(jnp.dot(tokens, attn_weights[2], precision=highest) + vectors[1]))
    own_blocks = jnp.arange(block_total, dtype=jnp.int32)
    window = jnp.stack([own_blocks - 1, own_blocks, own_blocks + 1], axis=1)
    slot_ids = jnp.concatenate([window, jnp.broadcast_to(glob_ids[None, :], (block_total, 2)), rand_ids], axis=1).astype(jnp.int32)
    slot_count = slot_ids.shape[1]
    slot_rows = slot_ids[:, :, None] * BLOCK + jnp.arange(BLOCK, dtype=jnp.int32)
    slot_valid = (((slot_ids >= 0) & (slot_ids < block_total))[:, :, None] & (slot_rows < seq_len)).reshape(block_total, slot_count * BLOCK)
    key_blocks = key_rows.reshape(block_total, BLOCK, D)
    value_blocks = value_rows.reshape(block_total, BLOCK, D)
    group = min(block_total, max(1, 512 // BLOCK))
    group_count = block_total // group

    def sparse_group(pieces):
        query_part, id_part, valid_part = pieces
        picked = jnp.clip(id_part, 0, block_total - 1)
        key_heads = key_blocks[picked].reshape(group, slot_count * BLOCK, HEADS, HEAD)
        value_heads = value_blocks[picked].reshape(group, slot_count * BLOCK, HEADS, HEAD)
        query_heads = query_part.reshape(group, BLOCK, HEADS, HEAD)
        scores = low_back(jnp.einsum('bqhd,bkhd->bhqk', query_heads, key_heads, precision=highest) * scale)
        scores = jnp.where(valid_part[:, None, None, :], scores, MASKED_SCORE)
        probs = low(softmax_rows(scores))
        mixed = jnp.einsum('bhqk,bkhd->bqhd', probs, value_heads, precision=highest)
        return mixed.reshape(group * BLOCK, D)
    sparse_out = lax.map(jax.checkpoint(sparse_group), (query_rows.reshape(group_count, group, BLOCK, D), slot_ids.reshape(group_count, group, slot_count), slot_valid.reshape(group_count, group, slot_count * BLOCK)))
    attended = sparse_out.reshape(block_total, BLOCK, D)
    glob_query = jnp.concatenate([lax.dynamic_slice_in_dim(query_rows, (glob_ids[slot_index] * BLOCK).astype(jnp.int32), BLOCK, 0) for slot_index in range(2)], axis=0)
    key_valid = jnp.arange(LENGTH, dtype=jnp.int32) < seq_len
    glob_scores = low_back(jnp.einsum('qhd,khd->hqk', glob_query.reshape(2 * BLOCK, HEADS, HEAD), key_rows.reshape(LENGTH, HEADS, HEAD), precision=highest) * scale)
    glob_scores = jnp.where(key_valid[None, None, :], glob_scores, MASKED_SCORE)
    glob_probs = low(softmax_rows(glob_scores))
    glob_out = jnp.einsum('hqk,khd->qhd', glob_probs, value_rows.reshape(LENGTH, HEADS, HEAD), precision=highest).reshape(2, BLOCK, D)
    for slot_index in range(2):
        attended = jnp.where((own_blocks == glob_ids[slot_index])[:, None, None], glob_out[slot_index][None], attended)
    attended = low_back(low(attended.reshape(LENGTH, D)))
    branch = low_back(jnp.dot(attended, attn_weights[3], precision=highest) + vectors[2])
    norm_one = norm_layer(tokens + branch, vectors[4], vectors[5])
    upper = low_back(jnp.dot(low(norm_one), ffn_weights[0], precision=highest) + bias_up)
    hidden = low(gelu_exact(upper))
    down_out = low_back(jnp.dot(hidden, ffn_weights[1].T, precision=highest) + vectors[3])
    result = norm_layer(norm_one + down_out, vectors[6], vectors[7])
    return result * key_valid.astype(jnp.float32)[:, None]

def adam_moments(weight, first, second, grads):
    first_new = BETA_ONE * first + (1.0 - BETA_ONE) * grads
    second_new = BETA_TWO * second + (1.0 - BETA_TWO) * grads * grads
    return (first_new, second_new, first_new / (jnp.sqrt(second_new) + ADAM_EPS))

def reference(inputs, cotangent, lengths, global_ids, random_ids, attn_master, attn_m, attn_v, ffn_master, ffn_m, ffn_v, vec_master, vec_m, vec_v, bias_master, bias_m, bias_v):
    params = (copy_rounded(attn_master), copy_rounded(ffn_master), copy_rounded(vec_master), copy_rounded(bias_master))

    def one_sequence(carry, item):
        tokens, grad_in, seq_len, glob_ids, rand_ids = item

        def forward_only(weights, token_rows):
            return layer_forward(weights, token_rows, seq_len, glob_ids, rand_ids)
        result, pull = jax.vjp(forward_only, params, tokens.astype(jnp.float32))
        grad_params, grad_tokens = pull(grad_in.astype(jnp.float32))
        carry = tuple((total + part for total, part in zip(carry, grad_params)))
        return (carry, (result.astype(jnp.bfloat16), grad_tokens))
    start = tuple((jnp.zeros_like(weight) for weight in params))
    grads, (output, input_grad) = lax.scan(one_sequence, start, (inputs, cotangent, lengths, global_ids, random_ids))
    attn_grad, ffn_grad, vec_grad, bias_grad = grads
    attn_first, attn_second, attn_adam = adam_moments(attn_master, attn_m, attn_v, attn_grad)
    ffn_first, ffn_second, ffn_adam = adam_moments(ffn_master, ffn_m, ffn_v, ffn_grad)
    vec_first, vec_second, vec_adam = adam_moments(vec_master, vec_m, vec_v, vec_grad)
    bias_first, bias_second, bias_adam = adam_moments(bias_master, bias_m, bias_v, bias_grad)
    attn_step = attn_adam + WEIGHT_DECAY * attn_master
    ffn_step = ffn_adam + WEIGHT_DECAY * ffn_master
    weight_sq = jnp.concatenate([lax.optimization_barrier(jnp.sum(attn_master * attn_master, axis=(1, 2))), lax.optimization_barrier(jnp.sum(ffn_master * ffn_master, axis=(1, 2)))])
    step_sq = jnp.concatenate([lax.optimization_barrier(jnp.sum(attn_step * attn_step, axis=(1, 2))), lax.optimization_barrier(jnp.sum(ffn_step * ffn_step, axis=(1, 2)))])
    weight_norm = jnp.sqrt(weight_sq)
    step_norm = jnp.sqrt(step_sq)
    ratios = weight_norm / (step_norm + RATIO_EPS)
    attn_new = attn_master - STEP_RATE * ratios[:4, None, None] * attn_step
    ffn_new = ffn_master - STEP_RATE * ratios[4:, None, None] * ffn_step
    vec_new = vec_master - STEP_RATE * vec_adam
    bias_new = bias_master - STEP_RATE * bias_adam
    norms = jnp.stack([weight_norm, step_norm], axis=1)
    return (output, input_grad, attn_grad, ffn_grad, vec_grad, bias_grad, attn_new, ffn_new, vec_new, bias_new, attn_new.astype(jnp.bfloat16), ffn_new.astype(jnp.bfloat16), vec_new.astype(jnp.bfloat16), bias_new.astype(jnp.bfloat16), attn_first, ffn_first, vec_first, bias_first, attn_second, ffn_second, vec_second, bias_second, norms, ratios)
```

```python
import functools

import jax
import jax.numpy as jnp
from jax import lax
from jax.experimental import pallas as pl
from jax.experimental.pallas import tpu as pltpu
from jax.sharding import PartitionSpec as P

D = 768
HEADS = 12
HEAD = 64
FF = 3072
BLOCK = 64
RAND = 3
SLOTS = 8
PAIRS = HEADS // 2
PAIR = 2 * HEAD

MASKED_SCORE = -1e30
LN_EPS = 1e-06
ADAM_EPS = 1e-06
RATIO_EPS = 1e-06
BETA_ONE = 0.5
BETA_TWO = 0.5
WEIGHT_DECAY = 0.01
STEP_RATE = 0.2

F32 = jnp.float32
BF16 = jnp.bfloat16
NT = (((1,), (1,)), ((), ()))
NN = (((1,), (0,)), ((), ()))
TN = (((0,), (0,)), ((), ()))


def mm(a, b, dims=NN):
    return lax.dot_general(a, b, dims, preferred_element_type=F32)


def stacked_pair(part, half):
    zero = jnp.zeros_like(part)
    return jnp.concatenate([jnp.where(half, part, zero), jnp.where(half, zero, part)], axis=0)


def lane_half(rows):
    return lax.broadcasted_iota(jnp.int32, (rows, PAIR), 1) < HEAD


def slot_mask(nvalid_ref, base):
    lane = lax.broadcasted_iota(jnp.int32, (1, SLOTS * BLOCK), 1)
    limit = jnp.zeros((1, SLOTS * BLOCK), jnp.int32)
    for s in range(SLOTS):
        limit = jnp.where(lane // BLOCK == s, nvalid_ref[base + s], limit)
    return (lane % BLOCK) < limit


def sparse_fwd_kernel(table_ref, nvalid_ref, q_ref, *refs):
    kv = refs[:SLOTS]
    out_ref, lse_ref = refs[SLOTS:]
    ok = slot_mask(nvalid_ref, pl.program_id(0) * SLOTS)
    half = lane_half(BLOCK)
    lane = lax.broadcasted_iota(jnp.int32, (2 * BLOCK, 128), 1)
    lse_all = jnp.zeros((2 * BLOCK, 128), F32)
    for h in range(PAIRS):
        cols = slice(h * PAIR, (h + 1) * PAIR)
        vcols = slice(D + h * PAIR, D + (h + 1) * PAIR)
        q2 = stacked_pair(q_ref[:, cols], half)
        k = jnp.concatenate([r[0, :, cols] for r in kv], axis=0)
        v = jnp.concatenate([r[0, :, vcols] for r in kv], axis=0)
        s = jnp.where(ok, mm(q2, k, NT), MASKED_SCORE)
        top = jnp.max(s, axis=-1, keepdims=True)
        p = jnp.exp(s - top)
        total = jnp.sum(p, axis=-1, keepdims=True)
        o = mm(p.astype(BF16), v) / total
        out_ref[:, cols] = jnp.where(half, o[:BLOCK], o[BLOCK:]).astype(BF16)
        lse_all = jnp.where(lane == h, top + jnp.log(total), lse_all)
    lse_ref[0] = lse_all


def sparse_bwd_kernel(
    table_ref, nvalid_ref, q_ref, do_ref, lse_ref, *refs
):
    kv = refs[:SLOTS]
    dq_ref, rand_ref, near_ref, acc_ref = refs[SLOTS:]
    i = pl.program_id(0)
    ok = slot_mask(nvalid_ref, i * SLOTS)
    half = lane_half(BLOCK)

    @pl.when(i == 0)
    def _():
        acc_ref[...] = jnp.zeros_like(acc_ref)

    glob = acc_ref.shape[0] - 2
    for h in range(PAIRS):
        cols = slice(h * PAIR, (h + 1) * PAIR)
        vcols = slice(D + h * PAIR, D + (h + 1) * PAIR)
        q2 = stacked_pair(q_ref[:, cols], half)
        do2 = stacked_pair(do_ref[:, cols], half)
        k = jnp.concatenate([r[0, :, cols] for r in kv], axis=0)
        v = jnp.concatenate([r[0, :, vcols] for r in kv], axis=0)
        s = jnp.where(ok, mm(q2, k, NT), MASKED_SCORE)
        p = jnp.exp(s - lse_ref[0, :, h : h + 1])
        dp = mm(do2, v, NT)
        ds = (p * (dp - jnp.sum(p * dp, axis=-1, keepdims=True))).astype(BF16)
        dq = mm(ds, k) * (HEAD**-0.5)
        dq_ref[:, cols] = jnp.where(half, dq[:BLOCK], dq[BLOCK:]).astype(BF16)
        dk = mm(ds, q2, TN).reshape(SLOTS, BLOCK, PAIR)
        dv = mm(p.astype(BF16), do2, TN).reshape(SLOTS, BLOCK, PAIR)
        for grad, at in ((dk, cols), (dv, vcols)):
            acc_ref[pl.ds(i, 3), :, at] += grad[:3]
            acc_ref[glob : glob + 2, :, at] += grad[3:5]
            rand_ref[:, :, at] = grad[5:].astype(BF16)

    @pl.when(i == pl.num_programs(0) - 1)
    def _():
        near_ref[...] = acc_ref[...]


def global_fwd_kernel(nvalid_ref, q_ref, kv_ref, out_ref, lse_ref, top_ref, sum_ref, acc_ref):
    c = pl.program_id(0)
    rows = q_ref.shape[0]
    keys = kv_ref.shape[0]

    @pl.when(c == 0)
    def _():
        top_ref[...] = jnp.full_like(top_ref, MASKED_SCORE)
        sum_ref[...] = jnp.zeros_like(sum_ref)
        acc_ref[...] = jnp.zeros_like(acc_ref)

    half = lane_half(rows)

    @pl.when(nvalid_ref[c] > 0)
    def _():
        ok = lax.broadcasted_iota(jnp.int32, (1, keys), 1) < nvalid_ref[c]
        for h in range(PAIRS):
            cols = slice(h * PAIR, (h + 1) * PAIR)
            vcols = slice(D + h * PAIR, D + (h + 1) * PAIR)
            q2 = stacked_pair(q_ref[:, cols], half)
            s = jnp.where(ok, mm(q2, kv_ref[:, cols], NT), MASKED_SCORE)
            before = top_ref[h, :, :1]
            top = jnp.maximum(before, jnp.max(s, axis=-1, keepdims=True))
            p = jnp.exp(s - top)
            shrink = jnp.exp(before - top)
            total = sum_ref[h, :, :1] * shrink + jnp.sum(p, axis=-1, keepdims=True)
            acc_ref[h] = acc_ref[h] * shrink + mm(p.astype(BF16), kv_ref[:, vcols])
            top_ref[h] = jnp.broadcast_to(top, top_ref.shape[1:])
            sum_ref[h] = jnp.broadcast_to(total, sum_ref.shape[1:])

    @pl.when(c == pl.num_programs(0) - 1)
    def _():
        lane = lax.broadcasted_iota(jnp.int32, (2 * rows, 128), 1)
        lse_all = jnp.zeros((2 * rows, 128), F32)
        for h in range(PAIRS):
            cols = slice(h * PAIR, (h + 1) * PAIR)
            total = sum_ref[h, :, :1]
            o = acc_ref[h] / total
            out_ref[:, cols] = jnp.where(half, o[:rows], o[rows:]).astype(BF16)
            lse_all = jnp.where(lane == h, top_ref[h, :, :1] + jnp.log(total), lse_all)
        lse_ref[...] = lse_all


def global_bwd_kernel(
    nvalid_ref, q_ref, do_ref, out_ref, lse_ref, kv_ref, near_ref, used_ref, dq_ref, res_ref
):
    rows = q_ref.shape[0]
    keys = kv_ref.shape[0]
    half = lane_half(rows)
    ok = lax.broadcasted_iota(jnp.int32, (1, keys), 1) < nvalid_ref[0]
    near_rows = near_ref.shape[0]
    for h in range(PAIRS):
        cols = slice(h * PAIR, (h + 1) * PAIR)
        vcols = slice(D + h * PAIR, D + (h + 1) * PAIR)
        q2 = stacked_pair(q_ref[:, cols], half)
        do2 = stacked_pair(do_ref[:, cols], half)
        out2 = stacked_pair(out_ref[:, cols], half)
        dot = jnp.sum(do2.astype(F32) * out2.astype(F32), axis=-1, keepdims=True)
        k = kv_ref[:, cols]
        v = kv_ref[:, vcols]
        p = jnp.where(ok, jnp.exp(mm(q2, k, NT) - lse_ref[:, h : h + 1]), 0.0)
        ds = (p * (mm(do2, v, NT) - dot)).astype(BF16)
        dq = mm(ds, k) * (HEAD**-0.5)
        dq_ref[:, cols] = jnp.where(half, dq[:rows], dq[rows:]).astype(BF16)
        for grad, at in ((mm(ds, q2, TN), cols), (mm(p.astype(BF16), do2, TN), vcols)):
            res_ref[:BLOCK, at] = near_ref[:BLOCK, at].astype(BF16)
            res_ref[BLOCK : BLOCK + keys, at] = (near_ref[BLOCK : BLOCK + keys, at] + grad).astype(
                BF16
            )
            res_ref[BLOCK + keys : near_rows, at] = near_ref[BLOCK + keys : near_rows, at].astype(
                BF16
            )


def pick_blocks_kernel(table_ref, x_ref, out_ref, sems):
    count = out_ref.shape[0]
    copies = []
    for s in range(count):
        copies.append(pltpu.make_async_copy(x_ref.at[table_ref[s]], out_ref.at[s], sems.at[s]))
        copies[-1].start()
    for copy in copies:
        copy.wait()


def place_blocks_kernel(table_ref, x_ref, low_ref, high_ref):
    low_ref[...] = jnp.zeros_like(low_ref)
    high_ref[...] = jnp.zeros_like(high_ref)
    limit = low_ref.shape[0]

    def step(s, carry):
        to = table_ref[s]

        @pl.when(to < limit)
        def _():
            low_ref[to] = (low_ref[to].astype(F32) + x_ref[s].astype(F32)).astype(BF16)

        @pl.when(to >= limit)
        def _():
            high_ref[to - limit] = (
                high_ref[to - limit].astype(F32) + x_ref[s].astype(F32)
            ).astype(BF16)

        return carry

    lax.fori_loop(0, x_ref.shape[0], step, 0)


def whole(shape):
    return pl.BlockSpec(shape, lambda *a: (0,) * len(shape))


VMEM_SPEC = pl.BlockSpec(memory_space=pltpu.VMEM)
SMEM_SPEC = pl.BlockSpec(memory_space=pltpu.SMEM)


def params(limit=None):
    return pltpu.CompilerParams(vmem_limit_bytes=limit)


def cost(flops, moved, exps=0):
    return pl.CostEstimate(flops=int(flops), bytes_accessed=int(moved), transcendentals=int(exps))


def slot_specs():
    return [
        pl.BlockSpec((1, BLOCK, 2 * D), functools.partial(lambda s, i, t, n: (t[i * SLOTS + s], 0, 0), s))
        for s in range(SLOTS)
    ]


def sparse_fwd(table, nvalid, q, kv_blocks):
    rows = q.shape[0]
    blocks = rows // BLOCK
    work = 2 * rows * SLOTS * BLOCK * D
    return pl.pallas_call(
        sparse_fwd_kernel,
        grid_spec=pltpu.PrefetchScalarGridSpec(
            num_scalar_prefetch=2,
            grid=(blocks,),
            in_specs=[pl.BlockSpec((BLOCK, D), lambda i, t, n: (i, 0))] + slot_specs(),
            out_specs=[
                pl.BlockSpec((BLOCK, D), lambda i, t, n: (i, 0)),
                pl.BlockSpec((1, 2 * BLOCK, 128), lambda i, t, n: (i, 0, 0)),
            ],
        ),
        out_shape=[
            jax.ShapeDtypeStruct((rows, D), BF16),
            jax.ShapeDtypeStruct((blocks, 2 * BLOCK, 128), F32),
        ],
        cost_estimate=cost(2 * work, rows * SLOTS * D * 4, rows * SLOTS * BLOCK * HEADS),
        name="sparse_fwd",
    )(table, nvalid, q, *([kv_blocks] * SLOTS))


def sparse_bwd(table, nvalid, q, dout, lse, kv_blocks):
    rows = q.shape[0]
    blocks = rows // BLOCK
    near = blocks + 4
    used = near + RAND * blocks
    work = 2 * rows * SLOTS * BLOCK * D
    return pl.pallas_call(
        sparse_bwd_kernel,
        grid_spec=pltpu.PrefetchScalarGridSpec(
            num_scalar_prefetch=2,
            grid=(blocks,),
            in_specs=[
                pl.BlockSpec((BLOCK, D), lambda i, t, n: (i, 0)),
                pl.BlockSpec((BLOCK, D), lambda i, t, n: (i, 0)),
                pl.BlockSpec((1, 2 * BLOCK, 128), lambda i, t, n: (i, 0, 0)),
            ]
            + slot_specs(),
            out_specs=[
                pl.BlockSpec((BLOCK, D), lambda i, t, n: (i, 0)),
                pl.BlockSpec((RAND, BLOCK, 2 * D), lambda i, t, n: (near // RAND + i, 0, 0)),
                pl.BlockSpec((near, BLOCK, 2 * D), lambda i, t, n: (0, 0, 0)),
            ],
            scratch_shapes=[pltpu.VMEM((near, BLOCK, 2 * D), F32)],
        ),
        out_shape=[
            jax.ShapeDtypeStruct((rows, D), BF16),
            jax.ShapeDtypeStruct((used, BLOCK, 2 * D), BF16),
            jax.ShapeDtypeStruct((near, BLOCK, 2 * D), F32),
        ],
        cost_estimate=cost(5 * work, rows * SLOTS * D * 8, rows * SLOTS * BLOCK * HEADS),
        name="sparse_bwd",
    )(table, nvalid, q, dout, lse, *([kv_blocks] * SLOTS))


def global_fwd(nvalid, q, kv_all):
    rows = q.shape[0]
    chunks = nvalid.shape[0]
    keys = kv_all.shape[0] // chunks
    return pl.pallas_call(
        global_fwd_kernel,
        grid_spec=pltpu.PrefetchScalarGridSpec(
            num_scalar_prefetch=1,
            grid=(chunks,),
            in_specs=[
                pl.BlockSpec((rows, D), lambda c, n: (0, 0)),
                pl.BlockSpec((keys, 2 * D), lambda c, n: (c, 0)),
            ],
            out_specs=[
                pl.BlockSpec((rows, D), lambda c, n: (0, 0)),
                pl.BlockSpec((2 * rows, 128), lambda c, n: (0, 0)),
            ],
            scratch_shapes=[pltpu.VMEM((PAIRS, 2 * rows, 128), F32)] * 3,
        ),
        out_shape=[
            jax.ShapeDtypeStruct((rows, D), BF16),
            jax.ShapeDtypeStruct((2 * rows, 128), F32),
        ],
        cost_estimate=cost(
            4 * rows * kv_all.shape[0] * D, kv_all.size * 2, rows * kv_all.shape[0] * HEADS
        ),
        name="global_fwd",
    )(nvalid, q, kv_all)


def global_bwd(nvalid, q, dout, out, lse, kv_all, near, used):
    rows = q.shape[0]
    near_rows = near.shape[0] * BLOCK
    keys = near_rows - 4 * BLOCK
    near = near.reshape(near_rows, 2 * D)
    used_rows = used.shape[0] * BLOCK
    used = used.reshape(used_rows, 2 * D)
    return pl.pallas_call(
        global_bwd_kernel,
        grid_spec=pltpu.PrefetchScalarGridSpec(
            num_scalar_prefetch=1,
            grid=(1,),
            in_specs=[
                whole((rows, D)),
                whole((rows, D)),
                whole((rows, D)),
                whole((2 * rows, 128)),
                whole((keys, 2 * D)),
                whole((near_rows, 2 * D)),
                pl.BlockSpec(memory_space=pl.ANY),
            ],
            out_specs=[whole((rows, D)), whole((near_rows, 2 * D))],
        ),
        out_shape=[
            jax.ShapeDtypeStruct((rows, D), BF16),
            jax.ShapeDtypeStruct((used_rows, 2 * D), BF16),
        ],
        input_output_aliases={7: 1},
        cost_estimate=cost(10 * rows * keys * D, near_rows * D * 12, rows * keys * HEADS),
        name="global_bwd",
    )(nvalid, q, dout, out, lse, kv_all, near, used)


def pick_blocks(table, x_blocks):
    count = table.shape[0]
    shape = (count,) + x_blocks.shape[1:]
    return pl.pallas_call(
        pick_blocks_kernel,
        in_specs=[SMEM_SPEC, pl.BlockSpec(memory_space=pl.ANY)],
        out_specs=VMEM_SPEC,
        out_shape=jax.ShapeDtypeStruct(shape, BF16),
        scratch_shapes=[pltpu.SemaphoreType.DMA((count,))],
        cost_estimate=cost(0, 4 * count * BLOCK * D),
        name="pick_blocks",
    )(table, x_blocks)


def place_blocks(table, x_blocks, total):
    half = jax.ShapeDtypeStruct((total // 2,) + x_blocks.shape[1:], BF16)
    return pl.pallas_call(
        place_blocks_kernel,
        in_specs=[SMEM_SPEC, VMEM_SPEC],
        out_specs=[VMEM_SPEC, VMEM_SPEC],
        out_shape=[half, half],
        cost_estimate=cost(0, 2 * (total + 2 * x_blocks.shape[0]) * BLOCK * D),
        name="place_blocks",
    )(table, x_blocks)


def exchange(value, mask):
    count = lax.axis_size("ctx")
    return lax.ppermute(value, "ctx", [(i, i ^ mask) for i in range(count)])


def wa_shift(value, step):
    count = lax.axis_size("wa")
    return lax.ppermute(value, "wa", [(i, (i + step) % count) for i in range(count)])


def wa_gather(piece):
    count = lax.axis_size("wa")
    parts = [wa_shift(piece, step) for step in range(count - 1, 0, -1)] + [piece]
    rising = jnp.stack(parts + parts[:-1])
    return lax.dynamic_slice_in_dim(rising, count - 1 - lax.axis_index("wa"), count, 0)


def wa_reduce(chunks):
    count = lax.axis_size("wa")
    rank = lax.axis_index("wa")

    def chunk(step):
        return lax.dynamic_index_in_dim(chunks, (rank + step) % count, 0, keepdims=False)

    arrived = [wa_shift(chunk(step), step) for step in range(1, count)]
    total = chunk(0).astype(F32)
    for part in arrived:
        total = total + part.astype(F32)
    return total


def bit_of(mask):
    return (lax.axis_index("ctx") // mask) % 2 == 1


def gather_relative(own, order, slot_of):
    held = {0: own}
    for mask in order:
        held.update({at ^ slot_of(mask): exchange(part, mask) for at, part in list(held.items())})
    return held


def gather_absolute(own, order, axis):
    value = own
    for mask in order:
        other = exchange(value, mask)
        high = bit_of(mask)
        value = jnp.stack(
            [jnp.where(high, other, value), jnp.where(high, value, other)], axis=axis
        )
    return value


def add_low(first, second):
    return (first.astype(F32) + second.astype(F32)).astype(BF16)


def norm_parts(hidden):
    centre = hidden - jnp.mean(hidden, axis=-1, keepdims=True)
    spread = jnp.mean(centre * centre, axis=-1, keepdims=True)
    inverse = lax.rsqrt(spread + LN_EPS)
    return centre * inverse, inverse


def norm_back(grad, normal, inverse, gain):
    scaled = grad * gain
    return inverse * (
        scaled
        - jnp.mean(scaled, axis=-1, keepdims=True)
        - normal * jnp.mean(scaled * normal, axis=-1, keepdims=True)
    )


def adam_moments(first, second, grads):
    first_new = BETA_ONE * first + (1.0 - BETA_ONE) * grads
    second_new = BETA_TWO * second + (1.0 - BETA_TWO) * grads * grads
    return (first_new, second_new, first_new / (jnp.sqrt(second_new) + ADAM_EPS))


def shards(
    inputs,
    cotangent,
    lengths,
    global_ids,
    random_ids,
    attn_master,
    attn_m,
    attn_v,
    ffn_master,
    ffn_m,
    ffn_v,
    vec_master,
    vec_m,
    vec_v,
    bias_master,
    bias_m,
    bias_v,
):
    x = inputs[0]
    rows = x.shape[0]
    ctx_count = lax.axis_size("ctx")
    rank = lax.axis_index("ctx")
    wa_count = lax.axis_size("wa")
    wa_rank = lax.axis_index("wa")
    blocks = rows // BLOCK
    total_blocks = blocks * ctx_count
    wide = D // wa_count
    ffw = FF // ctx_count
    top = ctx_count // 2
    seq_len = lengths[0]
    glob_ids = global_ids[0]

    def slot_of(index):
        return index // 2 + (index % 2) * top

    def index_of(slot):
        return (slot % top) * 2 + slot // top

    links = [1 << i for i in range(1, ctx_count.bit_length() - 1)]
    if not links:
        links = [1]
    orders = [links[s:] + links[:s] + [1] for s in range(len(links))]
    streams = len(orders)
    my_slot = slot_of(rank)
    relative = jnp.arange(ctx_count, dtype=jnp.int32)
    owner_at = rank ^ index_of(relative)

    part = rows // streams
    held = [
        gather_relative(x[s * part : (s + 1) * part], orders[s], slot_of) for s in range(streams)
    ]
    x_all = jnp.concatenate([held[s][r] for r in range(ctx_count) for s in range(streams)], axis=0)

    attn_low = attn_master.astype(BF16)
    ffn_low = ffn_master.astype(BF16)
    thin = wide // ctx_count
    two = orders[0], orders[1 % streams]

    def row_place(order):
        place = 0
        for at, mask in enumerate(order):
            place = place + jnp.where(bit_of(mask), 1 << at, 0)
        return place

    def attn_stream(pair, order):
        piece = lax.dynamic_slice_in_dim(pair, row_place(order) * thin, thin, 1)
        full = gather_absolute(wa_gather(piece), order, 2)
        full = full.reshape(wa_count, 2, wide, D)
        return full.transpose(1, 0, 2, 3).reshape(2, D, D)

    kv_weights = attn_stream(attn_low[1:3], two[1])
    qo_weights = attn_stream(jnp.stack([attn_low[0], attn_low[3]]), two[0])
    w_query, w_out = qo_weights[0], qo_weights[1]
    w_kv = jnp.concatenate([kv_weights[0], kv_weights[1]], axis=1)

    ffn_piece = lax.dynamic_slice_in_dim(ffn_low, my_slot * ffw, ffw, 2)
    ffn_piece = wa_gather(ffn_piece)
    up_held = gather_relative(ffn_piece[:, 0].reshape(D, ffw), two[0], slot_of)
    down_held = gather_relative(ffn_piece[:, 1].reshape(D, ffw), two[1], slot_of)
    w_up = jnp.concatenate([up_held[r] for r in range(ctx_count)], axis=1)
    w_down = jnp.concatenate([down_held[r] for r in range(ctx_count)], axis=1)

    small = wa_gather(
        jnp.concatenate([vec_master.astype(BF16).reshape(-1), bias_master.astype(BF16)])
    )
    vectors = (
        small[:, : 8 * wide].reshape(wa_count, 8, wide).transpose(1, 0, 2).reshape(8, D)
    ).astype(F32)
    bias_blocks = small[:, 8 * wide :].reshape(ctx_count, ffw).astype(F32)
    bias_up = bias_blocks[my_slot ^ relative].reshape(FF)

    def place_of(block):
        block = jnp.clip(block, 0, total_blocks - 1)
        return slot_of((block // blocks) ^ rank) * blocks + block % blocks

    rand_ids = random_ids[0]
    own_blocks = rank * blocks + jnp.arange(blocks, dtype=jnp.int32)
    window = jnp.stack([own_blocks - 1, own_blocks, own_blocks + 1], axis=1)
    slot_ids = jnp.concatenate(
        [window, jnp.broadcast_to(glob_ids[None, :], (blocks, 2)), rand_ids], axis=1
    )
    slot_table = place_of(slot_ids).reshape(-1)
    slot_nvalid = jnp.where(
        (slot_ids >= 0) & (slot_ids < total_blocks), jnp.clip(seq_len - slot_ids * BLOCK, 0, BLOCK), 0
    ).reshape(-1)
    used_ids = jnp.concatenate(
        [
            rank * blocks - 1 + jnp.arange(blocks + 2, dtype=jnp.int32),
            glob_ids,
            rand_ids.reshape(-1),
        ]
    )
    used_table = place_of(used_ids)
    chunk_nvalid = jnp.clip(seq_len - owner_at * rows, 0, rows)
    positions = rank * rows + jnp.arange(rows, dtype=jnp.int32)
    row_weight = (positions < seq_len).astype(F32)[:, None]
    hits = own_blocks[None, :] == glob_ids[:, None]

    scale = HEAD**-0.5
    query = ((mm(x, w_query) + vectors[0]).astype(BF16) * BF16(scale)).astype(BF16)
    kv_bias = jnp.concatenate([jnp.zeros((D,), F32), vectors[1]])
    kv_all = (mm(x_all, w_kv) + kv_bias).astype(BF16)
    kv_blocks = kv_all.reshape(total_blocks, BLOCK, 2 * D)
    x_blocks = x_all.reshape(total_blocks, BLOCK, D)
    x_used = pick_blocks(used_table, x_blocks)
    x_glob = x_used[blocks + 2 : blocks + 4].reshape(2 * BLOCK, D)
    glob_query = ((mm(x_glob, w_query) + vectors[0]).astype(BF16) * BF16(scale)).astype(BF16)
    glob_out, glob_lse = global_fwd(chunk_nvalid, glob_query, kv_all)
    sparse_out, lse = sparse_fwd(slot_table, slot_nvalid, query, kv_blocks)
    attended = sparse_out.reshape(blocks, BLOCK, D)
    for g in range(2):
        attended = jnp.where(
            hits[g][:, None, None], glob_out[g * BLOCK : (g + 1) * BLOCK][None], attended
        )
    attended = attended.reshape(rows, D)

    first_sum = x.astype(F32) + mm(attended, w_out) + vectors[2]
    normal_one, inverse_one = norm_parts(first_sum)
    norm_one = normal_one * vectors[4] + vectors[5]
    norm_low = norm_one.astype(BF16)
    upper = mm(norm_low, w_up) + bias_up
    cdf = 0.5 * (1.0 + lax.erf(upper * (0.5**0.5)))
    hidden_low = (upper * cdf).astype(BF16)
    slope = cdf + upper * (jnp.exp(-0.5 * upper * upper) * 0.3989422804014327)
    second_sum = norm_one + mm(hidden_low, w_down, NT) + vectors[3]
    normal_two, inverse_two = norm_parts(second_sum)
    output = ((normal_two * vectors[6] + vectors[7]) * row_weight).astype(BF16)
    grad_out = cotangent[0].astype(F32) * row_weight
    grad_second = norm_back(grad_out, normal_two, inverse_two, vectors[6])
    grad_down = grad_second.astype(BF16)
    grad_upper = (mm(grad_down, w_down) * slope).astype(BF16)
    grad_norm = grad_second + mm(grad_upper, w_up, NT)
    grad_first = norm_back(grad_norm, normal_one, inverse_one, vectors[4])
    grad_branch = grad_first.astype(BF16)
    grad_attended = mm(grad_branch, w_out, NT).astype(BF16)

    def reduce_slots(keep, sent, order):
        held = add_low(keep, exchange(sent, 1)).reshape(D, top, ffw)
        slots = list(range(top))
        parts = {r: held[:, r] for r in slots}
        for mask in order:
            bit = slot_of(mask)
            stay = [r for r in parts if not r & bit]
            arrived = exchange(jnp.stack([parts[r | bit] for r in stay]), mask)
            parts = {r: add_low(parts[r], arrived[at]) for at, r in enumerate(stay)}
        return parts[0].reshape(wa_count, wide, ffw)

    cut = FF // 2
    up_sent = mm(norm_low, grad_upper[:, cut:], TN).astype(BF16)
    up_keep = mm(norm_low, grad_upper[:, :cut], TN).astype(BF16)
    down_sent = mm(grad_down, hidden_low[:, cut:], TN).astype(BF16)
    down_keep = mm(grad_down, hidden_low[:, :cut], TN).astype(BF16)
    up_sum = reduce_slots(up_keep, up_sent, two[0][:-1])
    down_sum = reduce_slots(down_keep, down_sent, two[1][:-1])
    ffn_mine = wa_reduce(jnp.stack([up_sum, down_sum], axis=1)).astype(BF16)

    def slots_in_order(piece, order):
        value = piece[None]
        for mask in sorted(order[:-1]) + [1]:
            other = exchange(value, mask)
            high = bit_of(mask)
            value = jnp.concatenate(
                [jnp.where(high, other, value), jnp.where(high, value, other)], axis=0
            )
        return value.transpose(1, 0, 2).reshape(wide, FF)

    grad_blocks = grad_attended.reshape(blocks, BLOCK, D)
    glob_part = jnp.sum(
        jnp.where(hits[:, :, None, None], grad_blocks[None], 0), axis=1, dtype=F32
    ).astype(BF16)
    for mask in [1] + links if ctx_count > 2 else [1]:
        glob_part = glob_part + exchange(glob_part, mask)
    grad_glob = glob_part.reshape(2 * BLOCK, D)
    grad_sparse = jnp.where((hits[0] | hits[1])[:, None, None], 0, grad_blocks).reshape(rows, D)
    grad_query, used_grads, near = sparse_bwd(
        slot_table, slot_nvalid, query, grad_sparse, lse, kv_blocks
    )
    glob_dquery, used_grads = global_bwd(
        chunk_nvalid[:1], glob_query, grad_glob, glob_out, glob_lse, kv_all, near, used_grads
    )

    dx_used = mm(used_grads, w_kv, NT)
    near_rows = (blocks + 2) * BLOCK
    dx_glob = dx_used[near_rows : near_rows + 2 * BLOCK] + mm(glob_dquery, w_query, NT)
    dx_used = lax.dynamic_update_slice(dx_used, dx_glob, (near_rows, 0)).astype(BF16)
    dx_keep, dx_sent = place_blocks(
        used_table, dx_used.reshape(used_table.shape[0], BLOCK, D), total_blocks
    )
    dx_held = add_low(dx_keep, exchange(dx_sent, 1)).reshape(top, streams, part, D)
    dx_own = []
    for s in range(streams):
        parts = {r: dx_held[r, s] for r in range(top)}
        for mask in orders[s][:-1] if ctx_count > 2 else []:
            bit = slot_of(mask)
            stay = [r for r in parts if not r & bit]
            arrived = exchange(jnp.stack([parts[r | bit] for r in stay]), mask)
            parts = {r: add_low(parts[r], arrived[at]) for at, r in enumerate(stay)}
        dx_own.append(parts[0])
    input_grad = (
        grad_first + mm(grad_query, w_query, NT) + jnp.concatenate(dx_own, axis=0).astype(F32)
    )

    used_rows = x_used.reshape(-1, D)
    query_rows = jnp.concatenate([x, x_glob], axis=0)
    query_grads = jnp.concatenate([grad_query, glob_dquery], axis=0)
    g_query = mm(query_rows, query_grads, TN).astype(BF16)
    g_kv = mm(used_rows, used_grads, TN).astype(BF16)
    g_out = mm(attended, grad_branch, TN).astype(BF16)

    def reduce_rows(mats, order):
        count = mats.shape[0]
        mats = mats.reshape(count, D, 2, D // 2)
        mine = rank % 2
        sent = lax.dynamic_index_in_dim(mats, 1 - mine, 2, keepdims=False)
        keep = lax.dynamic_index_in_dim(mats, mine, 2, keepdims=False)
        held = add_low(keep, exchange(sent, 1))
        held = held.reshape(count, wa_count, wide, D // 2)
        length = wide
        for mask in order[:-1] if ctx_count > 2 else []:
            length //= 2
            high = bit_of(mask).astype(jnp.int32)
            sent = lax.dynamic_slice_in_dim(held, (1 - high) * length, length, 2)
            keep = lax.dynamic_slice_in_dim(held, high * length, length, 2)
            held = add_low(keep, exchange(sent, mask))
        return held.transpose(1, 0, 2, 3)

    def rows_in_order(piece, order):
        value = piece
        for mask in (order[:-1] if ctx_count > 2 else [])[::-1]:
            other = exchange(value, mask)
            high = bit_of(mask)
            value = jnp.concatenate(
                [jnp.where(high, other, value), jnp.where(high, value, other)], axis=1
            )
        other = exchange(value, 1)
        high = bit_of(1)
        return jnp.concatenate(
            [jnp.where(high, other, value), jnp.where(high, value, other)], axis=2
        )

    first_pair = reduce_rows(jnp.stack([g_query, g_out]), two[0])
    second_pair = reduce_rows(jnp.stack([g_kv[:, :D], g_kv[:, D:]]), two[1])
    first_mine = wa_reduce(first_pair).astype(BF16)
    second_mine = wa_reduce(second_pair).astype(BF16)

    vec_local = jnp.stack(
        [
            jnp.sum(query_grads, axis=0, dtype=F32),
            jnp.sum(used_grads[:, D:], axis=0, dtype=F32),
            jnp.sum(grad_branch, axis=0, dtype=F32),
            jnp.sum(grad_down, axis=0, dtype=F32),
            jnp.sum(grad_norm * normal_one, axis=0),
            jnp.sum(grad_norm, axis=0),
            jnp.sum(grad_out * normal_two, axis=0),
            jnp.sum(grad_out, axis=0),
        ]
    )
    bias_local = jnp.sum(grad_upper, axis=0, dtype=F32).reshape(ctx_count, ffw)[
        my_slot ^ relative
    ]
    small_local = jnp.concatenate(
        [
            vec_local.reshape(8, wa_count, wide).transpose(1, 0, 2).reshape(wa_count, 8 * wide),
            bias_local.reshape(wa_count, FF // wa_count),
        ],
        axis=1,
    )
    small_sum = wa_reduce(small_local)
    for mask in [1] + links if ctx_count > 2 else [1]:
        small_sum = small_sum + exchange(small_sum, mask)
    vec_grad = small_sum[: 8 * wide].reshape(8, wide)
    bias_grad = small_sum[8 * wide :]

    ffn_grad = jnp.stack(
        [slots_in_order(ffn_mine[0], two[0]), slots_in_order(ffn_mine[1], two[1])]
    ).astype(F32)
    first_full = rows_in_order(first_mine, two[0]).astype(F32)
    second_full = rows_in_order(second_mine, two[1]).astype(F32)
    attn_grad = jnp.stack([first_full[0], second_full[0], second_full[1], first_full[1]])

    attn_first, attn_second, attn_adam = adam_moments(attn_m, attn_v, attn_grad)
    ffn_first, ffn_second, ffn_adam = adam_moments(ffn_m, ffn_v, ffn_grad)
    vec_first, vec_second, vec_adam = adam_moments(vec_m, vec_v, vec_grad)
    bias_first, bias_second, bias_adam = adam_moments(bias_m, bias_v, bias_grad)
    attn_step = attn_adam + WEIGHT_DECAY * attn_master
    ffn_step = ffn_adam + WEIGHT_DECAY * ffn_master
    squares = jnp.concatenate(
        [
            jnp.sum(attn_master * attn_master, axis=(1, 2)),
            jnp.sum(ffn_master * ffn_master, axis=(1, 2)),
            jnp.sum(attn_step * attn_step, axis=(1, 2)),
            jnp.sum(ffn_step * ffn_step, axis=(1, 2)),
        ]
    )
    squares = jnp.sum(wa_gather(squares), axis=0)
    weight_norm = jnp.sqrt(squares[:6])
    step_norm = jnp.sqrt(squares[6:])
    ratios = weight_norm / (step_norm + RATIO_EPS)
    attn_new = attn_master - STEP_RATE * ratios[:4, None, None] * attn_step
    ffn_new = ffn_master - STEP_RATE * ratios[4:, None, None] * ffn_step
    vec_new = vec_master - STEP_RATE * vec_adam
    bias_new = bias_master - STEP_RATE * bias_adam
    norms = jnp.stack([weight_norm, step_norm], axis=1)
    return (
        output[None],
        input_grad[None],
        attn_grad,
        ffn_grad,
        vec_grad,
        bias_grad,
        attn_new,
        ffn_new,
        vec_new,
        bias_new,
        attn_new.astype(BF16),
        ffn_new.astype(BF16),
        vec_new.astype(BF16),
        bias_new.astype(BF16),
        attn_first,
        ffn_first,
        vec_first,
        bias_first,
        attn_second,
        ffn_second,
        vec_second,
        bias_second,
        norms,
        ratios,
    )


def solution(mesh):
    tokens = P("wa", "ctx", None)
    mats = P(None, "wa", None)
    vecs = P(None, "wa")
    line = P("wa")
    state = (mats, mats, vecs, line)
    in_specs = (
        (tokens, tokens, P("wa"), P("wa", None), tokens)
        + (mats,) * 6
        + (vecs,) * 3
        + (line,) * 3
    )
    out_specs = (tokens, tokens) + state * 5 + (P(), P())
    return jax.shard_map(shards, mesh=mesh, in_specs=in_specs, out_specs=out_specs, check_vma=False)
```

```python
import functools

import jax
import jax.numpy as jnp
from jax import lax
from jax.experimental import pallas as pl
from jax.experimental.pallas import tpu as pltpu
from jax.sharding import PartitionSpec as P


D = 768
HEADS = 12
HEAD = 64
FF = 3072
BLOCK = 64
RAND = 3
SLOTS = 8
PAIRS = HEADS // 2
PAIR = 2 * HEAD
QUADS = HEADS // 4
QUAD = 4 * HEAD

MASKED_SCORE = -1e30
LN_EPS = 1e-06
ADAM_EPS = 1e-06
RATIO_EPS = 1e-06
BETA_ONE = 0.5
BETA_TWO = 0.5
WEIGHT_DECAY = 0.01
STEP_RATE = 0.2

CTX = "ctx"
WA = "wa"

F32 = jnp.float32
BF16 = jnp.bfloat16
NT = (((1,), (1,)), ((), ()))
NN = (((1,), (0,)), ((), ()))
TN = (((0,), (0,)), ((), ()))


def mm(a, b, dims=NN):
    return lax.dot_general(a, b, dims, preferred_element_type=F32)


def heads_apart(part):
    lane = lax.broadcasted_iota(jnp.int32, part.shape, 1) // HEAD
    zero = jnp.zeros_like(part)
    return jnp.concatenate(
        [jnp.where(lane == head, part, zero) for head in range(part.shape[1] // HEAD)], axis=0
    )


def heads_joined(parts):
    count = parts.shape[1] // HEAD
    rows = parts.shape[0] // count
    lane = lax.broadcasted_iota(jnp.int32, (rows, parts.shape[1]), 1) // HEAD
    joined = parts[:rows]
    for head in range(1, count):
        joined = jnp.where(lane == head, parts[head * rows : (head + 1) * rows], joined)
    return joined


FRINGE = 4


def window_places(i, blocks):
    before = jnp.where(i == 0, blocks, i - 1)
    after = jnp.where(i == blocks - 1, blocks + 1, i + 1)
    return before, i, after


def slot_scores(keys, queries, nvalid_ref, base):
    s = mm(keys, queries, NT)
    row = lax.broadcasted_iota(jnp.int32, (BLOCK, s.shape[1]), 0)
    parts = [
        jnp.where(row < nvalid_ref[base + at], s[at * BLOCK : (at + 1) * BLOCK], MASKED_SCORE)
        for at in range(3)
    ]
    return jnp.concatenate(parts + [s[3 * BLOCK :]], axis=0)


def slot_rows(near_ref, rand_ref, i, columns):
    blocks = near_ref.shape[0] - FRINGE
    places = window_places(i, blocks) + (blocks + 2, blocks + 3)
    rows = [near_ref[at, :, columns] for at in places]
    return jnp.concatenate(rows + [rand_ref[at, :, columns] for at in range(RAND)], axis=0)


def sparse_fwd_kernel(nvalid_ref, q_ref, near_ref, rand_ref, out_ref, lse_ref):
    i = pl.program_id(0)
    for h in range(QUADS):
        cols = slice(h * QUAD, (h + 1) * QUAD)
        vcols = slice(D + h * QUAD, D + (h + 1) * QUAD)
        queries = heads_apart(q_ref[:, cols])
        k = slot_rows(near_ref, rand_ref, i, cols)
        v = slot_rows(near_ref, rand_ref, i, vcols)
        s = slot_scores(k, queries, nvalid_ref, i * 3)
        top = jnp.max(s, axis=0, keepdims=True)
        p = jnp.exp(s - top)
        total = jnp.sum(p, axis=0, keepdims=True)
        p = (p * (1.0 / total)).astype(BF16)
        out_ref[:, cols] = heads_joined(mm(p, v, TN)).astype(BF16)
        lse_ref[0, h : h + 1, :] = top + jnp.log(total)


def sparse_bwd_kernel(
    nvalid_ref, q_ref, do_ref, lse_ref, near_ref, rand_ref, dq_ref, grads_ref, acc_ref
):
    i = pl.program_id(0)

    @pl.when(i == 0)
    def _():
        acc_ref[...] = jnp.zeros_like(acc_ref)

    blocks = near_ref.shape[0] - FRINGE
    places = window_places(i, blocks) + (blocks + 2, blocks + 3)
    for h in range(QUADS):
        cols = slice(h * QUAD, (h + 1) * QUAD)
        vcols = slice(D + h * QUAD, D + (h + 1) * QUAD)
        queries = heads_apart(q_ref[:, cols])
        douts = heads_apart(do_ref[:, cols])
        k = slot_rows(near_ref, rand_ref, i, cols)
        v = slot_rows(near_ref, rand_ref, i, vcols)
        s = slot_scores(k, queries, nvalid_ref, i * 3)
        p = jnp.exp(s - lse_ref[0, h : h + 1, :])
        dp = mm(v, douts, NT)
        ds = (p * (dp - jnp.sum(p * dp, axis=0, keepdims=True))).astype(BF16)
        dq = heads_joined(mm(ds, k, TN)) * (HEAD**-0.5)
        dq_ref[:, cols] = dq.astype(BF16)
        dk = mm(ds, queries).reshape(SLOTS, BLOCK, QUAD)
        dv = mm(p.astype(BF16), douts).reshape(SLOTS, BLOCK, QUAD)
        for grad, to in ((dk, cols), (dv, vcols)):
            for at, place in enumerate(places):
                acc_ref[place, :, to] += grad[at]
            grads_ref[:, :, to] = grad[len(places) :].astype(BF16)


def piece_copies(held, slot, buf_ref, sems, to):
    group, place = divmod(slot, GROUP)
    side, place = divmod(place, 4)
    own, first, second, up, low = held[10 * group + 5 * side : 10 * group + 5 * side + 5]
    half = buf_ref.shape[1] // 2
    if place < 3:
        return [pltpu.make_async_copy((own, first, second)[place], buf_ref.at[to], sems.at[to, 0])]
    return [
        pltpu.make_async_copy(up, buf_ref.at[to, pl.ds(0, half)], sems.at[to, 0]),
        pltpu.make_async_copy(low, buf_ref.at[to, pl.ds(half, half)], sems.at[to, 1]),
    ]


def global_fwd_kernel(pair_ref, nvalid_ref, q_ref, k_ref, v_ref, b_ref, *refs):
    held = refs[:-6]
    out_ref, top_ref, sum_ref, acc_ref, buf_ref, sems = refs[-6:]
    c = pl.program_id(0)
    rows = q_ref.shape[0]
    keys = buf_ref.shape[1]
    count = len(held) // 10 * GROUP

    @pl.when(c == 0)
    def _():
        top_ref[...] = jnp.full_like(top_ref, MASKED_SCORE)
        sum_ref[...] = jnp.zeros_like(sum_ref)
        acc_ref[...] = jnp.zeros_like(acc_ref)

    for at in range(count):

        @pl.when(c == at)
        def _():
            if at == 0:
                for copy in piece_copies(held, 0, buf_ref, sems, 0):
                    copy.start()
            if at + 1 < count:
                for copy in piece_copies(held, at + 1, buf_ref, sems, (at + 1) % 2):
                    copy.start()
            for copy in piece_copies(held, at, buf_ref, sems, at % 2):
                copy.wait()

    @pl.when(nvalid_ref[c] > 0)
    def _():
        x = buf_ref[lax.rem(c, 2)]
        k = mm(x, k_ref[...]).astype(BF16)
        v = (mm(x, v_ref[...]) + b_ref[...]).astype(BF16)
        ok = lax.broadcasted_iota(jnp.int32, (keys, 2 * rows), 0) < nvalid_ref[c]
        s = jnp.where(ok, mm(k, heads_apart(q_ref[...]), NT), MASKED_SCORE)
        before = top_ref[...]
        top = jnp.maximum(before, jnp.max(s, axis=0, keepdims=True))
        p = jnp.exp(s - top)
        shrink = jnp.exp(before - top)
        sum_ref[...] = sum_ref[...] * shrink + jnp.sum(p, axis=0, keepdims=True)
        acc_ref[...] = acc_ref[...] * shrink + mm(v, p.astype(BF16), TN)
        top_ref[...] = top

    @pl.when(c == pl.num_programs(0) - 1)
    def _():
        total = sum_ref[...]
        lse = top_ref[...] + jnp.log(total)
        out_ref[:rows] = heads_joined((acc_ref[...] / total).T)
        out_ref[rows : rows + 1] = lse[:, :rows]
        out_ref[rows + 1 : rows + 2] = lse[:, rows:]
        out_ref[rows + 2 :] = jnp.zeros((6, PAIR), F32)


def global_bwd_kernel(
    nvalid_ref, q_ref, do_ref, out_ref, kv_ref, near_ref, used_ref, own_ref, dq_ref, res_ref
):
    rows = q_ref.shape[0]
    keys = kv_ref.shape[0]
    ok = lax.broadcasted_iota(jnp.int32, (keys, 2 * rows), 0) < nvalid_ref[0]
    dq_ref[:rows] = jnp.zeros((rows, D), BF16)
    for h in range(PAIRS):
        cols = slice(h * PAIR, (h + 1) * PAIR)
        vcols = slice(D + h * PAIR, D + (h + 1) * PAIR)
        queries = heads_apart(q_ref[:, cols])
        douts = heads_apart(do_ref[:, cols])
        outs = jnp.concatenate([out_ref[h, :rows], out_ref[h, :rows]], axis=0)
        dot = jnp.sum((douts.astype(F32) * outs).T, axis=0, keepdims=True)
        lse = jnp.concatenate(
            [out_ref[h, rows : rows + 1], out_ref[h, rows + 1 : rows + 2]], axis=1
        )
        k = kv_ref[:, cols]
        v = kv_ref[:, vcols]
        p = jnp.where(ok, jnp.exp(mm(k, queries, NT) - lse), 0.0)
        ds = (p * (mm(v, douts, NT) - dot)).astype(BF16)
        dq = heads_joined(mm(ds, k, TN)) * (HEAD**-0.5)
        dq_ref[rows:, cols] = dq.astype(BF16)
        for grad, at in ((mm(ds, queries), cols), (mm(p.astype(BF16), douts), vcols)):
            res_ref[:keys, at] = (near_ref[:keys, at] + grad).astype(BF16)
            res_ref[keys:, at] = near_ref[keys:, at].astype(BF16)


def kv_used_kernel(source_ref, index_ref, w_ref, b_ref, *refs):
    held = refs[:-4]
    kv_ref, x_ref, buf_ref, sems = refs[-4:]
    step = pl.program_id(0)
    count = buf_ref.shape[1] // BLOCK

    def rows_of(to, at):
        return buf_ref.at[to, pl.ds(at * BLOCK, BLOCK)]

    def fetch(group, to):
        for at in range(count):
            place = group * count + at
            for which, ref in enumerate(held):

                @pl.when(source_ref[place] == which)
                def _():
                    start = pl.multiple_of(index_ref[place] * BLOCK, BLOCK)
                    pltpu.make_async_copy(
                        ref.at[pl.ds(start, BLOCK)], rows_of(to, at), sems.at[to, at]
                    ).start()

    now = lax.rem(step, 2)

    @pl.when(step == 0)
    def _():
        fetch(0, 0)

    @pl.when(step + 1 < pl.num_programs(0))
    def _():
        fetch(step + 1, 1 - now)

    for at in range(count):
        pltpu.make_async_copy(
            held[0].at[pl.ds(0, BLOCK)], rows_of(now, at), sems.at[now, at]
        ).wait()
    rows = buf_ref[now]
    x_ref[...] = rows
    kv_ref[...] = (mm(rows, w_ref[...]) + b_ref[...]).astype(BF16)


def place_blocks_kernel(table_ref, x_ref, q_ref, low_ref, high_ref):
    low_ref[...] = jnp.zeros_like(low_ref)
    high_ref[...] = jnp.zeros_like(high_ref)
    limit = low_ref.shape[0]

    def step(s, with_query):
        to = table_ref[s]
        part = x_ref[s] + q_ref[s] if with_query else x_ref[s]

        @pl.when(to < limit)
        def _():
            low_ref[to] += part

        @pl.when(to >= limit)
        def _():
            high_ref[to - limit] += part

    @pl.loop(0, q_ref.shape[0])
    def _(s):
        step(s, True)

    @pl.loop(q_ref.shape[0], x_ref.shape[0])
    def _(s):
        step(s, False)


def whole(shape):
    return pl.BlockSpec(shape, lambda *a: (0,) * len(shape))


VMEM_SPEC = pl.BlockSpec(memory_space=pltpu.VMEM)
SMEM_SPEC = pl.BlockSpec(memory_space=pltpu.SMEM)


def cost(flops, moved, exps=0):
    return pl.CostEstimate(flops=int(flops), bytes_accessed=int(moved), transcendentals=int(exps))


def near_spec(near):
    return pl.BlockSpec((near, BLOCK, 2 * D), lambda i, n: (0, 0, 0))


def rand_spec(near):
    return pl.BlockSpec((RAND, BLOCK, 2 * D), lambda i, n: (near // RAND + i, 0, 0))


def sparse_fwd(nvalid, q, kv_used):
    rows = q.shape[0]
    blocks = rows // BLOCK
    near = blocks + FRINGE
    work = 2 * rows * SLOTS * BLOCK * D
    return pl.pallas_call(
        sparse_fwd_kernel,
        grid_spec=pltpu.PrefetchScalarGridSpec(
            num_scalar_prefetch=1,
            grid=(blocks,),
            in_specs=[
                pl.BlockSpec((BLOCK, D), lambda i, n: (i, 0)),
                near_spec(near),
                rand_spec(near),
            ],
            out_specs=[
                pl.BlockSpec((BLOCK, D), lambda i, n: (i, 0)),
                pl.BlockSpec((1, 8, QUAD), lambda i, n: (i, 0, 0)),
            ],
        ),
        out_shape=[
            jax.ShapeDtypeStruct((rows, D), BF16),
            jax.ShapeDtypeStruct((blocks, 8, QUAD), F32),
        ],
        cost_estimate=cost(2 * work, rows * SLOTS * D * 4, rows * SLOTS * BLOCK * HEADS),
        name="sf",
    )(nvalid, q, kv_used, kv_used)


def sparse_bwd(nvalid, q, dout, lse, kv_used):
    rows = q.shape[0]
    blocks = rows // BLOCK
    near = blocks + FRINGE
    used = kv_used.shape[0]
    work = 2 * rows * SLOTS * BLOCK * D
    return pl.pallas_call(
        sparse_bwd_kernel,
        grid_spec=pltpu.PrefetchScalarGridSpec(
            num_scalar_prefetch=1,
            grid=(blocks,),
            in_specs=[
                pl.BlockSpec((BLOCK, D), lambda i, n: (i, 0)),
                pl.BlockSpec((BLOCK, D), lambda i, n: (i, 0)),
                pl.BlockSpec((1, 8, QUAD), lambda i, n: (i, 0, 0)),
                near_spec(near),
                rand_spec(near),
            ],
            out_specs=[
                pl.BlockSpec((BLOCK, D), lambda i, n: (i, 0)),
                rand_spec(near),
                near_spec(near),
            ],
        ),
        out_shape=[
            jax.ShapeDtypeStruct((near * BLOCK, D), BF16),
            jax.ShapeDtypeStruct((used, BLOCK, 2 * D), BF16),
            jax.ShapeDtypeStruct((near, BLOCK, 2 * D), F32),
        ],
        cost_estimate=cost(5 * work, rows * SLOTS * D * 8, rows * SLOTS * BLOCK * HEADS),
        name="sb",
    )(nvalid, q, dout, lse, kv_used, kv_used)


def global_fwd(pair, nvalid, q, w_kv, kv_bias, held):
    rows = q.shape[0]
    chunks = nvalid.shape[0]
    keys = held[0].shape[0]
    return pl.pallas_call(
        global_fwd_kernel,
        grid_spec=pltpu.PrefetchScalarGridSpec(
            num_scalar_prefetch=2,
            grid=(chunks,),
            in_specs=[
                pl.BlockSpec((rows, PAIR), lambda c, p, n: (0, p[0])),
                pl.BlockSpec((D, PAIR), lambda c, p, n: (0, p[0])),
                pl.BlockSpec((D, PAIR), lambda c, p, n: (0, PAIRS + p[0])),
                pl.BlockSpec((1, PAIR), lambda c, p, n: (0, PAIRS + p[0])),
            ]
            + [pl.BlockSpec(memory_space=pl.ANY)] * len(held),
            out_specs=pl.BlockSpec((rows + 8, PAIR), lambda c, p, n: (0, 0)),
            scratch_shapes=[pltpu.VMEM((1, 2 * rows), F32)] * 2
            + [
                pltpu.VMEM((PAIR, 2 * rows), F32),
                pltpu.VMEM((2, keys, D), BF16),
                pltpu.SemaphoreType.DMA((2, 2)),
            ],
        ),
        out_shape=jax.ShapeDtypeStruct((rows + 8, PAIR), F32),
        cost_estimate=cost(
            4 * (rows + D) * chunks * keys * PAIR,
            2 * chunks * keys * D,
            2 * rows * chunks * keys,
        ),
        name="gf",
    )(pair[None], nvalid, q, w_kv, w_kv, kv_bias, *held)


def global_bwd(nvalid, q, dout, out, kv_used, near, used, dq):
    rows = q.shape[0]
    near_rows = near.shape[0] * BLOCK
    keys = near_rows - FRINGE * BLOCK
    near = near.reshape(near_rows, 2 * D)
    used_rows = used.shape[0] * BLOCK
    fringe = FRINGE * BLOCK
    return pl.pallas_call(
        global_bwd_kernel,
        grid_spec=pltpu.PrefetchScalarGridSpec(
            num_scalar_prefetch=1,
            grid=(1,),
            in_specs=[
                whole((rows, D)),
                whole((rows, D)),
                whole(out.shape),
                whole((keys, 2 * D)),
                whole((near_rows, 2 * D)),
                pl.BlockSpec(memory_space=pl.ANY),
                pl.BlockSpec(memory_space=pl.ANY),
            ],
            out_specs=[
                pl.BlockSpec((fringe, D), lambda i, n: (keys // fringe, 0)),
                whole((near_rows, 2 * D)),
            ],
        ),
        out_shape=[
            jax.ShapeDtypeStruct((near_rows, D), BF16),
            jax.ShapeDtypeStruct((used_rows, 2 * D), BF16),
        ],
        input_output_aliases={6: 1, 7: 0},
        cost_estimate=cost(10 * rows * keys * D, near_rows * D * 12, rows * keys * HEADS),
        name="gb",
    )(
        nvalid,
        q,
        dout,
        out,
        kv_used.reshape(used_rows, 2 * D),
        near,
        used.reshape(used_rows, 2 * D),
        dq,
    )


def kv_used_rows(source, index, w_kv, kv_bias, held):
    count = source.shape[0]
    each = 4
    rows = each * BLOCK
    return pl.pallas_call(
        kv_used_kernel,
        grid_spec=pltpu.PrefetchScalarGridSpec(
            num_scalar_prefetch=2,
            grid=(count // each,),
            in_specs=[whole((D, 2 * D)), whole((1, 2 * D))]
            + [pl.BlockSpec(memory_space=pl.ANY)] * len(held),
            out_specs=[
                pl.BlockSpec((rows, 2 * D), lambda t, *a: (t, 0)),
                pl.BlockSpec((rows, D), lambda t, *a: (t, 0)),
            ],
            scratch_shapes=[
                pltpu.VMEM((2, rows, D), BF16),
                pltpu.SemaphoreType.DMA((2, each)),
            ],
        ),
        out_shape=[
            jax.ShapeDtypeStruct((count * BLOCK, 2 * D), BF16),
            jax.ShapeDtypeStruct((count * BLOCK, D), BF16),
        ],
        cost_estimate=cost(4 * count * BLOCK * D * D, 8 * count * BLOCK * D),
        name="kv",
    )(source, index, w_kv, kv_bias, *held)


def place_blocks(table, x_blocks, q_blocks, total):
    half = jax.ShapeDtypeStruct((total // 2,) + x_blocks.shape[1:], BF16)
    return pl.pallas_call(
        place_blocks_kernel,
        in_specs=[SMEM_SPEC, VMEM_SPEC, VMEM_SPEC],
        out_specs=[VMEM_SPEC, VMEM_SPEC],
        out_shape=[half, half],
        cost_estimate=cost(0, 2 * (total + 2 * x_blocks.shape[0]) * BLOCK * D),
        name="pb",
    )(table, x_blocks, q_blocks)


CORE, FIRST, SECOND = 1, 2, 4
GROUP = 8
CUT = 3 * D // GROUP + D // GROUP


def exchange(value, mask):
    count = lax.axis_size(CTX)
    return lax.ppermute(value, CTX, [(i, i ^ mask) for i in range(count)])


def slot_of(index):
    return index // GROUP * GROUP + index // 2 % 4 + index % 2 * 4


def index_of(slot):
    return slot // GROUP * GROUP + slot % 4 * 2 + slot // 4 % 2


def spare_masks():
    return [1 << i for i in range(3, lax.axis_size(CTX).bit_length() - 1)]


def all_masks():
    return [CORE, FIRST, SECOND] + spare_masks()


def wa_shift(value, step):
    count = lax.axis_size(WA)
    return lax.ppermute(value, WA, [(i, (i + step) % count) for i in range(count)])


def wa_parts(piece):
    return [piece] + [wa_shift(piece, step) for step in range(1, lax.axis_size(WA))]


def wa_reduce(chunks):
    count = lax.axis_size(WA)
    rank = lax.axis_index(WA)

    def chunk(step):
        return lax.dynamic_index_in_dim(chunks, (rank + step) % count, 0, keepdims=False)

    arrived = [wa_shift(chunk(step), step) for step in range(1, count)]
    total = chunk(0).astype(F32)
    for part in arrived:
        total = total + part.astype(F32)
    return total


def wa_total(value):
    count = lax.axis_size(WA)
    rank = lax.axis_index(WA)
    parts = jnp.stack(wa_parts(value))
    total = parts[rank % count]
    for index in range(1, count):
        total = total + parts[(rank - index) % count]
    return total


def bit_of(mask):
    return (lax.axis_index(CTX) // mask) % 2 == 1


def gather_group(own, then=None):
    cut = own.shape[0] // 2
    first = exchange(own, FIRST)
    second = exchange(own, SECOND)
    upper, lower = first[:cut], second[cut:]
    if then is not None:
        upper, lower, then = lax.optimization_barrier((upper, lower, then))
    upper = exchange(upper, SECOND)
    lower = exchange(lower, FIRST)
    near = [own, first, second, upper, lower]
    held = near + [exchange(part, CORE) for part in near]
    return held if then is None else (held, then)


def group_in_order(own):
    value = own[None]
    for mask in (FIRST, SECOND, CORE):
        other = exchange(value, mask)
        high = bit_of(mask)
        value = jnp.concatenate(
            [jnp.where(high, other, value), jnp.where(high, value, other)], axis=0
        )
    return value


def add_low(first, second):
    return (first.astype(F32) + second.astype(F32)).astype(BF16)


def cut_kernel(where_ref, attn_ref, ffn_ref, vec_ref, bias_ref, attn_out, ffn_out):
    wide = attn_ref.shape[1]
    attn_out[:wide, :] = attn_ref[0].astype(BF16)
    small = jnp.concatenate([vec_ref[...], bias_ref[...], jnp.zeros((4, wide), F32)], axis=0)
    attn_out[wide:, :wide] = small.astype(BF16)
    attn_out[wide:, wide:] = jnp.zeros((16, CUT - wide), BF16)
    ffn_out[:, :CUT] = ffn_ref[0].astype(BF16)
    ffn_out[:, CUT:] = ffn_ref[1].astype(BF16)


def cut_pieces(slot, attn_master, ffn_master, vec_master, bias_rows):
    wide = attn_master.shape[1]
    return pl.pallas_call(
        cut_kernel,
        grid_spec=pltpu.PrefetchScalarGridSpec(
            num_scalar_prefetch=1,
            grid=(1,),
            in_specs=[
                pl.BlockSpec((1, wide, CUT), lambda i, w: (w[0] // 2, 0, w[0] % 2)),
                pl.BlockSpec((2, wide, CUT), lambda i, w: (0, 0, w[0])),
                whole((8, wide)),
                whole((4, wide)),
            ],
            out_specs=[whole((wide + 16, CUT)), whole((wide, 2 * CUT))],
        ),
        out_shape=[
            jax.ShapeDtypeStruct((wide + 16, CUT), BF16),
            jax.ShapeDtypeStruct((wide, 2 * CUT), BF16),
        ],
        cost_estimate=cost(0, wide * CUT * 18),
        name="cut",
    )(slot[None], attn_master, ffn_master, vec_master, bias_rows)


def join_kernel(rank_ref, *refs):
    parts, outs = refs[: len(refs) - 2], refs[len(refs) - 2 :]
    count = len(parts)
    wide = outs[0].shape[0] // count
    for step, part in enumerate(parts):
        at = lax.rem(rank_ref[0] - step + count, count)
        outs[0][pl.ds(pl.multiple_of(at * wide, 16), wide), :] = part[:wide]
        outs[1][at] = part[part.shape[0] - 16 :]


def join_rows(rank, parts):
    count = len(parts)
    extra = parts[0].shape[0] % 32
    wide = parts[0].shape[0] - extra
    columns = parts[0].shape[1]
    return pl.pallas_call(
        join_kernel,
        in_specs=[SMEM_SPEC] + [VMEM_SPEC] * count,
        out_specs=[VMEM_SPEC, VMEM_SPEC],
        out_shape=[
            jax.ShapeDtypeStruct((count * wide, columns), BF16),
            jax.ShapeDtypeStruct((count, 16, columns), BF16),
        ],
        cost_estimate=cost(0, 4 * count * wide * columns),
        name="join",
    )(rank[None], *parts)


def held_specs(rows, columns, tiles):
    shape = (rows // tiles, columns)
    middle = tiles // 2
    each = [
        pl.BlockSpec(shape, lambda t, *a: (t, 0)),
        pl.BlockSpec(shape, lambda t, *a: (t, 0)),
        pl.BlockSpec(shape, lambda t, *a: (t, 0)),
        pl.BlockSpec(shape, lambda t, *a: (jnp.minimum(t, middle - 1), 0)),
        pl.BlockSpec(shape, lambda t, *a: (jnp.maximum(t - middle, 0), 0)),
    ]
    return each + each


def for_each_slot(held, body):
    upper = pl.program_id(0) < pl.num_programs(0) // 2
    for side in range(2):
        own, first, second, up, low = held[5 * side : 5 * side + 5]
        for at, ref in enumerate((own, first, second)):
            body(4 * side + at, ref)
        pl.when(upper)(functools.partial(body, 4 * side + 3, up))
        pl.when(jnp.logical_not(upper))(functools.partial(body, 4 * side + 3, low))


def attn_weights_kernel(slot_ref, *refs):
    held, (q_ref, kv_ref, o_ref) = refs[:10], refs[10:]

    def body(slot, ref):
        at = slot_ref[0] ^ slot
        for out, start, stop in ((q_ref, 0, 2), (kv_ref, 2, 6), (o_ref, 6, 8)):

            @pl.when((at >= start) & (at < stop))
            def _():
                out[:, pl.ds(pl.multiple_of((at - start) * CUT, 128), CUT)] = ref[...]

    for_each_slot(held, body)


def attn_weights(slot, held):
    rows = held[0].shape[0]
    tiles = 4
    size = rows // tiles
    widths = (D, 2 * D, D)
    return pl.pallas_call(
        attn_weights_kernel,
        grid_spec=pltpu.PrefetchScalarGridSpec(
            num_scalar_prefetch=1,
            grid=(tiles,),
            in_specs=held_specs(rows, CUT, tiles),
            out_specs=[pl.BlockSpec((size, w), lambda t, *a: (t, 0)) for w in widths],
        ),
        out_shape=[jax.ShapeDtypeStruct((rows, w), BF16) for w in widths],
        cost_estimate=cost(0, 4 * rows * GROUP * CUT),
        name="aw",
    )(slot[None], *held)


STRIDE = 2


def matrix_copies(held, step, up_ref, down_ref, sems, to):
    jobs = []
    for at in range(STRIDE):
        side, place = divmod(step * STRIDE + at, 4)
        own, first, second, upper, lower = held[5 * side : 5 * side + 5]
        half = D // 2
        parts = [((own, first, second)[place], 0, D)] if place < 3 else [(upper, 0, half), (lower, half, half)]
        for ref, start, size in parts:
            for which, buf in enumerate((up_ref, down_ref)):
                source = ref.at[:, pl.ds(which * CUT, CUT)]
                target = buf.at[to, pl.ds(start, size), pl.ds(at * CUT, CUT)]
                jobs.append(pltpu.make_async_copy(source, target, sems.at[to, len(jobs)]))
    return jobs


def fetch_matrices(held, up_ref, down_ref, sems):
    step = pl.program_id(0)
    for at in range(GROUP // STRIDE):

        @pl.when(step == at)
        def _():
            if at == 0:
                for copy in matrix_copies(held, 0, up_ref, down_ref, sems, 0):
                    copy.start()
            if at + 1 < GROUP // STRIDE:
                for copy in matrix_copies(held, at + 1, up_ref, down_ref, sems, (at + 1) % 2):
                    copy.start()
            for copy in matrix_copies(held, at, up_ref, down_ref, sems, at % 2):
                copy.wait()

    return lax.rem(step, 2)


def add_up(total_ref, part):
    @pl.when(pl.program_id(0) == 0)
    def _():
        total_ref[...] = part

    @pl.when(pl.program_id(0) > 0)
    def _():
        total_ref[...] += part


def ffn_fwd_kernel(n_ref, b_ref, *refs):
    held = refs[:10]
    hidden_ref, slope_ref, total_ref, w_up_ref, w_down_ref, up_ref, down_ref, sems = refs[10:]
    now = fetch_matrices(held, up_ref, down_ref, sems)
    up = mm(n_ref[...], up_ref[now]) + b_ref[0]
    cdf = 0.5 * (1.0 + lax.erf(up * (0.5**0.5)))
    hidden = (up * cdf).astype(BF16)
    hidden_ref[...] = hidden
    slope_ref[...] = (cdf + up * (jnp.exp(-0.5 * up * up) * 0.3989422804014327)).astype(BF16)
    add_up(total_ref, mm(hidden, down_ref[now], NT))
    w_up_ref[...] = up_ref[now]
    w_down_ref[...] = down_ref[now]


def ffn_scratch():
    buf = pltpu.VMEM((2, D, STRIDE * CUT), BF16)
    return [buf, buf, pltpu.SemaphoreType.DMA((2, 4 * STRIDE))]


def ffn_fwd(norm_low, bias, held):
    rows = norm_low.shape[0]
    wide = pl.BlockSpec((rows, STRIDE * CUT), lambda t: (0, t))
    full = pl.BlockSpec((D, STRIDE * CUT), lambda t: (0, t))
    return pl.pallas_call(
        ffn_fwd_kernel,
        grid=(GROUP // STRIDE,),
        in_specs=[whole((rows, D)), pl.BlockSpec((1, 1, STRIDE * CUT), lambda t: (t, 0, 0))]
        + [pl.BlockSpec(memory_space=pl.ANY)] * 10,
        out_specs=[wide, wide, whole((rows, D)), full, full],
        out_shape=[
            jax.ShapeDtypeStruct((rows, FF), BF16),
            jax.ShapeDtypeStruct((rows, FF), BF16),
            jax.ShapeDtypeStruct((rows, D), F32),
            jax.ShapeDtypeStruct((D, FF), BF16),
            jax.ShapeDtypeStruct((D, FF), BF16),
        ],
        scratch_shapes=ffn_scratch(),
        cost_estimate=cost(4 * rows * D * FF, 4 * rows * FF + 4 * D * FF, 2 * rows * FF),
        name="ff",
    )(norm_low, bias.reshape(-1, 1, STRIDE * CUT), *held)


def spread_kernel(slot_ref, *refs, read):
    keep = refs[: len(refs) - 5]
    x_ref, y_ref, own_ref, first_ref, second_ref = refs[len(refs) - 5 :]
    upper = pl.program_id(0) < pl.num_programs(0) // 2

    def part(slot):
        return read(slot_ref, keep, slot).astype(BF16)

    own_ref[...] = part(0)

    @pl.when(upper)
    def _():
        x_ref[0] = part(3)
        x_ref[1] = part(1)
        second_ref[...] = part(2)

    @pl.when(jnp.logical_not(upper))
    def _():
        y_ref[0] = part(3)
        y_ref[1] = part(2)
        first_ref[...] = part(1)


def read_ffn(slot_ref, refs, slot):
    at = slice(slot * CUT, (slot + 1) * CUT)
    up, down, up_in, down_in = (r[:, at].astype(F32) for r in refs)
    return jnp.concatenate([up + up_in, down + down_in], axis=1)


def read_attn(slot_ref, refs, slot):
    at = (slot_ref[0] ^ slot) % 4
    columns = pl.ds(pl.multiple_of(at % 2 * CUT, 128), CUT)
    return refs[0][at // 2, :, columns].astype(F32) + refs[1][at // 2, :, columns].astype(F32)


def read_rows(slot_ref, refs, slot):
    return refs[0][slot].astype(F32) + refs[1][slot].astype(F32)


def spread(slot, arrays, in_specs, rows, columns, read, tiles):
    size = rows // tiles
    middle = tiles // 2
    low = lambda t: jnp.minimum(t, middle - 1)
    high = lambda t: jnp.maximum(t - middle, 0)
    half = jax.ShapeDtypeStruct((rows // 2, columns), BF16)
    pair = jax.ShapeDtypeStruct((2, rows // 2, columns), BF16)
    return pl.pallas_call(
        functools.partial(spread_kernel, read=read),
        grid_spec=pltpu.PrefetchScalarGridSpec(
            num_scalar_prefetch=1,
            grid=(tiles,),
            in_specs=in_specs,
            out_specs=[
                pl.BlockSpec((2, size, columns), lambda t, *a: (0, low(t), 0)),
                pl.BlockSpec((2, size, columns), lambda t, *a: (0, high(t), 0)),
                pl.BlockSpec((size, columns), lambda t, *a: (t, 0)),
                pl.BlockSpec((size, columns), lambda t, *a: (high(t), 0)),
                pl.BlockSpec((size, columns), lambda t, *a: (low(t), 0)),
            ],
        ),
        out_shape=[pair, pair, jax.ShapeDtypeStruct((rows, columns), BF16), half, half],
        cost_estimate=cost(0, rows * columns * 24),
    )(slot[None], *arrays)


def reduce_group(slot, arrays, in_specs, rows, columns, read, tiles=4):
    x_out, y_out, own, first, second = spread(slot, arrays, in_specs, rows, columns, read, tiles)
    x_in = exchange(x_out, FIRST)
    y_in = exchange(y_out, SECOND)
    x_last = exchange(add_low(first, y_in[0]), FIRST)
    y_last = exchange(add_low(second, x_in[0]), SECOND)
    cut = rows // 2
    upper = own[:cut].astype(F32) + x_in[1].astype(F32) + y_last.astype(F32)
    lower = own[cut:].astype(F32) + y_in[1].astype(F32) + x_last.astype(F32)
    return upper, lower


def adam_kernel(slot_ref, *refs, pieces):
    held = refs[:10]
    w_ref, m_ref, v_ref, grad_ref, first_ref, second_ref, step_ref, sums_ref = refs[10:]

    def body(slot, ref):
        at = slot_ref[0] ^ slot
        if pieces == 1:
            columns = pl.ds(pl.multiple_of(at % 2 * CUT, 128), CUT)
            grad_ref[at // 2, :, columns] = ref[...].astype(F32)
        else:
            columns = pl.ds(pl.multiple_of(at * CUT, 128), CUT)
            grad_ref[0, :, columns] = ref[:, :CUT].astype(F32)
            grad_ref[1, :, columns] = ref[:, CUT:].astype(F32)

    for_each_slot(held, body)

    @pl.when(pl.program_id(0) == 0)
    def _():
        sums_ref[...] = jnp.zeros_like(sums_ref)

    mats, rows, columns = grad_ref.shape
    each = 8 if columns > D else 24

    @pl.loop(0, mats * (rows // each))
    def _(step):
        mat = step // (rows // each)
        here = pl.ds(pl.multiple_of(step % (rows // each) * each, each), each)
        grad = grad_ref[mat, here]
        first = BETA_ONE * m_ref[mat, here] + (1.0 - BETA_ONE) * grad
        second = BETA_TWO * v_ref[mat, here] + (1.0 - BETA_TWO) * grad * grad
        weight = w_ref[mat, here]
        move = first / (jnp.sqrt(second) + ADAM_EPS) + WEIGHT_DECAY * weight
        first_ref[mat, here] = first
        second_ref[mat, here] = second
        step_ref[mat, here] = move
        for row, part in ((mat, weight), (mats + mat, move)):
            sums_ref[row] += jnp.sum((part * part).reshape(each // 8, 8, columns), axis=0)


def final(ratios, master, step):
    new = master - (STEP_RATE * ratios)[:, None, None] * step
    return new, new.astype(BF16)


def adam(slot, held, master, first, second):
    mats, wide, columns = master.shape
    tiles = 2
    size = wide // tiles
    piece_columns = held[0].shape[1]
    block = pl.BlockSpec((mats, size, columns), lambda t, *a: (0, t, 0))
    full = jax.ShapeDtypeStruct(master.shape, F32)
    return pl.pallas_call(
        functools.partial(adam_kernel, pieces=piece_columns // CUT),
        grid_spec=pltpu.PrefetchScalarGridSpec(
            num_scalar_prefetch=1,
            grid=(tiles,),
            in_specs=held_specs(wide, piece_columns, tiles) + [block] * 3,
            out_specs=[block] * 4 + [whole((2 * mats, 8, columns))],
        ),
        out_shape=[full] * 4 + [jax.ShapeDtypeStruct((2 * mats, 8, columns), F32)],
        cost_estimate=cost(20 * master.size, 30 * master.size, master.size),
    )(slot[None], *held, master, first, second)


def norm_parts(hidden):
    centre = hidden - jnp.mean(hidden, axis=-1, keepdims=True)
    spread = jnp.mean(centre * centre, axis=-1, keepdims=True)
    inverse = lax.rsqrt(spread + LN_EPS)
    return centre * inverse, inverse


def norm_back(grad, normal, inverse, gain):
    scaled = grad * gain
    return inverse * (
        scaled
        - jnp.mean(scaled, axis=-1, keepdims=True)
        - normal * jnp.mean(scaled * normal, axis=-1, keepdims=True)
    )


def adam_moments(first, second, grads):
    first_new = BETA_ONE * first + (1.0 - BETA_ONE) * grads
    second_new = BETA_TWO * second + (1.0 - BETA_TWO) * grads * grads
    return (first_new, second_new, first_new / (jnp.sqrt(second_new) + ADAM_EPS))


def shards(
    inputs,
    cotangent,
    lengths,
    global_ids,
    random_ids,
    attn_master,
    attn_m,
    attn_v,
    ffn_master,
    ffn_m,
    ffn_v,
    vec_master,
    vec_m,
    vec_v,
    bias_master,
    bias_m,
    bias_v,
):
    x = inputs[0]
    rows = x.shape[0]
    ctx_count = lax.axis_size(CTX)
    rank = lax.axis_index(CTX)
    wa_count = lax.axis_size(WA)
    wa_rank = lax.axis_index(WA)
    blocks = rows // BLOCK
    total_blocks = blocks * ctx_count
    wide = D // wa_count
    seq_len = lengths[0]
    glob_ids = global_ids[0]
    my_slot = slot_of(rank) % GROUP
    relative = jnp.arange(ctx_count, dtype=jnp.int32)
    owner_at = rank ^ index_of(relative)

    attn_piece, ffn_piece = cut_pieces(
        my_slot, attn_master, ffn_master, vec_master, bias_master.reshape(4, wide)
    )
    attn_parts = wa_parts(attn_piece)
    x_held, attn_parts = gather_group(x, attn_parts)
    attn_rows, small = join_rows(wa_rank, attn_parts)
    attn_held = gather_group(attn_rows)
    w_query, w_kv, w_out = attn_weights(my_slot, attn_held)
    ffn_parts = wa_parts(ffn_piece)
    ffn_parts, w_kv = lax.optimization_barrier((ffn_parts, w_kv))
    ffn_rows, _ = join_rows(wa_rank, ffn_parts)
    ffn_held = gather_group(ffn_rows)

    small = small[:, :, :wide]
    vectors = small[:, :8].transpose(1, 0, 2).reshape(8, D).astype(F32)
    bias_blocks = small[:, 8:12].reshape(GROUP, CUT).astype(F32)
    bias_up = bias_blocks[my_slot ^ relative[:GROUP]]

    def place_of(block):
        block = jnp.clip(block, 0, total_blocks - 1)
        return slot_of((block // blocks) ^ rank) * blocks + block % blocks

    rand_ids = random_ids[0]
    own_blocks = rank * blocks + jnp.arange(blocks, dtype=jnp.int32)
    window = jnp.stack([own_blocks - 1, own_blocks, own_blocks + 1], axis=1)
    window_nvalid = jnp.where(
        (window >= 0) & (window < total_blocks), jnp.clip(seq_len - window * BLOCK, 0, BLOCK), 0
    ).reshape(-1)
    used_table = place_of(
        jnp.concatenate(
            [own_blocks, own_blocks[:1] - 1, own_blocks[-1:] + 1, glob_ids, rand_ids.reshape(-1)]
        )
    )
    used_slot, used_at = used_table // blocks, used_table % blocks
    split = (used_slot % 4 == 3) & (used_at >= blocks // 2)
    used_source = used_slot // 4 * 5 + used_slot % 4 + split
    used_index = used_at - jnp.where(split, blocks // 2, 0)
    chunk_nvalid = jnp.clip(seq_len - owner_at * rows, 0, rows)
    positions = rank * rows + jnp.arange(rows, dtype=jnp.int32)
    row_weight = (positions < seq_len).astype(F32)[:, None]
    hits = own_blocks[None, :] == glob_ids[:, None]

    scale = HEAD**-0.5
    kv_bias = jnp.concatenate([jnp.zeros((D,), F32), vectors[1]])[None]
    groups = [x_held]
    for mask in spare_masks():
        groups += [[exchange(part, mask) for part in held] for held in groups]
    x_held = [part for held in groups for part in held]
    kv_used, x_used = kv_used_rows(used_source, used_index, w_kv, kv_bias, x_held)
    near_rows = (blocks + FRINGE) * BLOCK
    x_near = x_used[:near_rows]
    x_glob = x_near[near_rows - 2 * BLOCK :]
    kv_used = kv_used.reshape(-1, BLOCK, 2 * D)
    glob_query = ((mm(x_glob, w_query) + vectors[0]).astype(BF16) * BF16(scale)).astype(BF16)
    glob_part = global_fwd(
        jnp.minimum(my_slot, PAIRS - 1), chunk_nvalid, glob_query, w_kv, kv_bias, x_held
    )
    glob_pairs = group_in_order(glob_part)
    query = ((mm(x, w_query, NN) + vectors[0]).astype(BF16) * BF16(scale)).astype(BF16)
    sparse_out, lse = sparse_fwd(window_nvalid, query, kv_used)
    glob_out = (
        glob_pairs[:PAIRS, : 2 * BLOCK].transpose(1, 0, 2).reshape(2, BLOCK, D).astype(BF16)
    )
    attended = sparse_out.reshape(blocks, BLOCK, D)
    for g in range(2):
        attended = jnp.where(hits[g][:, None, None], glob_out[g][None], attended)
    attended = attended.reshape(rows, D)

    first_sum = x.astype(F32) + mm(attended, w_out) + vectors[2]
    normal_one, inverse_one = norm_parts(first_sum)
    norm_one = normal_one * vectors[4] + vectors[5]
    norm_low = norm_one.astype(BF16)
    hidden_low, slope, down, w_up, w_down = ffn_fwd(norm_low, bias_up, ffn_held)
    second_sum = norm_one + down + vectors[3]
    normal_two, inverse_two = norm_parts(second_sum)
    output = ((normal_two * vectors[6] + vectors[7]) * row_weight).astype(BF16)
    grad_out = cotangent[0].astype(F32) * row_weight
    grad_second = norm_back(grad_out, normal_two, inverse_two, vectors[6])
    grad_down = grad_second.astype(BF16)
    grad_upper = (mm(grad_down, w_down) * slope.astype(F32)).astype(BF16)
    grad_norm = grad_second + mm(grad_upper, w_up, NT)
    grad_first = norm_back(grad_norm, normal_one, inverse_one, vectors[4])
    grad_branch = grad_first.astype(BF16)
    grad_attended = mm(grad_branch, w_out, NT).astype(BF16)

    cut = FF // 2
    up_sent = mm(norm_low, grad_upper[:, cut:], TN).astype(BF16)
    down_sent = mm(grad_down, hidden_low[:, cut:], TN).astype(BF16)
    up_keep = mm(norm_low, grad_upper[:, :cut], TN).astype(BF16)
    down_keep = mm(grad_down, hidden_low[:, :cut], TN).astype(BF16)
    tiles = 4
    ffn_spec = pl.BlockSpec((D // tiles, cut), lambda t, *a: (t, 0))

    def finish(upper, lower):
        total = jnp.concatenate([upper, lower], axis=0).astype(BF16)
        for mask in spare_masks():
            total = add_low(total, exchange(total, mask))
        return wa_reduce(total.reshape(wa_count, wide, total.shape[1])).astype(BF16)

    ffn_mine = finish(
        *reduce_group(
            my_slot,
            [up_keep, down_keep, exchange(up_sent, CORE), exchange(down_sent, CORE)],
            [ffn_spec] * 4,
            D,
            2 * CUT,
            read_ffn,
            tiles,
        ),
    )
    ffn_grad, ffn_first, ffn_second, ffn_step, ffn_sums = adam(
        my_slot, gather_group(ffn_mine), ffn_master, ffn_m, ffn_v
    )

    grad_blocks = grad_attended.reshape(blocks, BLOCK, D)
    glob_part = jnp.sum(
        jnp.where(hits[:, :, None, None], grad_blocks[None], 0), axis=1, dtype=F32
    ).astype(BF16)
    for mask in all_masks():
        glob_part = glob_part + exchange(glob_part, mask)
    grad_glob = glob_part.reshape(2 * BLOCK, D)
    grad_sparse = jnp.where((hits[0] | hits[1])[:, None, None], 0, grad_blocks).reshape(rows, D)
    near_dquery, used_grads, near = sparse_bwd(window_nvalid, query, grad_sparse, lse, kv_used)
    near_dquery, used_grads = global_bwd(
        chunk_nvalid[:1], glob_query, grad_glob, glob_pairs, kv_used, near, used_grads, near_dquery
    )

    g_query = mm(x_near, near_dquery, TN).astype(BF16)
    g_kv = mm(x_used, used_grads, TN).astype(BF16)
    g_key, g_value = g_kv[:, :D], g_kv[:, D:]
    g_out = mm(attended, grad_branch, TN).astype(BF16)
    on_core = bit_of(CORE)
    early, late = jnp.stack([g_query, g_key]), jnp.stack([g_value, g_out])
    attn_sent = jnp.where(on_core, early, late)
    attn_keep = jnp.where(on_core, late, early)
    attn_spec = pl.BlockSpec((2, D // tiles, D), lambda t, *a: (0, t, 0))
    attn_mine = finish(
        *reduce_group(
            my_slot,
            [attn_keep, exchange(attn_sent, CORE)],
            [attn_spec] * 2,
            D,
            CUT,
            read_attn,
            tiles,
        ),
    )
    attn_grad, attn_first, attn_second, attn_step, attn_sums = adam(
        my_slot, gather_group(attn_mine), attn_master, attn_m, attn_v
    )

    dx_used = mm(used_grads, w_kv, NT).astype(BF16)
    dx_query = mm(near_dquery, w_query, NT).astype(BF16)
    dx_keep, dx_sent = place_blocks(
        used_table,
        dx_used.reshape(-1, BLOCK, D),
        dx_query.reshape(-1, BLOCK, D),
        total_blocks,
    )
    for mask in spare_masks()[::-1]:
        dx_keep = add_low(dx_keep, exchange(dx_sent, mask))
        dx_keep, dx_sent = jnp.split(dx_keep, 2, axis=0)
    dx_spec = pl.BlockSpec((4, rows // tiles, D), lambda t, *a: (0, t, 0))
    dx_own = reduce_group(
        my_slot,
        [dx_keep.reshape(4, rows, D), exchange(dx_sent, CORE).reshape(4, rows, D)],
        [dx_spec] * 2,
        rows,
        D,
        read_rows,
        tiles,
    )
    input_grad = grad_first + jnp.concatenate(dx_own, axis=0)

    vec_local = jnp.stack(
        [
            jnp.sum(near_dquery, axis=0, dtype=F32),
            jnp.sum(used_grads[:, D:], axis=0, dtype=F32),
            jnp.sum(grad_branch, axis=0, dtype=F32),
            jnp.sum(grad_down, axis=0, dtype=F32),
            jnp.sum(grad_norm * normal_one, axis=0),
            jnp.sum(grad_norm, axis=0),
            jnp.sum(grad_out * normal_two, axis=0),
            jnp.sum(grad_out, axis=0),
        ]
    )
    bias_local = jnp.sum(grad_upper, axis=0, dtype=F32).reshape(GROUP, CUT)[
        my_slot ^ relative[:GROUP]
    ]
    small_local = jnp.concatenate(
        [
            vec_local.reshape(8, wa_count, wide).transpose(1, 0, 2).reshape(wa_count, 8 * wide),
            bias_local.reshape(wa_count, FF // wa_count),
        ],
        axis=1,
    )
    small_sum = wa_reduce(small_local)
    for mask in all_masks():
        small_sum = small_sum + exchange(small_sum, mask)
    vec_grad = small_sum[: 8 * wide].reshape(8, wide)
    bias_grad = small_sum[8 * wide :]

    vec_first, vec_second, vec_adam = adam_moments(vec_m, vec_v, vec_grad)
    bias_first, bias_second, bias_adam = adam_moments(bias_m, bias_v, bias_grad)

    def ratio_of(sums):
        squares = jnp.sqrt(wa_total(jnp.sum(sums, axis=(1, 2))))
        count = squares.shape[0] // 2
        return squares[:count], squares[count:], squares[:count] / (squares[count:] + RATIO_EPS)

    ffn_norm, ffn_length, ffn_ratio = ratio_of(ffn_sums)
    ffn_new, ffn_copy = final(ffn_ratio, ffn_master, ffn_step)
    attn_norm, attn_length, attn_ratio = ratio_of(attn_sums)
    attn_new, attn_copy = final(attn_ratio, attn_master, attn_step)
    ratios = jnp.concatenate([attn_ratio, ffn_ratio])
    norms = jnp.stack(
        [
            jnp.concatenate([attn_norm, ffn_norm]),
            jnp.concatenate([attn_length, ffn_length]),
        ],
        axis=1,
    )
    vec_new = vec_master - STEP_RATE * vec_adam
    bias_new = bias_master - STEP_RATE * bias_adam
    return (
        output[None],
        input_grad[None],
        attn_grad,
        ffn_grad,
        vec_grad,
        bias_grad,
        attn_new,
        ffn_new,
        vec_new,
        bias_new,
        attn_copy,
        ffn_copy,
        vec_new.astype(BF16),
        bias_new.astype(BF16),
        attn_first,
        ffn_first,
        vec_first,
        bias_first,
        attn_second,
        ffn_second,
        vec_second,
        bias_second,
        norms,
        ratios,
    )


def solution(mesh):
    tokens = P(WA, CTX, None)
    mats = P(None, WA, None)
    vecs = P(None, WA)
    line = P(WA)
    state = (mats, mats, vecs, line)
    in_specs = (
        (tokens, tokens, P(WA), P(WA, None), tokens)
        + (mats,) * 6
        + (vecs,) * 3
        + (line,) * 3
    )
    out_specs = (tokens, tokens) + state * 5 + (P(), P())
    return jax.shard_map(shards, mesh=mesh, in_specs=in_specs, out_specs=out_specs, check_vma=False)
```

```python
import functools

import jax
import jax.numpy as jnp
from jax import lax
from jax.experimental import pallas as pl
from jax.experimental.pallas import tpu as pltpu
from jax.sharding import PartitionSpec as P


D = 768
HEADS = 12
HEAD = 64
FF = 3072
BLOCK = 64
RAND = 3
SLOTS = 8
PAIRS = HEADS // 2
PAIR = 2 * HEAD
QUADS = HEADS // 4
QUAD = 4 * HEAD
EACH = 6

MASKED_SCORE = -1e30
LN_EPS = 1e-06
ADAM_EPS = 1e-06
RATIO_EPS = 1e-06
BETA_ONE = 0.5
BETA_TWO = 0.5
WEIGHT_DECAY = 0.01
STEP_RATE = 0.2

CTX = "ctx"
WA = "wa"

F32 = jnp.float32
BF16 = jnp.bfloat16
NT = (((1,), (1,)), ((), ()))
NN = (((1,), (0,)), ((), ()))
TN = (((0,), (0,)), ((), ()))


def mm(a, b, dims=NN):
    return lax.dot_general(a, b, dims, preferred_element_type=F32)


def heads_apart(part):
    lane = lax.broadcasted_iota(jnp.int32, part.shape, 1) // HEAD
    zero = jnp.zeros_like(part)
    return jnp.concatenate(
        [jnp.where(lane == head, part, zero) for head in range(part.shape[1] // HEAD)], axis=0
    )


def heads_joined(parts):
    count = parts.shape[1] // HEAD
    rows = parts.shape[0] // count
    lane = lax.broadcasted_iota(jnp.int32, (rows, parts.shape[1]), 1) // HEAD
    joined = parts[:rows]
    for head in range(1, count):
        joined = jnp.where(lane == head, parts[head * rows : (head + 1) * rows], joined)
    return joined


FRINGE = 4


def window_places(i, blocks):
    before = jnp.where(i == 0, blocks, i - 1)
    after = jnp.where(i == blocks - 1, blocks + 1, i + 1)
    return before, i, after


def slot_scores(keys, queries, nvalid_ref, base):
    s = mm(keys, queries, NT)
    row = lax.broadcasted_iota(jnp.int32, (BLOCK, s.shape[1]), 0)
    parts = [
        jnp.where(row < nvalid_ref[base + at], s[at * BLOCK : (at + 1) * BLOCK], MASKED_SCORE)
        for at in range(3)
    ]
    return jnp.concatenate(parts + [s[3 * BLOCK :]], axis=0)


def slot_rows(near_ref, rand_ref, i, columns):
    blocks = near_ref.shape[0] - FRINGE
    places = window_places(i, blocks) + (blocks + 2, blocks + 3)
    rows = [near_ref[at, :, columns] for at in places]
    return jnp.concatenate(rows + [rand_ref[at, :, columns] for at in range(RAND)], axis=0)


def sparse_fwd_kernel(nvalid_ref, q_ref, near_ref, rand_ref, out_ref, lse_ref):
    i = pl.program_id(0)
    for h in range(QUADS):
        cols = slice(h * QUAD, (h + 1) * QUAD)
        vcols = slice(D + h * QUAD, D + (h + 1) * QUAD)
        queries = heads_apart(q_ref[:, cols])
        k = slot_rows(near_ref, rand_ref, i, cols)
        v = slot_rows(near_ref, rand_ref, i, vcols)
        s = slot_scores(k, queries, nvalid_ref, i * 3)
        top = jnp.max(s, axis=0, keepdims=True)
        p = jnp.exp(s - top)
        total = jnp.sum(p, axis=0, keepdims=True)
        p = (p * (1.0 / total)).astype(BF16)
        out_ref[:, cols] = heads_joined(mm(p, v, TN)).astype(BF16)
        lse_ref[0, h : h + 1, :] = top + jnp.log(total)


def attention_bwd_kernel(
    nvalid_ref, q_ref, do_ref, lse_ref, near_ref, rand_ref, gq_ref, gdo_ref, gdo_in_ref, gout_ref,
    dq_ref, grads_ref, acc_ref
):
    i = pl.program_id(0)
    blocks = near_ref.shape[0] - FRINGE
    rows = gq_ref.shape[0]
    keys = blocks * BLOCK

    @pl.when(i == 0)
    def _():
        acc_ref[...] = jnp.zeros_like(acc_ref)
        dq_ref[keys:] = jnp.zeros((FRINGE * BLOCK, D), BF16)

    @pl.when(i < blocks)
    def _():
        places = window_places(i, blocks) + (blocks + 2, blocks + 3)
        for h in range(QUADS):
            cols = slice(h * QUAD, (h + 1) * QUAD)
            vcols = slice(D + h * QUAD, D + (h + 1) * QUAD)
            queries = heads_apart(q_ref[:, cols])
            douts = heads_apart(do_ref[:, cols])
            k = slot_rows(near_ref, rand_ref, i, cols)
            v = slot_rows(near_ref, rand_ref, i, vcols)
            s = slot_scores(k, queries, nvalid_ref, i * 3)
            p = jnp.exp(s - lse_ref[0, h : h + 1, :])
            dp = mm(v, douts, NT)
            ds = (p * (dp - jnp.sum(p * dp, axis=0, keepdims=True))).astype(BF16)
            dq = heads_joined(mm(ds, k, TN)) * (HEAD**-0.5)
            dq_ref[pl.ds(pl.multiple_of(i * BLOCK, BLOCK), BLOCK), cols] = dq.astype(BF16)
            dk = mm(ds, queries).reshape(SLOTS, BLOCK, QUAD)
            dv = mm(p.astype(BF16), douts).reshape(SLOTS, BLOCK, QUAD)
            for grad, to in ((dk, cols), (dv, vcols)):
                for at, place in enumerate(places):
                    acc_ref[place, :, to] += grad[at]
                grads_ref[:, :, to] = grad[len(places) :].astype(BF16)

    @pl.when(i == blocks)
    def _():
        ok = lax.broadcasted_iota(jnp.int32, (keys, 2 * rows), 0) < nvalid_ref[blocks * 3]

        @pl.loop(0, PAIRS)
        def _(h):
            cols = pl.ds(pl.multiple_of(h * PAIR, PAIR), PAIR)
            vcols = pl.ds(pl.multiple_of(D + h * PAIR, PAIR), PAIR)
            queries = heads_apart(gq_ref[:, cols])
            douts = heads_apart(gdo_ref[:, cols] + gdo_in_ref[:, cols])
            out = gout_ref[h, :rows]
            outs = jnp.concatenate([out, out], axis=0)
            dot = jnp.sum((douts.astype(F32) * outs).T, axis=0, keepdims=True)
            lse = jnp.concatenate(
                [gout_ref[h, rows : rows + 1], gout_ref[h, rows + 1 : rows + 2]], axis=1
            )
            k = near_ref[:blocks, :, cols].reshape(keys, PAIR)
            v = near_ref[:blocks, :, vcols].reshape(keys, PAIR)
            p = jnp.where(ok, jnp.exp(mm(k, queries, NT) - lse), 0.0)
            ds = (p * (mm(v, douts, NT) - dot)).astype(BF16)
            dq = heads_joined(mm(ds, k, TN)) * (HEAD**-0.5)
            dq_ref[keys + FRINGE * BLOCK - rows :, cols] = dq.astype(BF16)
            acc_ref[:blocks, :, cols] += mm(ds, queries).reshape(blocks, BLOCK, PAIR)
            acc_ref[:blocks, :, vcols] += mm(p.astype(BF16), douts).reshape(blocks, BLOCK, PAIR)

    @pl.when(i >= blocks)
    def _():
        grads_ref[...] = acc_ref[pl.ds((i - blocks) * RAND, RAND)].astype(BF16)


def piece_copies(held, slot, buf_ref, sems, to):
    group, place = divmod(slot, GROUP)
    side, place = divmod(place, 4)
    own, first, second, up, low = held[10 * group + 5 * side : 10 * group + 5 * side + 5]
    half = buf_ref.shape[1] // 2
    if place < 3:
        return [pltpu.make_async_copy((own, first, second)[place], buf_ref.at[to], sems.at[to, 0])]
    return [
        pltpu.make_async_copy(up, buf_ref.at[to, pl.ds(0, half)], sems.at[to, 0]),
        pltpu.make_async_copy(low, buf_ref.at[to, pl.ds(half, half)], sems.at[to, 1]),
    ]


def global_fwd_kernel(pair_ref, nvalid_ref, q_ref, k_ref, v_ref, b_ref, *refs):
    held = refs[:-6]
    out_ref, top_ref, sum_ref, acc_ref, buf_ref, sems = refs[-6:]
    c = pl.program_id(0)
    rows = q_ref.shape[0]
    keys = buf_ref.shape[1]
    count = len(held) // 10 * GROUP

    @pl.when(c == 0)
    def _():
        top_ref[...] = jnp.full_like(top_ref, MASKED_SCORE)
        sum_ref[...] = jnp.zeros_like(sum_ref)
        acc_ref[...] = jnp.zeros_like(acc_ref)

    for at in range(count):

        @pl.when(c == at)
        def _():
            if at == 0:
                for copy in piece_copies(held, 0, buf_ref, sems, 0):
                    copy.start()
            if at + 1 < count:
                for copy in piece_copies(held, at + 1, buf_ref, sems, (at + 1) % 2):
                    copy.start()
            for copy in piece_copies(held, at, buf_ref, sems, at % 2):
                copy.wait()

    @pl.when(nvalid_ref[c] > 0)
    def _():
        x = buf_ref[lax.rem(c, 2)]
        k = mm(x, k_ref[...]).astype(BF16)
        v = (mm(x, v_ref[...]) + b_ref[...]).astype(BF16)
        ok = lax.broadcasted_iota(jnp.int32, (keys, 2 * rows), 0) < nvalid_ref[c]
        s = jnp.where(ok, mm(k, heads_apart(q_ref[...]), NT), MASKED_SCORE)
        before = top_ref[...]
        top = jnp.maximum(before, jnp.max(s, axis=0, keepdims=True))
        p = jnp.exp(s - top)
        shrink = jnp.exp(before - top)
        sum_ref[...] = sum_ref[...] * shrink + jnp.sum(p, axis=0, keepdims=True)
        acc_ref[...] = acc_ref[...] * shrink + mm(v, p.astype(BF16), TN)
        top_ref[...] = top

    @pl.when(c == pl.num_programs(0) - 1)
    def _():
        total = sum_ref[...]
        lse = top_ref[...] + jnp.log(total)
        out_ref[:rows] = heads_joined((acc_ref[...] / total).T)
        out_ref[rows : rows + 1] = lse[:, :rows]
        out_ref[rows + 1 : rows + 2] = lse[:, rows:]
        out_ref[rows + 2 :] = jnp.zeros((6, PAIR), F32)


def kv_used_kernel(start_ref, order_ref, index_ref, w_ref, b_ref, *refs):
    held = refs[:-4]
    kv_ref, x_ref, buf_ref, sems = refs[-4:]
    step = pl.program_id(0)
    each = x_ref.shape[0] // BLOCK

    def copy(ref, start, at):
        start = pl.multiple_of(start * BLOCK, BLOCK)
        return pltpu.make_async_copy(ref.at[pl.ds(start, BLOCK)], buf_ref.at[at], sems.at[at])

    @pl.when(step == 0)
    def _():
        for which, ref in enumerate(held):

            @pl.loop(start_ref[which], start_ref[which + 1])
            def _(n):
                copy(ref, index_ref[n], order_ref[n]).start()

    for at in range(each):
        copy(held[0], 0, step * each + at).wait()
    x_ref[...] = buf_ref[pl.ds(step * each, each)].reshape(each * BLOCK, D)

    kv_ref[...] = (mm(x_ref[...], w_ref[...]) + b_ref[...]).astype(BF16)


def place_blocks_kernel(table_ref, x_ref, q_ref, low_ref, high_ref):
    low_ref[...] = jnp.zeros_like(low_ref)
    high_ref[...] = jnp.zeros_like(high_ref)
    limit = low_ref.shape[0]

    def step(s, part):
        to = table_ref[s]

        @pl.when(to < limit)
        def _():
            low_ref[to] += part

        @pl.when(to >= limit)
        def _():
            high_ref[to - limit] += part

    @pl.loop(0, q_ref.shape[0])
    def _(s):
        step(s, x_ref[s] + q_ref[s])

    @pl.loop(q_ref.shape[0], x_ref.shape[0])
    def _(s):
        step(s, x_ref[s])


def whole(shape):
    return pl.BlockSpec(shape, lambda *a: (0,) * len(shape))


VMEM_SPEC = pl.BlockSpec(memory_space=pltpu.VMEM)
SMEM_SPEC = pl.BlockSpec(memory_space=pltpu.SMEM)


def cost(flops, moved, exps=0):
    return pl.CostEstimate(flops=int(flops), bytes_accessed=int(moved), transcendentals=int(exps))


def near_spec(near):
    return pl.BlockSpec((near, BLOCK, 2 * D), lambda i, n: (0, 0, 0))


def rand_spec(near):
    return pl.BlockSpec((RAND, BLOCK, 2 * D), lambda i, n: (near // RAND + i, 0, 0))


def sparse_fwd(nvalid, q, kv_used):
    rows = q.shape[0]
    blocks = rows // BLOCK
    near = blocks + FRINGE
    work = 2 * rows * SLOTS * BLOCK * D
    return pl.pallas_call(
        sparse_fwd_kernel,
        grid_spec=pltpu.PrefetchScalarGridSpec(
            num_scalar_prefetch=1,
            grid=(blocks,),
            in_specs=[
                pl.BlockSpec((BLOCK, D), lambda i, n: (i, 0)),
                near_spec(near),
                rand_spec(near),
            ],
            out_specs=[
                pl.BlockSpec((BLOCK, D), lambda i, n: (i, 0)),
                pl.BlockSpec((1, 8, QUAD), lambda i, n: (i, 0, 0)),
            ],
        ),
        out_shape=[
            jax.ShapeDtypeStruct((rows, D), BF16),
            jax.ShapeDtypeStruct((blocks, 8, QUAD), F32),
        ],
        cost_estimate=cost(2 * work, rows * SLOTS * D * 4, rows * SLOTS * BLOCK * HEADS),
        name="sf",
    )(nvalid, q, kv_used, kv_used)


def attention_bwd(nvalid, q, dout, lse, kv_used, glob_q, glob_do, glob_do_in, glob_out):
    rows = q.shape[0]
    blocks = rows // BLOCK
    near = blocks + FRINGE
    last = blocks - 1
    glob = glob_q.shape[0]
    work = 2 * (rows + glob) * SLOTS * BLOCK * D
    each = pl.BlockSpec((BLOCK, D), lambda i, n: (jnp.minimum(i, last), 0))
    rand = (RAND, BLOCK, 2 * D)
    return pl.pallas_call(
        attention_bwd_kernel,
        grid_spec=pltpu.PrefetchScalarGridSpec(
            num_scalar_prefetch=1,
            grid=(blocks + near // RAND,),
            in_specs=[
                each,
                each,
                pl.BlockSpec((1, 8, QUAD), lambda i, n: (jnp.minimum(i, last), 0, 0)),
                near_spec(near),
                pl.BlockSpec(rand, lambda i, n: (near // RAND + jnp.minimum(i, last), 0, 0)),
                whole((glob, D)),
                whole((glob, D)),
                whole((glob, D)),
                whole(glob_out.shape),
            ],
            out_specs=[
                whole((near * BLOCK, D)),
                pl.BlockSpec(
                    rand,
                    lambda i, n: (jnp.where(i < blocks, near // RAND + i, i - blocks), 0, 0),
                ),
            ],
            scratch_shapes=[pltpu.VMEM((near, BLOCK, 2 * D), F32)],
        ),
        out_shape=[
            jax.ShapeDtypeStruct((near * BLOCK, D), BF16),
            jax.ShapeDtypeStruct(kv_used.shape, BF16),
        ],
        cost_estimate=cost(5 * work, rows * SLOTS * D * 8, rows * SLOTS * BLOCK * HEADS),
        name="sb",
    )(nvalid, q, dout, lse, kv_used, kv_used, glob_q, glob_do, glob_do_in, glob_out)


def global_fwd(pair, nvalid, q, w_kv, kv_bias, held):
    rows = q.shape[0]
    chunks = nvalid.shape[0]
    keys = held[0].shape[0]
    return pl.pallas_call(
        global_fwd_kernel,
        grid_spec=pltpu.PrefetchScalarGridSpec(
            num_scalar_prefetch=2,
            grid=(chunks,),
            in_specs=[
                pl.BlockSpec((rows, PAIR), lambda c, p, n: (0, p[0])),
                pl.BlockSpec((D, PAIR), lambda c, p, n: (0, p[0])),
                pl.BlockSpec((D, PAIR), lambda c, p, n: (0, PAIRS + p[0])),
                pl.BlockSpec((1, PAIR), lambda c, p, n: (0, PAIRS + p[0])),
            ]
            + [pl.BlockSpec(memory_space=pl.ANY)] * len(held),
            out_specs=pl.BlockSpec((rows + 8, PAIR), lambda c, p, n: (0, 0)),
            scratch_shapes=[pltpu.VMEM((1, 2 * rows), F32)] * 2
            + [
                pltpu.VMEM((PAIR, 2 * rows), F32),
                pltpu.VMEM((2, keys, D), BF16),
                pltpu.SemaphoreType.DMA((2, 2)),
            ],
        ),
        out_shape=jax.ShapeDtypeStruct((rows + 8, PAIR), F32),
        cost_estimate=cost(
            4 * (rows + D) * chunks * keys * PAIR,
            2 * chunks * keys * D,
            2 * rows * chunks * keys,
        ),
        name="gf",
    )(pair[None], nvalid, q, w_kv, w_kv, kv_bias, *held)


def kv_used_rows(source, index, w_kv, kv_bias, held):
    count = source.shape[0]
    each = EACH
    rows = each * BLOCK
    number = jnp.arange(count, dtype=jnp.int32)
    earlier = (source[None] < source[:, None]) | (
        (source[None] == source[:, None]) & (number[None] < number[:, None])
    )
    rank = jnp.sum(earlier, axis=1, dtype=jnp.int32)
    chosen = (rank[None] == number[:, None]).astype(jnp.int32)
    order = jnp.sum(chosen * number[None], axis=1, dtype=jnp.int32)
    places = jnp.sum(chosen * index[None], axis=1, dtype=jnp.int32)
    sources = jnp.arange(len(held) + 1, dtype=jnp.int32)
    starts = jnp.sum(source[None] < sources[:, None], axis=1, dtype=jnp.int32)
    return pl.pallas_call(
        kv_used_kernel,
        grid_spec=pltpu.PrefetchScalarGridSpec(
            num_scalar_prefetch=3,
            grid=(count // each,),
            in_specs=[whole((D, 2 * D)), whole((1, 2 * D))]
            + [pl.BlockSpec(memory_space=pl.ANY)] * len(held),
            out_specs=[
                pl.BlockSpec((rows, 2 * D), lambda t, *a: (t, 0)),
                pl.BlockSpec((rows, D), lambda t, *a: (t, 0)),
            ],
            scratch_shapes=[
                pltpu.VMEM((count, BLOCK, D), BF16),
                pltpu.SemaphoreType.DMA((count,)),
            ],
        ),
        out_shape=[
            jax.ShapeDtypeStruct((count * BLOCK, 2 * D), BF16),
            jax.ShapeDtypeStruct((count * BLOCK, D), BF16),
        ],
        cost_estimate=cost(4 * count * BLOCK * D * D, 8 * count * BLOCK * D),
        name="kv",
    )(starts, order, places, w_kv, kv_bias, *held)


def place_blocks(table, x_blocks, q_blocks, total):
    half = jax.ShapeDtypeStruct((total // 2,) + x_blocks.shape[1:], BF16)
    return pl.pallas_call(
        place_blocks_kernel,
        in_specs=[SMEM_SPEC, VMEM_SPEC, VMEM_SPEC],
        out_specs=[VMEM_SPEC, VMEM_SPEC],
        out_shape=[half, half],
        cost_estimate=cost(0, 2 * (total + 2 * x_blocks.shape[0]) * BLOCK * D),
        name="pb",
    )(table, x_blocks, q_blocks)


CORE, FIRST, SECOND = 1, 2, 4
GROUP = 8
CUT = 3 * D // GROUP + D // GROUP


def exchange(value, mask):
    count = lax.axis_size(CTX)
    return lax.ppermute(value, CTX, [(i, i ^ mask) for i in range(count)])


def slot_of(index):
    return index // GROUP * GROUP + index // 2 % 4 + index % 2 * 4


def index_of(slot):
    return slot // GROUP * GROUP + slot % 4 * 2 + slot // 4 % 2


def spare_masks():
    return [1 << i for i in range(3, lax.axis_size(CTX).bit_length() - 1)]


def all_masks():
    return [CORE, FIRST, SECOND] + spare_masks()


def wa_shift(value, step):
    count = lax.axis_size(WA)
    return lax.ppermute(value, WA, [(i, (i + step) % count) for i in range(count)])


def wa_parts(piece):
    return [piece] + [wa_shift(piece, step) for step in range(1, lax.axis_size(WA))]


def wa_reduce(chunks):
    count = lax.axis_size(WA)
    rank = lax.axis_index(WA)

    def chunk(step):
        return lax.dynamic_index_in_dim(chunks, (rank + step) % count, 0, keepdims=False)

    arrived = [wa_shift(chunk(step), step) for step in range(1, count)]
    total = chunk(0).astype(F32)
    for part in arrived:
        total = total + part.astype(F32)
    return total


def wa_total(value):
    count = lax.axis_size(WA)
    mask = 1
    while mask < count:
        pairs = [(i, i ^ mask) for i in range(count)]
        value = value + lax.ppermute(value, WA, pairs)
        mask *= 2
    return value


def bit_of(mask):
    return (lax.axis_index(CTX) // mask) % 2 == 1


def gather_group(own, then=None):
    cut = own.shape[0] // 2
    first = exchange(own, FIRST)
    second = exchange(own, SECOND)
    upper, lower = first[:cut], second[cut:]
    if then is not None:
        upper, lower, then = lax.optimization_barrier((upper, lower, then))
    upper = exchange(upper, SECOND)
    lower = exchange(lower, FIRST)
    near = [own, first, second, upper, lower]
    held = near + [exchange(part, CORE) for part in near]
    return held if then is None else (held, then)


def gather_direct(own):
    near = [own] + [exchange(own, mask) for mask in (FIRST, SECOND, FIRST | SECOND)]
    return near + [exchange(part, CORE) for part in near]


def group_in_order(own):
    value = own[None]
    for mask in (FIRST, SECOND, CORE):
        other = exchange(value, mask)
        high = bit_of(mask)
        value = jnp.concatenate(
            [jnp.where(high, other, value), jnp.where(high, value, other)], axis=0
        )
    return value


def add_low(first, second):
    return (first.astype(F32) + second.astype(F32)).astype(BF16)


def cut_kernel(where_ref, attn_ref, ffn_ref, vec_ref, bias_ref, attn_out, ffn_out):
    wide = attn_ref.shape[1]
    attn_out[:wide, :] = attn_ref[0].astype(BF16)
    small = jnp.concatenate([vec_ref[...], bias_ref[...], jnp.zeros((4, wide), F32)], axis=0)
    attn_out[wide:, :wide] = small.astype(BF16)
    attn_out[wide:, wide:] = jnp.zeros((16, CUT - wide), BF16)
    ffn_out[:, :CUT] = ffn_ref[0].astype(BF16)
    ffn_out[:, CUT:] = ffn_ref[1].astype(BF16)


def cut_pieces(slot, attn_master, ffn_master, vec_master, bias_rows):
    wide = attn_master.shape[1]
    return pl.pallas_call(
        cut_kernel,
        grid_spec=pltpu.PrefetchScalarGridSpec(
            num_scalar_prefetch=1,
            grid=(1,),
            in_specs=[
                pl.BlockSpec((1, wide, CUT), lambda i, w: (w[0] // 2, 0, w[0] % 2)),
                pl.BlockSpec((2, wide, CUT), lambda i, w: (0, 0, w[0])),
                whole((8, wide)),
                whole((4, wide)),
            ],
            out_specs=[whole((wide + 16, CUT)), whole((wide, 2 * CUT))],
        ),
        out_shape=[
            jax.ShapeDtypeStruct((wide + 16, CUT), BF16),
            jax.ShapeDtypeStruct((wide, 2 * CUT), BF16),
        ],
        cost_estimate=cost(0, wide * CUT * 18),
        name="cut",
    )(slot[None], attn_master, ffn_master, vec_master, bias_rows)


def join_kernel(rank_ref, *refs):
    parts, outs = refs[: len(refs) - 2], refs[len(refs) - 2 :]
    count = len(parts)
    wide = outs[0].shape[0] // count
    for step, part in enumerate(parts):
        at = lax.rem(rank_ref[0] - step + count, count)
        outs[0][pl.ds(pl.multiple_of(at * wide, 16), wide), :] = part[:wide]
        outs[1][at] = part[part.shape[0] - 16 :]


def join_rows(rank, parts):
    count = len(parts)
    extra = parts[0].shape[0] % 32
    wide = parts[0].shape[0] - extra
    columns = parts[0].shape[1]
    return pl.pallas_call(
        join_kernel,
        in_specs=[SMEM_SPEC] + [VMEM_SPEC] * count,
        out_specs=[VMEM_SPEC, VMEM_SPEC],
        out_shape=[
            jax.ShapeDtypeStruct((count * wide, columns), BF16),
            jax.ShapeDtypeStruct((count, 16, columns), BF16),
        ],
        cost_estimate=cost(0, 4 * count * wide * columns),
        name="join",
    )(rank[None], *parts)


def held_specs(rows, columns, tiles):
    shape = (rows // tiles, columns)
    middle = tiles // 2
    each = [
        pl.BlockSpec(shape, lambda t, *a: (t, 0)),
        pl.BlockSpec(shape, lambda t, *a: (t, 0)),
        pl.BlockSpec(shape, lambda t, *a: (t, 0)),
        pl.BlockSpec(shape, lambda t, *a: (jnp.minimum(t, middle - 1), 0)),
        pl.BlockSpec(shape, lambda t, *a: (jnp.maximum(t - middle, 0), 0)),
    ]
    return each + each


def for_each_slot(held, body):
    upper = pl.program_id(0) < pl.num_programs(0) // 2
    for side in range(2):
        own, first, second, up, low = held[5 * side : 5 * side + 5]
        for at, ref in enumerate((own, first, second)):
            body(4 * side + at, ref)
        pl.when(upper)(functools.partial(body, 4 * side + 3, up))
        pl.when(jnp.logical_not(upper))(functools.partial(body, 4 * side + 3, low))


def attn_weights_kernel(slot_ref, *refs):
    held, (q_ref, kv_ref, o_ref) = refs[:10], refs[10:]

    def body(slot, ref):
        at = slot_ref[0] ^ slot
        for out, start, stop in ((q_ref, 0, 2), (kv_ref, 2, 6), (o_ref, 6, 8)):

            @pl.when((at >= start) & (at < stop))
            def _():
                out[:, pl.ds(pl.multiple_of((at - start) * CUT, 128), CUT)] = ref[...]

    for_each_slot(held, body)


def attn_weights(slot, held):
    rows = held[0].shape[0]
    tiles = 4
    size = rows // tiles
    widths = (D, 2 * D, D)
    return pl.pallas_call(
        attn_weights_kernel,
        grid_spec=pltpu.PrefetchScalarGridSpec(
            num_scalar_prefetch=1,
            grid=(tiles,),
            in_specs=held_specs(rows, CUT, tiles),
            out_specs=[pl.BlockSpec((size, w), lambda t, *a: (t, 0)) for w in widths],
        ),
        out_shape=[jax.ShapeDtypeStruct((rows, w), BF16) for w in widths],
        cost_estimate=cost(0, 4 * rows * GROUP * CUT),
        name="aw",
    )(slot[None], *held)


STRIDE = 2


def matrix_copies(held, step, up_ref, down_ref, sems, to):
    jobs = []
    half = D // 2
    for at in range(STRIDE):
        side, place = divmod(step * STRIDE + at, 4)
        own, first, second, upper, lower = held[5 * side : 5 * side + 5]
        parts = [(upper, 0, half), (lower, half, half)]
        if place < 3:
            parts = [((own, first, second)[place], 0, D)]
        for ref, start, size in parts:
            for which, buf in enumerate((up_ref, down_ref)):
                source = ref.at[:, pl.ds(which * CUT, CUT)]
                target = buf.at[to, pl.ds(start, size), pl.ds(at * CUT, CUT)]
                jobs.append(pltpu.make_async_copy(source, target, sems.at[to, len(jobs)]))
    return jobs


def fetch_matrices(held, up_ref, down_ref, sems):
    step = pl.program_id(0)
    for at in range(GROUP // STRIDE):

        @pl.when(step == at)
        def _():
            if at == 0:
                for copy in matrix_copies(held, 0, up_ref, down_ref, sems, 0):
                    copy.start()
            if at + 1 < GROUP // STRIDE:
                for copy in matrix_copies(held, at + 1, up_ref, down_ref, sems, (at + 1) % 2):
                    copy.start()
            for copy in matrix_copies(held, at, up_ref, down_ref, sems, at % 2):
                copy.wait()

    return lax.rem(step, 2)


def add_up(total_ref, part):
    @pl.when(pl.program_id(0) == 0)
    def _():
        total_ref[...] = part

    @pl.when(pl.program_id(0) > 0)
    def _():
        total_ref[...] += part


def ffn_fwd_kernel(n_ref, b_ref, *refs):
    held = refs[:10]
    hidden_ref, slope_ref, total_ref, w_up_ref, w_down_ref, up_ref, down_ref, sems = refs[10:]
    now = fetch_matrices(held, up_ref, down_ref, sems)
    up = mm(n_ref[...], up_ref[now]) + b_ref[0]
    cdf = 0.5 * (1.0 + lax.erf(up * (0.5**0.5)))
    hidden = (up * cdf).astype(BF16)
    hidden_ref[...] = hidden
    slope_ref[...] = (cdf + up * (jnp.exp(-0.5 * up * up) * 0.3989422804014327)).astype(BF16)
    add_up(total_ref, mm(hidden, down_ref[now], NT))
    w_up_ref[...] = up_ref[now]
    w_down_ref[...] = down_ref[now]


def ffn_scratch():
    buf = pltpu.VMEM((2, D, STRIDE * CUT), BF16)
    return [buf, buf, pltpu.SemaphoreType.DMA((2, 4 * STRIDE))]


def ffn_fwd(norm_low, bias, held):
    rows = norm_low.shape[0]
    wide = pl.BlockSpec((rows, STRIDE * CUT), lambda t: (0, t))
    full = pl.BlockSpec((D, STRIDE * CUT), lambda t: (0, t))
    return pl.pallas_call(
        ffn_fwd_kernel,
        grid=(GROUP // STRIDE,),
        in_specs=[whole((rows, D)), pl.BlockSpec((1, 1, STRIDE * CUT), lambda t: (t, 0, 0))]
        + [pl.BlockSpec(memory_space=pl.ANY)] * 10,
        out_specs=[wide, wide, whole((rows, D)), full, full],
        out_shape=[
            jax.ShapeDtypeStruct((rows, FF), BF16),
            jax.ShapeDtypeStruct((rows, FF), BF16),
            jax.ShapeDtypeStruct((rows, D), F32),
            jax.ShapeDtypeStruct((D, FF), BF16),
            jax.ShapeDtypeStruct((D, FF), BF16),
        ],
        scratch_shapes=ffn_scratch(),
        cost_estimate=cost(4 * rows * D * FF, 4 * rows * FF + 4 * D * FF, 2 * rows * FF),
        name="ff",
    )(norm_low, bias.reshape(-1, 1, STRIDE * CUT), *held)


def spread_kernel(slot_ref, *refs, read):
    keep, outs = refs[:-4], refs[-4:]
    for slot, out in enumerate(outs):
        out[...] = read(slot_ref, keep, slot).astype(BF16)


def read_ffn(slot_ref, refs, slot):
    at = slice(slot * CUT, (slot + 1) * CUT)
    up, down, up_in, down_in = (r[:, at].astype(F32) for r in refs)
    return jnp.concatenate([up + up_in, down + down_in], axis=1)


def read_attn(slot_ref, refs, slot):
    at = (slot_ref[0] ^ slot) % 4
    columns = pl.ds(pl.multiple_of(at % 2 * CUT, 128), CUT)
    return refs[0][at // 2, :, columns].astype(F32) + refs[1][at // 2, :, columns].astype(F32)


def read_rows(slot_ref, refs, slot):
    return refs[0][slot].astype(F32) + refs[1][slot].astype(F32)


def spread(slot, arrays, in_specs, rows, columns, read, tiles):
    block = pl.BlockSpec((rows // tiles, columns), lambda t, *a: (t, 0))
    return pl.pallas_call(
        functools.partial(spread_kernel, read=read),
        grid_spec=pltpu.PrefetchScalarGridSpec(
            num_scalar_prefetch=1, grid=(tiles,), in_specs=in_specs, out_specs=[block] * 4
        ),
        out_shape=[jax.ShapeDtypeStruct((rows, columns), BF16)] * 4,
        cost_estimate=cost(0, rows * columns * 24),
    )(slot[None], *arrays)


def reduce_group(slot, arrays, in_specs, rows, columns, read, tiles=4):
    own, *others = spread(slot, arrays, in_specs, rows, columns, read, tiles)
    total = own.astype(F32)
    for part, mask in zip(others, (FIRST, SECOND, FIRST | SECOND)):
        total = total + exchange(part, mask).astype(F32)
    return total


def adam_kernel(slot_ref, *refs, pieces):
    held = refs[:GROUP]
    w_ref, m_ref, v_ref, grad_ref, first_ref, second_ref, step_ref, sums_ref = refs[GROUP:]
    for slot, ref in enumerate(held):
        at = slot_ref[0] ^ slot
        if pieces == 1:
            columns = pl.ds(pl.multiple_of(at % 2 * CUT, 128), CUT)
            grad_ref[at // 2, :, columns] = ref[...].astype(F32)
        else:
            columns = pl.ds(pl.multiple_of(at * CUT, 128), CUT)
            grad_ref[0, :, columns] = ref[:, :CUT].astype(F32)
            grad_ref[1, :, columns] = ref[:, CUT:].astype(F32)

    @pl.when(pl.program_id(0) == 0)
    def _():
        sums_ref[...] = jnp.zeros_like(sums_ref)

    mats, rows, columns = grad_ref.shape
    each = 8 if columns > D else 24

    @pl.loop(0, mats * (rows // each))
    def _(step):
        mat = step // (rows // each)
        here = pl.ds(pl.multiple_of(step % (rows // each) * each, each), each)
        grad = grad_ref[mat, here]
        first = BETA_ONE * m_ref[mat, here] + (1.0 - BETA_ONE) * grad
        second = BETA_TWO * v_ref[mat, here] + (1.0 - BETA_TWO) * grad * grad
        weight = w_ref[mat, here]
        move = first / (jnp.sqrt(second) + ADAM_EPS) + WEIGHT_DECAY * weight
        first_ref[mat, here] = first
        second_ref[mat, here] = second
        step_ref[mat, here] = move.astype(BF16)
        for row, part in ((mat, weight), (mats + mat, move)):
            sums_ref[row] += jnp.sum((part * part).reshape(each // 8, 8, columns), axis=0)


def final(ratios, master, step):
    new = master - (STEP_RATE * ratios)[:, None, None] * step.astype(F32)
    return new, new.astype(BF16)


def adam(slot, held, master, first, second):
    mats, wide, columns = master.shape
    tiles = 2
    size = wide // tiles
    piece_columns = held[0].shape[1]
    block = pl.BlockSpec((mats, size, columns), lambda t, *a: (0, t, 0))
    full = jax.ShapeDtypeStruct(master.shape, F32)
    return pl.pallas_call(
        functools.partial(adam_kernel, pieces=piece_columns // CUT),
        grid_spec=pltpu.PrefetchScalarGridSpec(
            num_scalar_prefetch=1,
            grid=(tiles,),
            in_specs=[pl.BlockSpec((size, piece_columns), lambda t, *a: (t, 0))] * GROUP
            + [block] * 3,
            out_specs=[block] * 4 + [whole((2 * mats, 8, columns))],
        ),
        out_shape=[full] * 3
        + [
            jax.ShapeDtypeStruct(master.shape, BF16),
            jax.ShapeDtypeStruct((2 * mats, 8, columns), F32),
        ],
        cost_estimate=cost(20 * master.size, 30 * master.size, master.size),
    )(slot[None], *held, master, first, second)


def norm_parts(hidden):
    centre = hidden - jnp.mean(hidden, axis=-1, keepdims=True)
    spread = jnp.mean(centre * centre, axis=-1, keepdims=True)
    inverse = lax.rsqrt(spread + LN_EPS)
    return centre * inverse, inverse


def norm_back(grad, normal, inverse, gain):
    scaled = grad * gain
    return inverse * (
        scaled
        - jnp.mean(scaled, axis=-1, keepdims=True)
        - normal * jnp.mean(scaled * normal, axis=-1, keepdims=True)
    )


def adam_moments(first, second, grads):
    first_new = BETA_ONE * first + (1.0 - BETA_ONE) * grads
    second_new = BETA_TWO * second + (1.0 - BETA_TWO) * grads * grads
    return (first_new, second_new, first_new / (jnp.sqrt(second_new) + ADAM_EPS))


def shards(
    inputs,
    cotangent,
    lengths,
    global_ids,
    random_ids,
    attn_master,
    attn_m,
    attn_v,
    ffn_master,
    ffn_m,
    ffn_v,
    vec_master,
    vec_m,
    vec_v,
    bias_master,
    bias_m,
    bias_v,
):
    x = inputs[0]
    rows = x.shape[0]
    ctx_count = lax.axis_size(CTX)
    rank = lax.axis_index(CTX)
    wa_count = lax.axis_size(WA)
    wa_rank = lax.axis_index(WA)
    blocks = rows // BLOCK
    total_blocks = blocks * ctx_count
    wide = D // wa_count
    seq_len = lengths[0]
    glob_ids = global_ids[0]
    my_slot = slot_of(rank) % GROUP
    relative = jnp.arange(ctx_count, dtype=jnp.int32)
    owner_at = rank ^ index_of(relative)

    attn_piece, ffn_piece = cut_pieces(
        my_slot, attn_master, ffn_master, vec_master, bias_master.reshape(4, wide)
    )
    attn_parts = wa_parts(attn_piece)
    x_held, attn_parts = gather_group(x, attn_parts)
    attn_rows, small = join_rows(wa_rank, attn_parts)
    attn_held = gather_group(attn_rows)
    w_query, w_kv, w_out = attn_weights(my_slot, attn_held)
    ffn_parts = wa_parts(ffn_piece)
    ffn_parts, w_kv = lax.optimization_barrier((ffn_parts, w_kv))
    ffn_rows, _ = join_rows(wa_rank, ffn_parts)
    ffn_held = gather_group(ffn_rows)

    small = small[:, :, :wide]
    vectors = small[:, :8].transpose(1, 0, 2).reshape(8, D).astype(F32)
    bias_blocks = small[:, 8:12].reshape(GROUP, CUT).astype(F32)
    bias_up = bias_blocks[my_slot ^ relative[:GROUP]]

    def place_of(block):
        block = jnp.clip(block, 0, total_blocks - 1)
        return slot_of((block // blocks) ^ rank) * blocks + block % blocks

    rand_ids = random_ids[0]
    own_blocks = rank * blocks + jnp.arange(blocks, dtype=jnp.int32)
    window = jnp.stack([own_blocks - 1, own_blocks, own_blocks + 1], axis=1)
    window_nvalid = jnp.where(
        (window >= 0) & (window < total_blocks), jnp.clip(seq_len - window * BLOCK, 0, BLOCK), 0
    ).reshape(-1)
    used_table = place_of(
        jnp.concatenate(
            [own_blocks, own_blocks[:1] - 1, own_blocks[-1:] + 1, glob_ids, rand_ids.reshape(-1)]
        )
    )
    used_slot, used_at = used_table // blocks, used_table % blocks
    split = (used_slot % 4 == 3) & (used_at >= blocks // 2)
    used_source = used_slot // 4 * 5 + used_slot % 4 + split
    used_index = used_at - jnp.where(split, blocks // 2, 0)
    chunk_nvalid = jnp.clip(seq_len - owner_at * rows, 0, rows)
    positions = rank * rows + jnp.arange(rows, dtype=jnp.int32)
    row_weight = (positions < seq_len).astype(F32)[:, None]
    hits = own_blocks[None, :] == glob_ids[:, None]

    scale = HEAD**-0.5
    kv_bias = jnp.concatenate([jnp.zeros((D,), F32), vectors[1]])[None]
    groups = [x_held]
    for mask in spare_masks():
        groups += [[exchange(part, mask) for part in held] for held in groups]
    x_held = [part for held in groups for part in held]
    kv_used, x_used = kv_used_rows(used_source, used_index, w_kv, kv_bias, x_held)
    near_rows = (blocks + FRINGE) * BLOCK
    x_near = x_used[:near_rows]
    x_glob = x_near[near_rows - 2 * BLOCK :]
    kv_used = kv_used.reshape(-1, BLOCK, 2 * D)
    glob_query = ((mm(x_glob, w_query) + vectors[0]).astype(BF16) * BF16(scale)).astype(BF16)
    glob_part = global_fwd(
        jnp.minimum(my_slot, PAIRS - 1), chunk_nvalid, glob_query, w_kv, kv_bias, x_held
    )
    glob_pairs = group_in_order(glob_part)
    query = ((mm(x, w_query, NN) + vectors[0]).astype(BF16) * BF16(scale)).astype(BF16)
    sparse_out, lse = sparse_fwd(window_nvalid, query, kv_used)
    glob_out = (
        glob_pairs[:PAIRS, : 2 * BLOCK].transpose(1, 0, 2).reshape(2, BLOCK, D).astype(BF16)
    )
    attended = sparse_out.reshape(blocks, BLOCK, D)
    for g in range(2):
        attended = jnp.where(hits[g][:, None, None], glob_out[g][None], attended)
    attended = attended.reshape(rows, D)

    first_sum = x.astype(F32) + mm(attended, w_out) + vectors[2]
    normal_one, inverse_one = norm_parts(first_sum)
    norm_one = normal_one * vectors[4] + vectors[5]
    norm_low = norm_one.astype(BF16)
    hidden_low, slope, down, w_up, w_down = ffn_fwd(norm_low, bias_up, ffn_held)
    second_sum = norm_one + down + vectors[3]
    normal_two, inverse_two = norm_parts(second_sum)
    output = ((normal_two * vectors[6] + vectors[7]) * row_weight).astype(BF16)
    grad_out = cotangent[0].astype(F32) * row_weight
    grad_second = norm_back(grad_out, normal_two, inverse_two, vectors[6])
    grad_down = grad_second.astype(BF16)
    grad_upper = (mm(grad_down, w_down) * slope.astype(F32)).astype(BF16)
    grad_norm = grad_second + mm(grad_upper, w_up, NT)
    grad_first = norm_back(grad_norm, normal_one, inverse_one, vectors[4])
    grad_branch = grad_first.astype(BF16)
    grad_attended = mm(grad_branch, w_out, NT).astype(BF16)

    cut = FF // 2
    up_sent = mm(norm_low, grad_upper[:, cut:], TN).astype(BF16)
    down_sent = mm(grad_down, hidden_low[:, cut:], TN).astype(BF16)
    up_keep = mm(norm_low, grad_upper[:, :cut], TN).astype(BF16)
    down_keep = mm(grad_down, hidden_low[:, :cut], TN).astype(BF16)
    tiles = 4
    ffn_spec = pl.BlockSpec((D // tiles, cut), lambda t, *a: (t, 0))

    def finish(total, extra=None):
        total = total.astype(BF16)
        for mask in spare_masks():
            total = add_low(total, exchange(total, mask))
        total = total.reshape(wa_count, wide, total.shape[1])
        if extra is not None:
            total = jnp.concatenate([total, extra], axis=1)
        return wa_reduce(total)

    ffn_mine = finish(
        reduce_group(
            my_slot,
            [up_keep, down_keep, exchange(up_sent, CORE), exchange(down_sent, CORE)],
            [ffn_spec] * 4,
            D,
            2 * CUT,
            read_ffn,
            tiles,
        ),
    ).astype(BF16)
    ffn_grad, ffn_first, ffn_second, ffn_step, ffn_sums = adam(
        my_slot, gather_direct(ffn_mine), ffn_master, ffn_m, ffn_v
    )

    grad_blocks = grad_attended.reshape(blocks, BLOCK, D)
    glob_part = jnp.sum(
        jnp.where(hits[:, :, None, None], grad_blocks[None], 0), axis=1, dtype=F32
    ).astype(BF16)
    for mask in all_masks()[:-1]:
        glob_part = glob_part + exchange(glob_part, mask)
    glob_in = exchange(glob_part, all_masks()[-1])
    grad_sparse = jnp.where((hits[0] | hits[1])[:, None, None], 0, grad_blocks).reshape(rows, D)
    near_dquery, used_grads = attention_bwd(
        jnp.concatenate([window_nvalid, chunk_nvalid[:1]]),
        query,
        grad_sparse,
        lse,
        kv_used,
        glob_query,
        glob_part.reshape(2 * BLOCK, D),
        glob_in.reshape(2 * BLOCK, D),
        glob_pairs,
    )
    used_grads = used_grads.reshape(-1, 2 * D)

    g_query = mm(x_near, near_dquery, TN).astype(BF16)
    g_kv = mm(x_used, used_grads, TN).astype(BF16)
    g_key, g_value = g_kv[:, :D], g_kv[:, D:]
    g_out = mm(attended, grad_branch, TN).astype(BF16)
    on_core = bit_of(CORE)
    early, late = jnp.stack([g_query, g_key]), jnp.stack([g_value, g_out])
    attn_sent = jnp.where(on_core, early, late)
    attn_keep = jnp.where(on_core, late, early)
    attn_spec = pl.BlockSpec((2, D // tiles, D), lambda t, *a: (0, t, 0))
    vec_local = jnp.stack(
        [
            jnp.sum(near_dquery, axis=0, dtype=F32),
            jnp.sum(used_grads[:, D:], axis=0, dtype=F32),
            jnp.sum(grad_branch, axis=0, dtype=F32),
            jnp.sum(grad_down, axis=0, dtype=F32),
            jnp.sum(grad_norm * normal_one, axis=0),
            jnp.sum(grad_norm, axis=0),
            jnp.sum(grad_out * normal_two, axis=0),
            jnp.sum(grad_out, axis=0),
        ]
    )
    bias_local = jnp.sum(grad_upper, axis=0, dtype=F32).reshape(GROUP, CUT)[
        my_slot ^ relative[:GROUP]
    ]
    small_local = jnp.concatenate(
        [
            vec_local.reshape(8, wa_count, wide).transpose(1, 0, 2).reshape(wa_count, 8 * wide),
            bias_local.reshape(wa_count, FF // wa_count),
        ],
        axis=1,
    )
    small_sum = small_local
    for mask in all_masks():
        small_sum = small_sum + exchange(small_sum, mask)
    small_rows = jnp.pad(small_sum, ((0, 0), (0, 8 * CUT - small_sum.shape[1])))
    small_rows = small_rows.reshape(wa_count, 8, CUT).astype(BF16)

    attn_total = finish(
        reduce_group(
            my_slot,
            [attn_keep, exchange(attn_sent, CORE)],
            [attn_spec] * 2,
            D,
            CUT,
            read_attn,
            tiles,
        ),
        small_rows,
    )
    attn_mine = attn_total[:wide].astype(BF16)
    small_mine = attn_total[wide:].reshape(-1)
    vec_grad = small_mine[: 8 * wide].reshape(8, wide)
    bias_grad = small_mine[8 * wide : 8 * wide + FF // wa_count]
    attn_grad, attn_first, attn_second, attn_step, attn_sums = adam(
        my_slot, gather_direct(attn_mine), attn_master, attn_m, attn_v
    )

    dx_used = mm(used_grads, w_kv, NT).astype(BF16)
    dx_query = mm(near_dquery, w_query, NT).astype(BF16)
    dx_keep, dx_sent = place_blocks(
        used_table,
        dx_used.reshape(-1, BLOCK, D),
        dx_query.reshape(-1, BLOCK, D),
        total_blocks,
    )
    for mask in spare_masks()[::-1]:
        dx_keep = add_low(dx_keep, exchange(dx_sent, mask))
        dx_keep, dx_sent = jnp.split(dx_keep, 2, axis=0)
    dx_spec = pl.BlockSpec((4, rows // tiles, D), lambda t, *a: (0, t, 0))
    dx_own = reduce_group(
        my_slot,
        [dx_keep.reshape(4, rows, D), exchange(dx_sent, CORE).reshape(4, rows, D)],
        [dx_spec] * 2,
        rows,
        D,
        read_rows,
        tiles,
    )
    input_grad = grad_first + dx_own

    vec_first, vec_second, vec_adam = adam_moments(vec_m, vec_v, vec_grad)
    bias_first, bias_second, bias_adam = adam_moments(bias_m, bias_v, bias_grad)

    squares = wa_total(
        jnp.concatenate([jnp.sum(attn_sums, axis=(1, 2)), jnp.sum(ffn_sums, axis=(1, 2))])
    )
    squares = jnp.sqrt(squares)
    attn_norm, attn_length, ffn_norm, ffn_length = (
        squares[:4], squares[4:8], squares[8:10], squares[10:]
    )
    attn_ratio = attn_norm / (attn_length + RATIO_EPS)
    ffn_ratio = ffn_norm / (ffn_length + RATIO_EPS)
    ffn_new, ffn_copy = final(ffn_ratio, ffn_master, ffn_step)
    attn_new, attn_copy = final(attn_ratio, attn_master, attn_step)
    ratios = jnp.concatenate([attn_ratio, ffn_ratio])
    norms = jnp.stack(
        [
            jnp.concatenate([attn_norm, ffn_norm]),
            jnp.concatenate([attn_length, ffn_length]),
        ],
        axis=1,
    )
    vec_new = vec_master - STEP_RATE * vec_adam
    bias_new = bias_master - STEP_RATE * bias_adam
    return (
        output[None],
        input_grad[None],
        attn_grad,
        ffn_grad,
        vec_grad,
        bias_grad,
        attn_new,
        ffn_new,
        vec_new,
        bias_new,
        attn_copy,
        ffn_copy,
        vec_new.astype(BF16),
        bias_new.astype(BF16),
        attn_first,
        ffn_first,
        vec_first,
        bias_first,
        attn_second,
        ffn_second,
        vec_second,
        bias_second,
        norms,
        ratios,
    )


def solution(mesh):
    tokens = P(WA, CTX, None)
    mats = P(None, WA, None)
    vecs = P(None, WA)
    line = P(WA)
    state = (mats, mats, vecs, line)
    in_specs = (
        (tokens, tokens, P(WA), P(WA, None), tokens)
        + (mats,) * 6
        + (vecs,) * 3
        + (line,) * 3
    )
    out_specs = (tokens, tokens) + state * 5 + (P(), P())
    return jax.shard_map(shards, mesh=mesh, in_specs=in_specs, out_specs=out_specs, check_vma=False)
```

```python
import functools

import jax
import jax.numpy as jnp
from jax import lax
from jax.experimental import pallas as pl
from jax.experimental.pallas import tpu as pltpu
from jax.sharding import PartitionSpec as P


D = 768
HEADS = 12
HEAD = 64
FF = 3072
BLOCK = 64
RAND = 3
SLOTS = 8
PAIRS = HEADS // 2
PAIR = 2 * HEAD
QUADS = HEADS // 4
QUAD = 4 * HEAD
EACH = 6

MASKED_SCORE = -1e30
LN_EPS = 1e-06
ADAM_EPS = 1e-06
RATIO_EPS = 1e-06
BETA_ONE = 0.5
BETA_TWO = 0.5
WEIGHT_DECAY = 0.01
STEP_RATE = 0.2


def grant(mib):
    return pltpu.CompilerParams(vmem_limit_bytes=mib << 20)


CTX = "ctx"
WA = "wa"

F32 = jnp.float32
BF16 = jnp.bfloat16
NT = (((1,), (1,)), ((), ()))
NN = (((1,), (0,)), ((), ()))
TN = (((0,), (0,)), ((), ()))


def mm(a, b, dims=NN):
    return lax.dot_general(a, b, dims, preferred_element_type=F32)


def heads_apart(part):
    lane = lax.broadcasted_iota(jnp.int32, part.shape, 1) // HEAD
    zero = jnp.zeros_like(part)
    return jnp.concatenate(
        [jnp.where(lane == head, part, zero) for head in range(part.shape[1] // HEAD)], axis=0
    )


def heads_joined(parts):
    count = parts.shape[1] // HEAD
    rows = parts.shape[0] // count
    lane = lax.broadcasted_iota(jnp.int32, (rows, parts.shape[1]), 1) // HEAD
    joined = parts[:rows]
    for head in range(1, count):
        joined = jnp.where(lane == head, parts[head * rows : (head + 1) * rows], joined)
    return joined


FRINGE = 4


def window_places(i, blocks):
    before = jnp.where(i == 0, blocks, i - 1)
    after = jnp.where(i == blocks - 1, blocks + 1, i + 1)
    return before, i, after


def slot_scores(keys, queries, nvalid_ref, base):
    s = mm(keys, queries, NT)
    row = lax.broadcasted_iota(jnp.int32, (BLOCK, s.shape[1]), 0)
    parts = [
        jnp.where(row < nvalid_ref[base + at], s[at * BLOCK : (at + 1) * BLOCK], MASKED_SCORE)
        for at in range(3)
    ]
    return jnp.concatenate(parts + [s[3 * BLOCK :]], axis=0)


def slot_rows(near_ref, rand_ref, i, columns):
    blocks = near_ref.shape[0] - FRINGE
    places = window_places(i, blocks) + (blocks + 2, blocks + 3)
    rows = [near_ref[at, :, columns] for at in places]
    return jnp.concatenate(rows + [rand_ref[at, :, columns] for at in range(RAND)], axis=0)


def sparse_fwd_kernel(nvalid_ref, q_ref, near_ref, rand_ref, out_ref, lse_ref):
    i = pl.program_id(0)
    for h in range(PAIRS):
        cols = slice(h * PAIR, (h + 1) * PAIR)
        vcols = slice(D + h * PAIR, D + (h + 1) * PAIR)
        queries = heads_apart(q_ref[:, cols])
        k = slot_rows(near_ref, rand_ref, i, cols)
        v = slot_rows(near_ref, rand_ref, i, vcols)
        s = slot_scores(k, queries, nvalid_ref, i * 3)
        top = jnp.max(s, axis=0, keepdims=True)
        p = jnp.exp(s - top)
        total = jnp.sum(p, axis=0, keepdims=True)
        p = (p * (1.0 / total)).astype(BF16)
        out_ref[:, cols] = heads_joined(mm(p, v, TN)).astype(BF16)
        at = slice(h % 2 * PAIR, (h % 2 + 1) * PAIR)
        lse_ref[0, h // 2 : h // 2 + 1, at] = top + jnp.log(total)


def attention_bwd_kernel(
    nvalid_ref, q_ref, do_ref, lse_ref, near_ref, rand_ref, gq_ref, gdo_ref, gdo_in_ref, gout_ref,
    dq_ref, grads_ref, acc_ref
):
    i = pl.program_id(0)
    blocks = near_ref.shape[0] - FRINGE
    rows = gq_ref.shape[0]
    keys = blocks * BLOCK

    @pl.when(i == 0)
    def _():
        acc_ref[...] = jnp.zeros_like(acc_ref)
        dq_ref[keys:] = jnp.zeros((FRINGE * BLOCK, D), BF16)

    @pl.when(i < blocks)
    def _():
        places = window_places(i, blocks) + (blocks + 2, blocks + 3)
        for h in range(QUADS):
            cols = slice(h * QUAD, (h + 1) * QUAD)
            vcols = slice(D + h * QUAD, D + (h + 1) * QUAD)
            queries = heads_apart(q_ref[:, cols])
            douts = heads_apart(do_ref[:, cols])
            k = slot_rows(near_ref, rand_ref, i, cols)
            v = slot_rows(near_ref, rand_ref, i, vcols)
            s = slot_scores(k, queries, nvalid_ref, i * 3)
            p = jnp.exp(s - lse_ref[0, h : h + 1, :])
            dp = mm(v, douts, NT)
            ds = (p * (dp - jnp.sum(p * dp, axis=0, keepdims=True))).astype(BF16)
            dq = heads_joined(mm(ds, k, TN)) * (HEAD**-0.5)
            dq_ref[pl.ds(pl.multiple_of(i * BLOCK, BLOCK), BLOCK), cols] = dq.astype(BF16)
            dk = mm(ds, queries).reshape(SLOTS, BLOCK, QUAD)
            dv = mm(p.astype(BF16), douts).reshape(SLOTS, BLOCK, QUAD)
            for grad, to in ((dk, cols), (dv, vcols)):
                for at, place in enumerate(places):
                    acc_ref[place, :, to] += grad[at]
                grads_ref[:, :, to] = grad[len(places) :].astype(BF16)

    @pl.when(i == blocks)
    def _():
        ok = lax.broadcasted_iota(jnp.int32, (keys, 2 * rows), 0) < nvalid_ref[blocks * 3]

        @pl.loop(0, PAIRS)
        def _(h):
            cols = pl.ds(pl.multiple_of(h * PAIR, PAIR), PAIR)
            vcols = pl.ds(pl.multiple_of(D + h * PAIR, PAIR), PAIR)
            queries = heads_apart(gq_ref[:, cols])
            douts = heads_apart(gdo_ref[:, cols] + gdo_in_ref[:, cols])
            out = gout_ref[h, :rows]
            outs = jnp.concatenate([out, out], axis=0)
            dot = jnp.sum((douts.astype(F32) * outs).T, axis=0, keepdims=True)
            lse = jnp.concatenate(
                [gout_ref[h, rows : rows + 1], gout_ref[h, rows + 1 : rows + 2]], axis=1
            )
            k = near_ref[:blocks, :, cols].reshape(keys, PAIR)
            v = near_ref[:blocks, :, vcols].reshape(keys, PAIR)
            p = jnp.where(ok, jnp.exp(mm(k, queries, NT) - lse), 0.0)
            ds = (p * (mm(v, douts, NT) - dot)).astype(BF16)
            dq = heads_joined(mm(ds, k, TN)) * (HEAD**-0.5)
            dq_ref[keys + FRINGE * BLOCK - rows :, cols] = dq.astype(BF16)
            acc_ref[:blocks, :, cols] += mm(ds, queries).reshape(blocks, BLOCK, PAIR)
            acc_ref[:blocks, :, vcols] += mm(p.astype(BF16), douts).reshape(blocks, BLOCK, PAIR)

    @pl.when(i >= blocks)
    def _():
        grads_ref[...] = acc_ref[pl.ds((i - blocks) * RAND, RAND)].astype(BF16)


def piece_copies(held, slot, buf_ref, sems, to, part):
    group, place = divmod(slot, GROUP)
    side, place = divmod(place, 4)
    own, first, second, upper, lower = held[10 * group + 5 * side : 10 * group + 5 * side + 5]
    rows = own.shape[0]
    half = rows // 2
    start = part * rows
    jobs = [(upper, start, half), (lower, start + half, half)]
    if place < 3:
        jobs = [((own, first, second)[place], start, rows)]
    return [
        pltpu.make_async_copy(ref, buf_ref.at[to, pl.ds(at, size)], sems.at[to, 2 * part + n])
        for n, (ref, at, size) in enumerate(jobs)
    ]


def global_fwd_kernel(pair_ref, nvalid_ref, q_ref, k_ref, v_ref, b_ref, *refs):
    held = refs[:-7]
    out_ref, top_ref, sum_ref, acc_ref, w_ref, buf_ref, sems = refs[-7:]
    c = pl.program_id(0)
    rows = q_ref.shape[0]
    keys = buf_ref.shape[1]
    count = len(held) // 10 * GROUP // 2

    def copies(at, to):
        return piece_copies(held, 2 * at, buf_ref, sems, to, 0) + piece_copies(
            held, 2 * at + 1, buf_ref, sems, to, 1
        )

    @pl.when(c == 0)
    def _():
        w_ref[:, :PAIR] = k_ref[...]
        w_ref[:, PAIR:] = v_ref[...]
        top_ref[...] = jnp.full_like(top_ref, MASKED_SCORE)
        sum_ref[...] = jnp.zeros_like(sum_ref)
        acc_ref[...] = jnp.zeros_like(acc_ref)

    for at in range(count):

        @pl.when(c == at)
        def _():
            if at == 0:
                for copy in copies(0, 0):
                    copy.start()
            if at + 1 < count:
                for copy in copies(at + 1, (at + 1) % 2):
                    copy.start()
            for copy in copies(at, at % 2):
                copy.wait()

    @pl.when(nvalid_ref[2 * c] + nvalid_ref[2 * c + 1] > 0)
    def _():
        x = buf_ref[lax.rem(c, 2)]
        kv = mm(x, w_ref[...])
        k = kv[:, :PAIR].astype(BF16)
        v = (kv[:, PAIR:] + b_ref[...]).astype(BF16)
        row = lax.broadcasted_iota(jnp.int32, (keys // 2, 2 * rows), 0)
        s = mm(k, heads_apart(q_ref[...]), NT)
        s = jnp.concatenate(
            [
                jnp.where(row < nvalid_ref[2 * c], s[: keys // 2], MASKED_SCORE),
                jnp.where(row < nvalid_ref[2 * c + 1], s[keys // 2 :], MASKED_SCORE),
            ],
            axis=0,
        )
        before = top_ref[...]
        top = jnp.maximum(before, jnp.max(s, axis=0, keepdims=True))
        p = jnp.exp(s - top)
        shrink = jnp.exp(before - top)
        sum_ref[...] = sum_ref[...] * shrink + jnp.sum(p, axis=0, keepdims=True)
        acc_ref[...] = acc_ref[...] * shrink + mm(v, p.astype(BF16), TN)
        top_ref[...] = top

    @pl.when(c == pl.num_programs(0) - 1)
    def _():
        total = sum_ref[...]
        lse = top_ref[...] + jnp.log(total)
        out_ref[:rows] = heads_joined((acc_ref[...] / total).T)
        out_ref[rows : rows + 1] = lse[:, :rows]
        out_ref[rows + 1 : rows + 2] = lse[:, rows:]
        out_ref[rows + 2 :] = jnp.zeros((6, PAIR), F32)


def kv_used_kernel(start_ref, order_ref, index_ref, w_ref, b_ref, *refs):
    held = refs[:-4]
    kv_ref, x_ref, buf_ref, sems = refs[-4:]
    step = pl.program_id(0)
    each = x_ref.shape[0] // BLOCK

    def copy(ref, start, at):
        start = pl.multiple_of(start * BLOCK, BLOCK)
        return pltpu.make_async_copy(ref.at[pl.ds(start, BLOCK)], buf_ref.at[at], sems.at[at])

    @pl.when(step == 0)
    def _():
        for which, ref in enumerate(held):

            @pl.loop(start_ref[which], start_ref[which + 1])
            def _(n):
                copy(ref, index_ref[n], order_ref[n]).start()

    for at in range(each):
        copy(held[0], 0, step * each + at).wait()
    x_ref[...] = buf_ref[pl.ds(step * each, each)].reshape(each * BLOCK, D)

    kv_ref[...] = (mm(x_ref[...], w_ref[...]) + b_ref[...]).astype(BF16)


def place_blocks_kernel(table_ref, x_ref, q_ref, low_ref, high_ref):
    low_ref[...] = jnp.zeros_like(low_ref)
    high_ref[...] = jnp.zeros_like(high_ref)
    limit = low_ref.shape[0]

    def step(s, part):
        to = table_ref[s]

        @pl.when(to < limit)
        def _():
            low_ref[to] += part

        @pl.when(to >= limit)
        def _():
            high_ref[to - limit] += part

    @pl.loop(0, q_ref.shape[0])
    def _(s):
        step(s, x_ref[s] + q_ref[s])

    @pl.loop(q_ref.shape[0], x_ref.shape[0])
    def _(s):
        step(s, x_ref[s])


def whole(shape):
    return pl.BlockSpec(shape, lambda *a: (0,) * len(shape))


VMEM_SPEC = pl.BlockSpec(memory_space=pltpu.VMEM)
SMEM_SPEC = pl.BlockSpec(memory_space=pltpu.SMEM)


def cost(flops, moved, exps=0):
    return pl.CostEstimate(flops=int(flops), bytes_accessed=int(moved), transcendentals=int(exps))


def near_spec(near):
    return pl.BlockSpec((near, BLOCK, 2 * D), lambda i, n: (0, 0, 0))


def rand_spec(near):
    return pl.BlockSpec((RAND, BLOCK, 2 * D), lambda i, n: (near // RAND + i, 0, 0))


def sparse_fwd(nvalid, q, kv_used):
    rows = q.shape[0]
    blocks = rows // BLOCK
    near = blocks + FRINGE
    work = 2 * rows * SLOTS * BLOCK * D
    return pl.pallas_call(
        sparse_fwd_kernel,
        grid_spec=pltpu.PrefetchScalarGridSpec(
            num_scalar_prefetch=1,
            grid=(blocks,),
            in_specs=[
                pl.BlockSpec((BLOCK, D), lambda i, n: (i, 0)),
                near_spec(near),
                rand_spec(near),
            ],
            out_specs=[
                pl.BlockSpec((BLOCK, D), lambda i, n: (i, 0)),
                pl.BlockSpec((1, 8, QUAD), lambda i, n: (i, 0, 0)),
            ],
        ),
        out_shape=[
            jax.ShapeDtypeStruct((rows, D), BF16),
            jax.ShapeDtypeStruct((blocks, 8, QUAD), F32),
        ],
        cost_estimate=cost(2 * work, rows * SLOTS * D * 4, rows * SLOTS * BLOCK * HEADS),
        compiler_params=grant(8),
        name="sf",
    )(nvalid, q, kv_used, kv_used)


def attention_bwd(nvalid, q, dout, lse, kv_used, glob_q, glob_do, glob_do_in, glob_out):
    rows = q.shape[0]
    blocks = rows // BLOCK
    near = blocks + FRINGE
    last = blocks - 1
    glob = glob_q.shape[0]
    work = 2 * (rows + glob) * SLOTS * BLOCK * D
    each = pl.BlockSpec((BLOCK, D), lambda i, n: (jnp.minimum(i, last), 0))
    rand = (RAND, BLOCK, 2 * D)
    return pl.pallas_call(
        attention_bwd_kernel,
        grid_spec=pltpu.PrefetchScalarGridSpec(
            num_scalar_prefetch=1,
            grid=(blocks + near // RAND,),
            in_specs=[
                each,
                each,
                pl.BlockSpec((1, 8, QUAD), lambda i, n: (jnp.minimum(i, last), 0, 0)),
                near_spec(near),
                pl.BlockSpec(rand, lambda i, n: (near // RAND + jnp.minimum(i, last), 0, 0)),
                whole((glob, D)),
                whole((glob, D)),
                whole((glob, D)),
                whole(glob_out.shape),
            ],
            out_specs=[
                whole((near * BLOCK, D)),
                pl.BlockSpec(
                    rand,
                    lambda i, n: (jnp.where(i < blocks, near // RAND + i, i - blocks), 0, 0),
                ),
            ],
            scratch_shapes=[pltpu.VMEM((near, BLOCK, 2 * D), F32)],
        ),
        out_shape=[
            jax.ShapeDtypeStruct((near * BLOCK, D), BF16),
            jax.ShapeDtypeStruct(kv_used.shape, BF16),
        ],
        cost_estimate=cost(5 * work, rows * SLOTS * D * 8, rows * SLOTS * BLOCK * HEADS),
        compiler_params=grant(20),
        name="sb",
    )(nvalid, q, dout, lse, kv_used, kv_used, glob_q, glob_do, glob_do_in, glob_out)


def global_fwd(pair, nvalid, q, w_kv, kv_bias, held):
    rows = q.shape[0]
    chunks = nvalid.shape[0]
    keys = 2 * held[0].shape[0]
    chunks //= 2
    return pl.pallas_call(
        global_fwd_kernel,
        grid_spec=pltpu.PrefetchScalarGridSpec(
            num_scalar_prefetch=2,
            grid=(chunks,),
            in_specs=[
                pl.BlockSpec((rows, PAIR), lambda c, p, n: (0, p[0])),
                pl.BlockSpec((D, PAIR), lambda c, p, n: (0, p[0])),
                pl.BlockSpec((D, PAIR), lambda c, p, n: (0, PAIRS + p[0])),
                pl.BlockSpec((1, PAIR), lambda c, p, n: (0, PAIRS + p[0])),
            ]
            + [pl.BlockSpec(memory_space=pl.ANY)] * len(held),
            out_specs=pl.BlockSpec((rows + 8, PAIR), lambda c, p, n: (0, 0)),
            scratch_shapes=[pltpu.VMEM((1, 2 * rows), F32)] * 2
            + [
                pltpu.VMEM((PAIR, 2 * rows), F32),
                pltpu.VMEM((D, 2 * PAIR), BF16),
                pltpu.VMEM((2, keys, D), BF16),
                pltpu.SemaphoreType.DMA((2, 4)),
            ],
        ),
        out_shape=jax.ShapeDtypeStruct((rows + 8, PAIR), F32),
        cost_estimate=cost(
            4 * (rows + D) * chunks * keys * PAIR,
            2 * chunks * keys * D,
            2 * rows * chunks * keys,
        ),
        compiler_params=grant(8),
        name="gf",
    )(pair[None], nvalid, q, w_kv, w_kv, kv_bias, *held)


def source_lists(source, index, ctx_count):
    number = jnp.arange(source.shape[0], dtype=jnp.int32)
    earlier = (source[None] < source[:, None]) | (
        (source[None] == source[:, None]) & (number[None] < number[:, None])
    )
    rank = jnp.sum(earlier, axis=1, dtype=jnp.int32)
    chosen = (rank[None] == number[:, None]).astype(jnp.int32)
    order = jnp.sum(chosen * number[None], axis=1, dtype=jnp.int32)
    places = jnp.sum(chosen * index[None], axis=1, dtype=jnp.int32)
    sources = jnp.arange(ctx_count // GROUP * 10 + 1, dtype=jnp.int32)
    starts = jnp.sum(source[None] < sources[:, None], axis=1, dtype=jnp.int32)
    return order, places, starts


def kv_used_rows(starts, order, places, w_kv, kv_bias, held):
    count = order.shape[0]
    each = EACH
    rows = each * BLOCK
    return pl.pallas_call(
        kv_used_kernel,
        grid_spec=pltpu.PrefetchScalarGridSpec(
            num_scalar_prefetch=3,
            grid=(count // each,),
            in_specs=[whole((D, 2 * D)), whole((1, 2 * D))]
            + [pl.BlockSpec(memory_space=pl.ANY)] * len(held),
            out_specs=[
                pl.BlockSpec((rows, 2 * D), lambda t, *a: (t, 0)),
                pl.BlockSpec((rows, D), lambda t, *a: (t, 0)),
            ],
            scratch_shapes=[
                pltpu.VMEM((count, BLOCK, D), BF16),
                pltpu.SemaphoreType.DMA((count,)),
            ],
        ),
        out_shape=[
            jax.ShapeDtypeStruct((count * BLOCK, 2 * D), BF16),
            jax.ShapeDtypeStruct((count * BLOCK, D), BF16),
        ],
        cost_estimate=cost(4 * count * BLOCK * D * D, 8 * count * BLOCK * D),
        compiler_params=grant(16),
        name="kv",
    )(starts, order, places, w_kv, kv_bias, *held)


def place_blocks(table, x_blocks, q_blocks, total):
    half = jax.ShapeDtypeStruct((total // 2,) + x_blocks.shape[1:], BF16)
    return pl.pallas_call(
        place_blocks_kernel,
        in_specs=[SMEM_SPEC, VMEM_SPEC, VMEM_SPEC],
        out_specs=[VMEM_SPEC, VMEM_SPEC],
        out_shape=[half, half],
        cost_estimate=cost(0, 2 * (total + 2 * x_blocks.shape[0]) * BLOCK * D),
        compiler_params=grant(4 + (total + x_blocks.shape[0] + q_blocks.shape[0]) * BLOCK * D // (1 << 19)),
        name="pb",
    )(table, x_blocks, q_blocks)


CORE, FIRST, SECOND = 1, 2, 4
GROUP = 8
CUT = 3 * D // GROUP + D // GROUP


def exchange(value, mask):
    count = lax.axis_size(CTX)
    return lax.ppermute(value, CTX, [(i, i ^ mask) for i in range(count)])


def slot_of(index):
    return index // GROUP * GROUP + index // 2 % 4 + index % 2 * 4


def index_of(slot):
    return slot // GROUP * GROUP + slot % 4 * 2 + slot // 4 % 2


def spare_masks():
    return [1 << i for i in range(3, lax.axis_size(CTX).bit_length() - 1)]


def all_masks():
    return [CORE, FIRST, SECOND] + spare_masks()


def wa_shift(value, step):
    count = lax.axis_size(WA)
    return lax.ppermute(value, WA, [(i, (i + step) % count) for i in range(count)])


def wa_parts(piece):
    return [piece] + [wa_shift(piece, step) for step in range(1, lax.axis_size(WA))]


def wa_reduce(chunks):
    count = lax.axis_size(WA)
    rank = lax.axis_index(WA)

    def chunk(step):
        return lax.dynamic_index_in_dim(chunks, (rank + step) % count, 0, keepdims=False)

    arrived = [wa_shift(chunk(step), step) for step in range(1, count)]
    total = chunk(0).astype(F32)
    for part in arrived:
        total = total + part.astype(F32)
    return total


def wa_total(value):
    count = lax.axis_size(WA)
    mask = 1
    while mask < count:
        pairs = [(i, i ^ mask) for i in range(count)]
        value = value + lax.ppermute(value, WA, pairs)
        mask *= 2
    return value


def bit_of(mask):
    return (lax.axis_index(CTX) // mask) % 2 == 1


def gather_group(own, then=None):
    cut = own.shape[0] // 2
    first = exchange(own, FIRST)
    second = exchange(own, SECOND)
    upper, lower = first[:cut], second[cut:]
    if then is not None:
        upper, lower, then = lax.optimization_barrier((upper, lower, then))
    upper = exchange(upper, SECOND)
    lower = exchange(lower, FIRST)
    near = [own, first, second, upper, lower]
    held = near + [exchange(part, CORE) for part in near]
    return held if then is None else (held, then)


def gather_direct(own):
    near = [own] + [exchange(own, mask) for mask in (FIRST, SECOND, FIRST | SECOND)]
    return near + [exchange(part, CORE) for part in near]


def group_in_order(own):
    value = own[None]
    for mask in (FIRST, SECOND, CORE):
        other = exchange(value, mask)
        high = bit_of(mask)
        value = jnp.concatenate(
            [jnp.where(high, other, value), jnp.where(high, value, other)], axis=0
        )
    return value


def add_low(first, second):
    return (first.astype(F32) + second.astype(F32)).astype(BF16)


def cut_kernel(where_ref, attn_ref, ffn_ref, vec_ref, bias_ref, attn_out, ffn_out):
    wide = attn_ref.shape[1]
    attn_out[:wide, :] = attn_ref[0].astype(BF16)
    empty = jnp.zeros((8, CUT - wide), F32)
    vectors = jnp.concatenate([vec_ref[...], empty], axis=1)
    count = bias_ref.shape[1] // CUT
    bias = [bias_ref[:, at * CUT : (at + 1) * CUT] for at in range(count)]
    small = jnp.concatenate([vectors] + bias + [jnp.zeros((8 - count, CUT), F32)], axis=0)
    attn_out[wide:, :] = small.astype(BF16)
    ffn_out[:, :CUT] = ffn_ref[0].astype(BF16)
    ffn_out[:, CUT:] = ffn_ref[1].astype(BF16)


def cut_pieces(slot, attn_master, ffn_master, vec_master, bias_row):
    wide = attn_master.shape[1]
    return pl.pallas_call(
        cut_kernel,
        grid_spec=pltpu.PrefetchScalarGridSpec(
            num_scalar_prefetch=1,
            grid=(1,),
            in_specs=[
                pl.BlockSpec((1, wide, CUT), lambda i, w: (w[0] // 2, 0, w[0] % 2)),
                pl.BlockSpec((2, wide, CUT), lambda i, w: (0, 0, w[0])),
                whole((8, wide)),
                whole(bias_row.shape),
            ],
            out_specs=[whole((wide + 16, CUT)), whole((wide, 2 * CUT))],
        ),
        out_shape=[
            jax.ShapeDtypeStruct((wide + 16, CUT), BF16),
            jax.ShapeDtypeStruct((wide, 2 * CUT), BF16),
        ],
        cost_estimate=cost(0, wide * CUT * 18),
        compiler_params=grant(4),
        name="cut",
    )(slot[None], attn_master, ffn_master, vec_master, bias_row)


def join_kernel(rank_ref, *refs):
    parts, outs = refs[: len(refs) - 2], refs[len(refs) - 2 :]
    count = len(parts)
    wide = outs[0].shape[0] // count
    for step, part in enumerate(parts):
        at = lax.rem(rank_ref[0] - step + count, count)
        outs[0][pl.ds(pl.multiple_of(at * wide, 16), wide), :] = part[:wide]
        outs[1][at] = part[part.shape[0] - 16 :]


def join_rows(rank, parts):
    count = len(parts)
    extra = parts[0].shape[0] % 32
    wide = parts[0].shape[0] - extra
    columns = parts[0].shape[1]
    return pl.pallas_call(
        join_kernel,
        in_specs=[SMEM_SPEC] + [VMEM_SPEC] * count,
        out_specs=[VMEM_SPEC, VMEM_SPEC],
        out_shape=[
            jax.ShapeDtypeStruct((count * wide, columns), BF16),
            jax.ShapeDtypeStruct((count, 16, columns), BF16),
        ],
        cost_estimate=cost(0, 4 * count * wide * columns),
        compiler_params=grant(6),
        name="join",
    )(rank[None], *parts)


def held_specs(rows, columns, tiles):
    shape = (rows // tiles, columns)
    middle = tiles // 2
    each = [
        pl.BlockSpec(shape, lambda t, *a: (t, 0)),
        pl.BlockSpec(shape, lambda t, *a: (t, 0)),
        pl.BlockSpec(shape, lambda t, *a: (t, 0)),
        pl.BlockSpec(shape, lambda t, *a: (jnp.minimum(t, middle - 1), 0)),
        pl.BlockSpec(shape, lambda t, *a: (jnp.maximum(t - middle, 0), 0)),
    ]
    return each + each


def for_each_slot(held, body):
    upper = pl.program_id(0) < pl.num_programs(0) // 2
    for side in range(2):
        own, first, second, up, low = held[5 * side : 5 * side + 5]
        for at, ref in enumerate((own, first, second)):
            body(4 * side + at, ref)
        pl.when(upper)(functools.partial(body, 4 * side + 3, up))
        pl.when(jnp.logical_not(upper))(functools.partial(body, 4 * side + 3, low))


def attn_weights_kernel(slot_ref, *refs):
    held, (q_ref, kv_ref, o_ref) = refs[:10], refs[10:]

    def body(slot, ref):
        at = slot_ref[0] ^ slot
        for out, start, stop in ((q_ref, 0, 2), (kv_ref, 2, 6), (o_ref, 6, 8)):

            @pl.when((at >= start) & (at < stop))
            def _():
                out[:, pl.ds(pl.multiple_of((at - start) * CUT, 128), CUT)] = ref[...]

    for_each_slot(held, body)


def attn_weights(slot, held):
    rows = held[0].shape[0]
    tiles = 4
    size = rows // tiles
    widths = (D, 2 * D, D)
    return pl.pallas_call(
        attn_weights_kernel,
        grid_spec=pltpu.PrefetchScalarGridSpec(
            num_scalar_prefetch=1,
            grid=(tiles,),
            in_specs=held_specs(rows, CUT, tiles),
            out_specs=[pl.BlockSpec((size, w), lambda t, *a: (t, 0)) for w in widths],
        ),
        out_shape=[jax.ShapeDtypeStruct((rows, w), BF16) for w in widths],
        cost_estimate=cost(0, 4 * rows * GROUP * CUT),
        compiler_params=grant(8),
        name="aw",
    )(slot[None], *held)


STRIDE = 2


def matrix_copies(held, step, up_ref, down_ref, sems, to):
    jobs = []
    half = D // 2
    for at in range(STRIDE):
        side, place = divmod(step * STRIDE + at, 4)
        own, first, second, upper, lower = held[5 * side : 5 * side + 5]
        parts = [(upper, 0, half), (lower, half, half)]
        if place < 3:
            parts = [((own, first, second)[place], 0, D)]
        for ref, start, size in parts:
            for which, buf in enumerate((up_ref, down_ref)):
                source = ref.at[:, pl.ds(which * CUT, CUT)]
                target = buf.at[to, pl.ds(start, size), pl.ds(at * CUT, CUT)]
                jobs.append(pltpu.make_async_copy(source, target, sems.at[to, len(jobs)]))
    return jobs


def fetch_matrices(held, up_ref, down_ref, sems):
    step = pl.program_id(0)
    for at in range(GROUP // STRIDE):

        @pl.when(step == at)
        def _():
            if at == 0:
                for copy in matrix_copies(held, 0, up_ref, down_ref, sems, 0):
                    copy.start()
            if at + 1 < GROUP // STRIDE:
                for copy in matrix_copies(held, at + 1, up_ref, down_ref, sems, (at + 1) % 2):
                    copy.start()
            for copy in matrix_copies(held, at, up_ref, down_ref, sems, at % 2):
                copy.wait()

    return lax.rem(step, 2)


def add_up(total_ref, part):
    @pl.when(pl.program_id(0) == 0)
    def _():
        total_ref[...] = part

    @pl.when(pl.program_id(0) > 0)
    def _():
        total_ref[...] += part


def ffn_fwd_kernel(n_ref, b_ref, *refs):
    held = refs[:10]
    hidden_ref, slope_ref, total_ref, w_up_ref, w_down_ref, up_ref, down_ref, sems = refs[10:]
    now = fetch_matrices(held, up_ref, down_ref, sems)
    up = mm(n_ref[...], up_ref[now]) + b_ref[0]
    cdf = 0.5 * (1.0 + lax.erf(up * (0.5**0.5)))
    hidden = (up * cdf).astype(BF16)
    hidden_ref[...] = hidden
    slope_ref[...] = (cdf + up * (jnp.exp(-0.5 * up * up) * 0.3989422804014327)).astype(BF16)
    add_up(total_ref, mm(hidden, down_ref[now], NT))
    w_up_ref[...] = up_ref[now]
    w_down_ref[...] = down_ref[now]


def ffn_scratch():
    buf = pltpu.VMEM((2, D, STRIDE * CUT), BF16)
    return [buf, buf, pltpu.SemaphoreType.DMA((2, 4 * STRIDE))]


def ffn_fwd(norm_low, bias, held):
    rows = norm_low.shape[0]
    wide = pl.BlockSpec((rows, STRIDE * CUT), lambda t: (0, t))
    full = pl.BlockSpec((D, STRIDE * CUT), lambda t: (0, t))
    return pl.pallas_call(
        ffn_fwd_kernel,
        grid=(GROUP // STRIDE,),
        in_specs=[whole((rows, D)), pl.BlockSpec((1, 1, STRIDE * CUT), lambda t: (t, 0, 0))]
        + [pl.BlockSpec(memory_space=pl.ANY)] * 10,
        out_specs=[wide, wide, whole((rows, D)), full, full],
        out_shape=[
            jax.ShapeDtypeStruct((rows, FF), BF16),
            jax.ShapeDtypeStruct((rows, FF), BF16),
            jax.ShapeDtypeStruct((rows, D), F32),
            jax.ShapeDtypeStruct((D, FF), BF16),
            jax.ShapeDtypeStruct((D, FF), BF16),
        ],
        scratch_shapes=ffn_scratch(),
        cost_estimate=cost(4 * rows * D * FF, 4 * rows * FF + 4 * D * FF, 2 * rows * FF),
        compiler_params=grant(22),
        name="ff",
    )(norm_low, bias.reshape(-1, 1, STRIDE * CUT), *held)


def spread_kernel(slot_ref, *refs, read):
    keep, outs = refs[:-4], refs[-4:]
    for slot, out in enumerate(outs):
        out[...] = read(slot_ref, keep, slot).astype(BF16)


def read_ffn(slot_ref, refs, slot):
    at = slice(slot * CUT, (slot + 1) * CUT)
    up, down, up_in, down_in = (r[:, at].astype(F32) for r in refs)
    return jnp.concatenate([up + up_in, down + down_in], axis=1)


def read_attn(slot_ref, refs, slot):
    at = (slot_ref[0] ^ slot) % 4
    columns = pl.ds(pl.multiple_of(at % 2 * CUT, 128), CUT)
    return refs[0][at // 2, :, columns].astype(F32) + refs[1][at // 2, :, columns].astype(F32)


def read_rows(slot_ref, refs, slot):
    return refs[0][slot].astype(F32) + refs[1][slot].astype(F32)


def spread(slot, arrays, in_specs, rows, columns, read, tiles):
    block = pl.BlockSpec((rows // tiles, columns), lambda t, *a: (t, 0))
    return pl.pallas_call(
        functools.partial(spread_kernel, read=read),
        grid_spec=pltpu.PrefetchScalarGridSpec(
            num_scalar_prefetch=1, grid=(tiles,), in_specs=in_specs, out_specs=[block] * 4
        ),
        out_shape=[jax.ShapeDtypeStruct((rows, columns), BF16)] * 4,
        cost_estimate=cost(0, rows * columns * 24),
        compiler_params=grant(10),
    )(slot[None], *arrays)


def reduce_group(slot, arrays, in_specs, rows, columns, read, tiles=4):
    own, *others = spread(slot, arrays, in_specs, rows, columns, read, tiles)
    total = own.astype(F32)
    for part, mask in zip(others, (FIRST, SECOND, FIRST | SECOND)):
        total = total + exchange(part, mask).astype(F32)
    return total


def pack_kernel(slot_ref, *refs):
    rows, bias_ref, out_ref = refs[:8], refs[8], refs[9]
    shards = out_ref.shape[0]
    wide = D // shards
    count = GROUP // shards if shards < GROUP else 1
    vectors = jnp.concatenate([ref[...] for ref in rows], axis=0)
    out_ref[...] = jnp.zeros_like(out_ref)
    for shard in range(shards):
        out_ref[shard, :8, :wide] = vectors[:, shard * wide : (shard + 1) * wide]
        for at in range(count):
            slot = slot_ref[0] ^ (shard * count + at)
            out_ref[shard, 8 + at : 9 + at, :] = bias_ref[
                :, pl.ds(pl.multiple_of(slot * CUT, 128), CUT)
            ]


def pack_small(slot, rows, bias, shards):
    return pl.pallas_call(
        pack_kernel,
        in_specs=[SMEM_SPEC] + [VMEM_SPEC] * 9,
        out_specs=VMEM_SPEC,
        out_shape=jax.ShapeDtypeStruct((shards, 16, CUT), F32),
        compiler_params=grant(4),
        cost_estimate=cost(0, 200000),
        name="pk",
    )(slot[None], *rows, bias)


def adam_kernel(slot_ref, *refs, pieces):
    held = refs[:GROUP]
    w_ref, m_ref, v_ref, grad_ref, first_ref, second_ref, step_ref, sums_ref = refs[GROUP:]
    for slot, ref in enumerate(held):
        at = slot_ref[0] ^ slot
        if pieces == 1:
            columns = pl.ds(pl.multiple_of(at % 2 * CUT, 128), CUT)
            grad_ref[at // 2, :, columns] = ref[...].astype(F32)
        else:
            columns = pl.ds(pl.multiple_of(at * CUT, 128), CUT)
            grad_ref[0, :, columns] = ref[:, :CUT].astype(F32)
            grad_ref[1, :, columns] = ref[:, CUT:].astype(F32)

    @pl.when(pl.program_id(0) == 0)
    def _():
        sums_ref[...] = jnp.zeros_like(sums_ref)

    mats, rows, columns = grad_ref.shape
    each = 8 if columns > D else 24

    @pl.loop(0, mats * (rows // each))
    def _(step):
        mat = step // (rows // each)
        here = pl.ds(pl.multiple_of(step % (rows // each) * each, each), each)
        grad = grad_ref[mat, here]
        first = BETA_ONE * m_ref[mat, here] + (1.0 - BETA_ONE) * grad
        second = BETA_TWO * v_ref[mat, here] + (1.0 - BETA_TWO) * grad * grad
        weight = w_ref[mat, here]
        move = first / (jnp.sqrt(second) + ADAM_EPS) + WEIGHT_DECAY * weight
        first_ref[mat, here] = first
        second_ref[mat, here] = second
        step_ref[mat, here] = move.astype(BF16)
        for row, part in ((mat, weight), (mats + mat, move)):
            sums_ref[row] += jnp.sum((part * part).reshape(each // 8, 8, columns), axis=0)


def final(ratios, master, step):
    new = master - (STEP_RATE * ratios)[:, None, None] * step.astype(F32)
    return new, new.astype(BF16)


def adam(slot, held, master, first, second):
    mats, wide, columns = master.shape
    tiles = 4
    size = wide // tiles
    piece_columns = held[0].shape[1]
    block = pl.BlockSpec((mats, size, columns), lambda t, *a: (0, t, 0))
    full = jax.ShapeDtypeStruct(master.shape, F32)
    return pl.pallas_call(
        functools.partial(adam_kernel, pieces=piece_columns // CUT),
        grid_spec=pltpu.PrefetchScalarGridSpec(
            num_scalar_prefetch=1,
            grid=(tiles,),
            in_specs=[pl.BlockSpec((size, piece_columns), lambda t, *a: (t, 0))] * GROUP
            + [block] * 3,
            out_specs=[block] * 4 + [whole((2 * mats, 8, columns))],
        ),
        out_shape=[full] * 3
        + [
            jax.ShapeDtypeStruct(master.shape, BF16),
            jax.ShapeDtypeStruct((2 * mats, 8, columns), F32),
        ],
        cost_estimate=cost(20 * master.size, 30 * master.size, master.size),
    )(slot[None], *held, master, first, second)


def norm_parts(hidden):
    centre = hidden - jnp.mean(hidden, axis=-1, keepdims=True)
    spread = jnp.mean(centre * centre, axis=-1, keepdims=True)
    inverse = lax.rsqrt(spread + LN_EPS)
    return centre * inverse, inverse


def norm_back(grad, normal, inverse, gain):
    scaled = grad * gain
    return inverse * (
        scaled
        - jnp.mean(scaled, axis=-1, keepdims=True)
        - normal * jnp.mean(scaled * normal, axis=-1, keepdims=True)
    )


def adam_moments(first, second, grads):
    first_new = BETA_ONE * first + (1.0 - BETA_ONE) * grads
    second_new = BETA_TWO * second + (1.0 - BETA_TWO) * grads * grads
    return (first_new, second_new, first_new / (jnp.sqrt(second_new) + ADAM_EPS))


def shards(
    inputs,
    cotangent,
    lengths,
    global_ids,
    random_ids,
    attn_master,
    attn_m,
    attn_v,
    ffn_master,
    ffn_m,
    ffn_v,
    vec_master,
    vec_m,
    vec_v,
    bias_master,
    bias_m,
    bias_v,
):
    x = inputs[0]
    rows = x.shape[0]
    ctx_count = lax.axis_size(CTX)
    rank = lax.axis_index(CTX)
    wa_count = lax.axis_size(WA)
    wa_rank = lax.axis_index(WA)
    blocks = rows // BLOCK
    total_blocks = blocks * ctx_count
    wide = D // wa_count
    seq_len = lengths[0]
    glob_ids = global_ids[0]
    my_slot = slot_of(rank) % GROUP
    relative = jnp.arange(ctx_count, dtype=jnp.int32)
    owner_at = rank ^ index_of(relative)

    attn_piece, ffn_piece = cut_pieces(
        my_slot, attn_master, ffn_master, vec_master, bias_master[None]
    )
    attn_parts = wa_parts(attn_piece)
    x_held, attn_parts = gather_group(x, attn_parts)
    attn_rows, small = join_rows(wa_rank, attn_parts)

    vectors = small[:, :8, :wide].transpose(1, 0, 2).reshape(8, D).astype(F32)
    bias_blocks = small[:, 8 : 8 + FF // wa_count // CUT].reshape(GROUP, CUT).astype(F32)
    bias_up = bias_blocks[my_slot ^ relative[:GROUP]]

    def place_of(block):
        block = jnp.clip(block, 0, total_blocks - 1)
        return slot_of((block // blocks) ^ rank) * blocks + block % blocks

    rand_ids = random_ids[0]
    own_blocks = rank * blocks + jnp.arange(blocks, dtype=jnp.int32)
    window = jnp.stack([own_blocks - 1, own_blocks, own_blocks + 1], axis=1)
    window_nvalid = jnp.where(
        (window >= 0) & (window < total_blocks), jnp.clip(seq_len - window * BLOCK, 0, BLOCK), 0
    ).reshape(-1)
    used_table = place_of(
        jnp.concatenate(
            [own_blocks, own_blocks[:1] - 1, own_blocks[-1:] + 1, glob_ids, rand_ids.reshape(-1)]
        )
    )
    used_slot, used_at = used_table // blocks, used_table % blocks
    split = (used_slot % 4 == 3) & (used_at >= blocks // 2)
    used_source = used_slot // 4 * 5 + used_slot % 4 + split
    used_index = used_at - jnp.where(split, blocks // 2, 0)
    chunk_nvalid = jnp.clip(seq_len - owner_at * rows, 0, rows)
    positions = rank * rows + jnp.arange(rows, dtype=jnp.int32)
    row_weight = (positions < seq_len).astype(F32)[:, None]
    hits = own_blocks[None, :] == glob_ids[:, None]

    kv_bias = jnp.concatenate([jnp.zeros((D,), F32), vectors[1]])[None]
    used_source, used_index, used_starts = source_lists(used_source, used_index, ctx_count)
    early = (
        vectors, bias_up, kv_bias, used_table, used_source, used_index, used_starts,
        window_nvalid, chunk_nvalid, row_weight, hits,
    )
    attn_held, early = gather_group(attn_rows, early)
    (
        vectors, bias_up, kv_bias, used_table, used_source, used_index, used_starts,
        window_nvalid, chunk_nvalid, row_weight, hits,
    ) = early
    w_query, w_kv, w_out = attn_weights(my_slot, attn_held)
    ffn_parts = wa_parts(ffn_piece)
    ffn_parts, w_kv = lax.optimization_barrier((ffn_parts, w_kv))
    ffn_rows, _ = join_rows(wa_rank, ffn_parts)
    ffn_held = gather_group(ffn_rows)

    scale = HEAD**-0.5
    groups = [x_held]
    for mask in spare_masks():
        groups += [[exchange(part, mask) for part in held] for held in groups]
    x_held = [part for held in groups for part in held]
    kv_used, x_used = kv_used_rows(used_starts, used_source, used_index, w_kv, kv_bias, x_held)
    near_rows = (blocks + FRINGE) * BLOCK
    x_near = x_used[:near_rows]
    x_glob = x_near[near_rows - 2 * BLOCK :]
    kv_used = kv_used.reshape(-1, BLOCK, 2 * D)
    glob_query = ((mm(x_glob, w_query) + vectors[0]).astype(BF16) * BF16(scale)).astype(BF16)
    glob_part = global_fwd(
        jnp.minimum(my_slot, PAIRS - 1), chunk_nvalid, glob_query, w_kv, kv_bias, x_held
    )
    glob_pairs = group_in_order(glob_part)
    query = ((mm(x, w_query, NN) + vectors[0]).astype(BF16) * BF16(scale)).astype(BF16)
    sparse_out, lse = sparse_fwd(window_nvalid, query, kv_used)
    glob_out = (
        glob_pairs[:PAIRS, : 2 * BLOCK].transpose(1, 0, 2).reshape(2, BLOCK, D).astype(BF16)
    )
    attended = sparse_out.reshape(blocks, BLOCK, D)
    for g in range(2):
        attended = jnp.where(hits[g][:, None, None], glob_out[g][None], attended)
    attended = attended.reshape(rows, D)

    first_sum = x.astype(F32) + mm(attended, w_out) + vectors[2]
    normal_one, inverse_one = norm_parts(first_sum)
    norm_one = normal_one * vectors[4] + vectors[5]
    norm_low = norm_one.astype(BF16)
    hidden_low, slope, down, w_up, w_down = ffn_fwd(norm_low, bias_up, ffn_held)
    second_sum = norm_one + down + vectors[3]
    normal_two, inverse_two = norm_parts(second_sum)
    output = ((normal_two * vectors[6] + vectors[7]) * row_weight).astype(BF16)
    grad_out = cotangent[0].astype(F32) * row_weight
    grad_second = norm_back(grad_out, normal_two, inverse_two, vectors[6])
    grad_down = grad_second.astype(BF16)
    grad_upper = (mm(grad_down, w_down) * slope.astype(F32)).astype(BF16)
    grad_norm = grad_second + mm(grad_upper, w_up, NT)
    grad_first = norm_back(grad_norm, normal_one, inverse_one, vectors[4])
    grad_branch = grad_first.astype(BF16)
    grad_attended = mm(grad_branch, w_out, NT).astype(BF16)

    cut = FF // 2
    up_sent = mm(norm_low, grad_upper[:, cut:], TN).astype(BF16)
    down_sent = mm(grad_down, hidden_low[:, cut:], TN).astype(BF16)
    up_keep = mm(norm_low, grad_upper[:, :cut], TN).astype(BF16)
    down_keep = mm(grad_down, hidden_low[:, :cut], TN).astype(BF16)
    tiles = 4
    ffn_spec = pl.BlockSpec((D // tiles, cut), lambda t, *a: (t, 0))

    def finish(total, extra=None):
        total = total.astype(BF16)
        for mask in spare_masks():
            total = add_low(total, exchange(total, mask))
        total = total.reshape(wa_count, wide, total.shape[1])
        if extra is not None:
            total = jnp.concatenate([total, extra], axis=1)
        return wa_reduce(total)

    ffn_mine = finish(
        reduce_group(
            my_slot,
            [up_keep, down_keep, exchange(up_sent, CORE), exchange(down_sent, CORE)],
            [ffn_spec] * 4,
            D,
            2 * CUT,
            read_ffn,
            tiles,
        ),
    ).astype(BF16)
    ffn_grad, ffn_first, ffn_second, ffn_step, ffn_sums = adam(
        my_slot, gather_direct(ffn_mine), ffn_master, ffn_m, ffn_v
    )

    grad_blocks = grad_attended.reshape(blocks, BLOCK, D)
    glob_part = jnp.sum(
        jnp.where(hits[:, :, None, None], grad_blocks[None], 0), axis=1, dtype=F32
    ).astype(BF16)
    for mask in all_masks()[:-1]:
        glob_part = glob_part + exchange(glob_part, mask)
    glob_in = exchange(glob_part, all_masks()[-1])
    grad_sparse = jnp.where((hits[0] | hits[1])[:, None, None], 0, grad_blocks).reshape(rows, D)
    near_dquery, used_grads = attention_bwd(
        jnp.concatenate([window_nvalid, chunk_nvalid[:1]]),
        query,
        grad_sparse,
        lse,
        kv_used,
        glob_query,
        glob_part.reshape(2 * BLOCK, D),
        glob_in.reshape(2 * BLOCK, D),
        glob_pairs,
    )
    used_grads = used_grads.reshape(-1, 2 * D)

    g_query = mm(x_near, near_dquery, TN).astype(BF16)
    g_kv = mm(x_used, used_grads, TN).astype(BF16)
    g_key, g_value = g_kv[:, :D], g_kv[:, D:]
    g_out = mm(attended, grad_branch, TN).astype(BF16)
    on_core = bit_of(CORE)
    early, late = jnp.stack([g_query, g_key]), jnp.stack([g_value, g_out])
    attn_sent = jnp.where(on_core, early, late)
    attn_keep = jnp.where(on_core, late, early)
    attn_spec = pl.BlockSpec((2, D // tiles, D), lambda t, *a: (0, t, 0))
    sums = [
        jnp.sum(part, axis=0, dtype=F32, keepdims=True)
        for part in (
            near_dquery,
            used_grads[:, D:],
            grad_branch,
            grad_down,
            grad_norm * normal_one,
            grad_norm,
            grad_out * normal_two,
            grad_out,
        )
    ]
    bias_sum = jnp.sum(grad_upper, axis=0, dtype=F32, keepdims=True)
    small_sum = pack_small(my_slot, sums, bias_sum, wa_count)
    for mask in all_masks():
        small_sum = small_sum + exchange(small_sum, mask)
    small_rows = small_sum.astype(BF16)

    attn_total = finish(
        reduce_group(
            my_slot,
            [attn_keep, exchange(attn_sent, CORE)],
            [attn_spec] * 2,
            D,
            CUT,
            read_attn,
            tiles,
        ),
        small_rows,
    )
    attn_mine = attn_total[:wide].astype(BF16)
    vec_grad = attn_total[wide : wide + 8, :wide]
    bias_grad = attn_total[wide + 8 : wide + 8 + FF // wa_count // CUT].reshape(-1)
    attn_grad, attn_first, attn_second, attn_step, attn_sums = adam(
        my_slot, gather_direct(attn_mine), attn_master, attn_m, attn_v
    )

    dx_used = mm(used_grads, w_kv, NT).astype(BF16)
    dx_query = mm(near_dquery, w_query, NT).astype(BF16)
    dx_keep, dx_sent = place_blocks(
        used_table,
        dx_used.reshape(-1, BLOCK, D),
        dx_query.reshape(-1, BLOCK, D),
        total_blocks,
    )
    for mask in spare_masks()[::-1]:
        dx_keep = add_low(dx_keep, exchange(dx_sent, mask))
        dx_keep, dx_sent = jnp.split(dx_keep, 2, axis=0)
    dx_spec = pl.BlockSpec((4, rows // tiles, D), lambda t, *a: (0, t, 0))
    dx_own = reduce_group(
        my_slot,
        [dx_keep.reshape(4, rows, D), exchange(dx_sent, CORE).reshape(4, rows, D)],
        [dx_spec] * 2,
        rows,
        D,
        read_rows,
        tiles,
    )
    input_grad = (grad_first + dx_own)[None]

    vec_first, vec_second, vec_adam = adam_moments(vec_m, vec_v, vec_grad)
    bias_first, bias_second, bias_adam = adam_moments(bias_m, bias_v, bias_grad)

    squares = wa_total(
        jnp.concatenate([jnp.sum(attn_sums, axis=(1, 2)), jnp.sum(ffn_sums, axis=(1, 2))])
    )
    squares = jnp.sqrt(squares)
    attn_norm, attn_length, ffn_norm, ffn_length = (
        squares[:4], squares[4:8], squares[8:10], squares[10:]
    )
    attn_ratio = attn_norm / (attn_length + RATIO_EPS)
    ffn_ratio = ffn_norm / (ffn_length + RATIO_EPS)
    ffn_new, ffn_copy = final(ffn_ratio, ffn_master, ffn_step)
    attn_new, attn_copy = final(attn_ratio, attn_master, attn_step)
    ratios = jnp.concatenate([attn_ratio, ffn_ratio])
    norms = jnp.stack(
        [
            jnp.concatenate([attn_norm, ffn_norm]),
            jnp.concatenate([attn_length, ffn_length]),
        ],
        axis=1,
    )
    vec_new = vec_master - STEP_RATE * vec_adam
    bias_new = bias_master - STEP_RATE * bias_adam
    return (
        output[None],
        input_grad,
        attn_grad,
        ffn_grad,
        vec_grad,
        bias_grad,
        attn_new,
        ffn_new,
        vec_new,
        bias_new,
        attn_copy,
        ffn_copy,
        vec_new.astype(BF16),
        bias_new.astype(BF16),
        attn_first,
        ffn_first,
        vec_first,
        bias_first,
        attn_second,
        ffn_second,
        vec_second,
        bias_second,
        norms,
        ratios,
    )


def solution(mesh):
    tokens = P(WA, CTX, None)
    mats = P(None, WA, None)
    vecs = P(None, WA)
    line = P(WA)
    state = (mats, mats, vecs, line)
    in_specs = (
        (tokens, tokens, P(WA), P(WA, None), tokens)
        + (mats,) * 6
        + (vecs,) * 3
        + (line,) * 3
    )
    out_specs = (tokens, tokens) + state * 5 + (P(), P())
    return jax.shard_map(shards, mesh=mesh, in_specs=in_specs, out_specs=out_specs, check_vma=False)
```
